256 devices in a mesh: elec: 16 (over y_lo, x, core), drop: 16 (over y_hi, z).
Axes of the slice: x: 4, y: 4 (y_hi: 2, y_lo: 2; y = y_hi * 2 + y_lo), z: 8, core: 2. Of those that a mesh axis runs over, the one named last changes fastest.
Arguments:
- elec_pos: float32 [3, 8192], P(None, 'elec'), may hold values from -3 to 3
- drop_vert: float32 [3, 16384], P(None, 'drop'), may hold values from -4 to 4
- drop_conn: int32 [3, 32768], P(None, 'drop'), may hold values from 0 to 16383, as said below
- elec_rhs: float32 [128, 8192], P(None, 'elec'), may hold values from -6 to 6
- drop_rhs: float32 [128, 32768], P(None, 'drop'), may hold values from -6 to 6
- elec_inv: float32 [64, 128, 128], P('elec')
- drop_inv: float32 [256, 128, 128], P('drop')
Outputs:
- charge_elec: float32 [128, 8192], P(None, 'elec')
- charge_drop: float32 [128, 32768], P(None, 'drop')
The draws below stay inside these ranges and needn't reach their ends.
Inputs may be any that keep to these rules, and one draw needn't show every extreme that they name: `drop_conn`: panel p's three vertices all lie in vertex block p // 2048, that is among vertices (1024) * (p // 2048) to 1024 * (p // 2048 + 1) - 1; every vertex is the first vertex of exactly two panels of its block.
All inputs are finite; a program needn't handle non-finite values.
Results may differ from the reference program's by a relative error of at most 0.0001.
Values sent between devices are 32-bit elements; how exact they have to be, the bound alone decides.
A program may use at most 64 MiB of HBM per device.

```python
import math
import jax
import jax.numpy as jnp
from jax import lax

ND_DEV = 2048
R = 128
BS = 128
ITERS = 2
NE = 8192
ND = 32768
NV = 16384


def inverse_blocks(key, block_count):
    first, second = jax.random.split(key)
    diagonal = jax.random.uniform(first, (block_count, BS), jnp.float32, 0.6, 1.6)
    noise = jax.random.normal(second, (block_count, BS, BS), jnp.float32) * (0.5 / math.sqrt(BS))
    return noise + diagonal[:, :, None] * jnp.eye(BS, dtype=jnp.float32)


def draw_elec_inv(key, part):
    return inverse_blocks(jax.random.fold_in(key, 21), NE // BS)


def draw_drop_inv(key, part):
    return inverse_blocks(jax.random.fold_in(key, 23), ND // BS)


def draw_drop_conn(key, part):
    block_count = ND // ND_DEV
    half_block = ND_DEV // 2
    perm_keys = jax.random.split(jax.random.fold_in(key, 11), 2 * block_count)
    firsts = jax.vmap(lambda single: jax.random.permutation(single, half_block))(perm_keys)
    firsts = firsts.astype(jnp.int32).reshape(1, block_count, ND_DEV)
    others = jax.random.randint(jax.random.fold_in(key, 13), (2, block_count, ND_DEV), 0, half_block, dtype=jnp.int32)
    offsets = (jnp.arange(block_count, dtype=jnp.int32) * half_block)[None, :, None]
    stacked = jnp.concatenate([firsts, others], axis=0) + offsets
    return stacked.reshape(3, ND)


def block_scale(key, extent, cuts, low, high):
    level = 1.0
    for axis_at, blocks in cuts:
        draws = jax.random.uniform(jax.random.fold_in(jax.random.fold_in(key, 6), axis_at), (blocks,), jnp.float32, low / len(cuts), high / len(cuts))
        level = level * jnp.repeat(jnp.exp(draws), extent[axis_at] // blocks).reshape((-1,) + (1,) * (len(extent) - 1 - axis_at))
    return level


def normal_values(rng, extent, spread, bound, shards=(), held_as=jnp.bfloat16):
    loudness = block_scale(rng, extent, shards, -0.22, 0.18) if shards else 1.0
    array = jax.random.normal(rng, extent, jnp.float32) * spread * loudness
    return jnp.minimum(jnp.maximum(array, -bound), bound).astype(held_as)


def setup_inputs(seed: int = 0) -> dict:
    arg_keys = jax.random.split(jax.random.key(seed), 8)
    return {
        "elec_pos": normal_values(arg_keys[0], (3, NE), 0.7, 3.0, ((1, 16),), jnp.float32),
        "drop_vert": normal_values(arg_keys[1], (3, NV), 1.0, 4.0, ((1, 16),), jnp.float32),
        "drop_conn": draw_drop_conn(jax.random.fold_in(arg_keys[7], 71), 0),
        "elec_rhs": normal_values(arg_keys[3], (R, NE), 1.0, 6.0, ((1, 16),), jnp.float32),
        "drop_rhs": normal_values(arg_keys[4], (R, ND), 1.0, 6.0, ((1, 16),), jnp.float32),
        "elec_inv": draw_elec_inv(jax.random.fold_in(arg_keys[7], 71), 0),
        "drop_inv": draw_drop_inv(jax.random.fold_in(arg_keys[7], 71), 0),
    }


HIGH = lax.Precision.HIGHEST

def constants(total_drop):
    screen = 1.0
    soften = 0.001
    couple = 1.0 / (3.0 * math.sqrt(total_drop))
    return (screen, soften, couple)

def centroids(drop_vert, conn):
    corners = jnp.take(drop_vert, conn, axis=1)
    return (corners[:, 0] + corners[:, 1] + corners[:, 2]) / 3.0

def kernel_tile(position, centres, screen, soften, couple):
    delta_x = position[0][:, None] - centres[0][None, :]
    delta_y = position[1][:, None] - centres[1][None, :]
    delta_z = position[2][:, None] - centres[2][None, :]
    distance = jnp.sqrt(delta_x * delta_x + delta_y * delta_y + delta_z * delta_z + soften)
    return couple * jnp.exp(-screen * distance) / distance

def block_solve(inverse, values):
    rhs_rows, columns = values.shape
    block_count, block_size, _ = inverse.shape
    shaped = values.reshape(rhs_rows, block_count, block_size)
    solved = jnp.einsum('bjk,rbk->rbj', inverse, shaped, precision=HIGH)
    return solved.reshape(rhs_rows, columns)

def reference(elec_pos, drop_vert, drop_conn, elec_rhs, drop_rhs, elec_inv, drop_inv):
    screen, soften, couple = constants(ND)
    centres = centroids(drop_vert, drop_conn)
    block_rows = math.gcd(NE, 512)
    block_count = NE // block_rows
    elec_blocks = jnp.moveaxis(elec_pos.reshape(3, block_count, block_rows), 1, 0)

    def cross(charge_elec, charge_drop):
        charge_blocks = jnp.moveaxis(charge_elec.reshape(R, block_count, block_rows), 1, 0)

        def visit_block(summed, inputs):
            position, charge_part = inputs
            kernel = kernel_tile(position, centres, screen, soften, couple)
            to_elec = lax.dot_general(charge_drop, kernel, (((1,), (1,)), ((), ())), precision=HIGH)
            summed = summed + jnp.dot(charge_part, kernel, precision=HIGH)
            return (summed, to_elec)
        field_drop, pieces = lax.scan(visit_block, jnp.zeros((R, ND), jnp.float32), (elec_blocks, charge_blocks))
        field_elec = jnp.moveaxis(pieces, 0, 1).reshape(R, NE)
        return (field_elec, field_drop)
    charge_elec = block_solve(elec_inv, elec_rhs)
    charge_drop = block_solve(drop_inv, drop_rhs)
    for iteration in range(ITERS):
        field_elec, field_drop = cross(charge_elec, charge_drop)
        charge_elec = block_solve(elec_inv, elec_rhs - field_elec)
        charge_drop = block_solve(drop_inv, drop_rhs - field_drop)
    return (charge_elec, charge_drop)
```

```python
import functools
import math

import jax
import jax.numpy as jnp
from jax import lax
from jax.experimental import pallas as pl
from jax.experimental.pallas import tpu as pltpu
from jax.sharding import PartitionSpec as P

ITERS = 2


HIGH = lax.Precision.HIGHEST
MESH = pl.DeviceIdType.MESH


def constants(total_drop):
    screen = 1.0
    soften = 0.001
    couple = 1.0 / (3.0 * math.sqrt(total_drop))
    return (screen, soften, couple)


def centroids(drop_vert, conn):
    corners = jnp.take(drop_vert, conn, axis=1)
    return (corners[:, 0] + corners[:, 1] + corners[:, 2]) / 3.0


def kernel_tile(position, centres, screen, soften, couple):
    delta_x = position[0][:, None] - centres[0][None, :]
    delta_y = position[1][:, None] - centres[1][None, :]
    delta_z = position[2][:, None] - centres[2][None, :]
    distance = jnp.sqrt(delta_x * delta_x + delta_y * delta_y + delta_z * delta_z + soften)
    return couple * jnp.exp(-screen * distance) / distance


def block_solve(inverse, values):
    rhs_rows, columns = values.shape
    block_count, block_size, _ = inverse.shape
    shaped = values.reshape(rhs_rows, block_count, block_size)
    solved = jnp.einsum("bjk,rbk->rbj", inverse, shaped, precision=HIGH)
    return solved.reshape(rhs_rows, columns)


def reduce_kernel(sizes, pieces, *refs):
    axes = ("drop", "elec")
    count = len(axes)
    ins = refs[:count]
    outs = refs[count:2 * count]
    scratch = refs[2 * count:]
    first = scratch[0:count]
    second = scratch[count:2 * count]
    summed = scratch[2 * count:3 * count]
    sems = scratch[3 * count:]

    barrier = pltpu.get_barrier_semaphore()
    total = 0
    for axis, size in zip(axes, sizes):
        me = lax.axis_index(axis)
        for step in range(1, size):
            peer = lax.rem(me + step, size)
            pl.semaphore_signal(barrier, inc=1, device_id={axis: peer}, device_id_type=MESH)
        total += size - 1
    pl.semaphore_wait(barrier, total)

    def rows(index, piece):
        return pl.ds(pl.multiple_of(index * piece, piece), piece)

    def exchange(phase, source_of, target):
        copies = []
        for a, (axis, size) in enumerate(zip(axes, sizes)):
            me = lax.axis_index(axis)
            send_sem, recv_sem = sems[4 * a + 2 * phase], sems[4 * a + 2 * phase + 1]
            for step in range(1, size):
                peer = lax.rem(me + step, size)
                copy = pltpu.make_async_remote_copy(
                    src_ref=source_of(a, peer),
                    dst_ref=target[a].at[step],
                    send_sem=send_sem.at[step],
                    recv_sem=recv_sem.at[step],
                    device_id={axis: peer},
                    device_id_type=MESH,
                )
                copy.start()
                copies.append(copy)
        for copy in copies:
            copy.wait()

    exchange(0, lambda a, peer: ins[a].at[rows(peer, pieces[a])], first)

    for a, (axis, size) in enumerate(zip(axes, sizes)):
        me = lax.axis_index(axis)
        acc = ins[a][rows(me, pieces[a]), :]
        for step in range(1, size):
            acc = acc + first[a][step]
        summed[a][...] = acc
        outs[a][rows(me, pieces[a]), :] = acc

    exchange(1, lambda a, peer: summed[a], second)

    for a, (axis, size) in enumerate(zip(axes, sizes)):
        me = lax.axis_index(axis)
        for step in range(1, size):
            source = lax.rem(me - step + size, size)
            outs[a][rows(source, pieces[a]), :] = second[a][step]


def all_reduce_both(part_elec, part_drop, sizes, collective):
    operands = (part_elec, part_drop)
    pieces = tuple(x.shape[0] // size for x, size in zip(operands, sizes))
    scratch = []
    for x, size in zip(operands, sizes):
        scratch.append(pltpu.VMEM((size, x.shape[0] // size, x.shape[1]), jnp.float32))
    for x, size in zip(operands, sizes):
        scratch.append(pltpu.VMEM((size, x.shape[0] // size, x.shape[1]), jnp.float32))
    for x, size in zip(operands, sizes):
        scratch.append(pltpu.VMEM((x.shape[0] // size, x.shape[1]), jnp.float32))
    for size in sizes:
        for _ in range(4):
            scratch.append(pltpu.SemaphoreType.DMA((size,)))
    vmem = pl.BlockSpec(memory_space=pltpu.VMEM)
    return pl.pallas_call(
        functools.partial(reduce_kernel, sizes, pieces),
        out_shape=tuple(jax.ShapeDtypeStruct(x.shape, x.dtype) for x in operands),
        in_specs=[vmem, vmem],
        out_specs=(vmem, vmem),
        scratch_shapes=scratch,
        compiler_params=pltpu.CompilerParams(collective_id=collective, has_side_effects=True),
    )(*operands)


def on_device(elec_pos, drop_vert, drop_conn, elec_rhs, drop_rhs, elec_inv, drop_inv):
    drop_devices = lax.axis_size("drop")
    elec_devices = lax.axis_size("elec")
    rhs_count, elec_local = elec_rhs.shape
    drop_local = drop_rhs.shape[1]
    screen, soften, couple = constants(drop_local * drop_devices)
    half_block = drop_vert.shape[1]
    local_conn = drop_conn - lax.axis_index("drop") * half_block
    centres = centroids(drop_vert, local_conn)
    kernel = kernel_tile(elec_pos, centres, screen, soften, couple)

    charge_elec = block_solve(elec_inv, elec_rhs)
    charge_drop = block_solve(drop_inv, drop_rhs)
    for iteration in range(ITERS):
        part_elec = lax.dot_general(charge_drop, kernel, (((1,), (1,)), ((), ())), precision=HIGH)
        part_drop = jnp.dot(charge_elec, kernel, precision=HIGH)
        field_elec, field_drop = all_reduce_both(
            part_elec, part_drop, (drop_devices, elec_devices), iteration
        )
        charge_elec = block_solve(elec_inv, elec_rhs - field_elec)
        charge_drop = block_solve(drop_inv, drop_rhs - field_drop)
    return (charge_elec, charge_drop)


def solution(mesh):
    placed = (
        P(None, "elec"),
        P(None, "drop"),
        P(None, "drop"),
        P(None, "elec"),
        P(None, "drop"),
        P("elec", None, None),
        P("drop", None, None),
    )
    return jax.shard_map(
        on_device,
        mesh=mesh,
        in_specs=placed,
        out_specs=(P(None, "elec"), P(None, "drop")),
        check_vma=False,
    )
```

```python
import functools
import math

import jax
import jax.numpy as jnp
from jax import lax
from jax.experimental import pallas as pl
from jax.experimental.pallas import tpu as pltpu
from jax.sharding import PartitionSpec as P

ITERS = 2


HIGH = lax.Precision.HIGHEST
MESH = pl.DeviceIdType.MESH


def constants(total_drop):
    screen = 1.0
    soften = 0.001
    couple = 1.0 / (3.0 * math.sqrt(total_drop))
    return (screen, soften, couple)


def centroids(drop_vert, conn):
    vertices = lax.broadcasted_iota(jnp.int32, (drop_vert.shape[1], conn.shape[1]), 0)
    counts = sum((conn[k][None, :] == vertices).astype(jnp.float32) for k in range(3))
    return jnp.dot(drop_vert, counts, precision=HIGH) / 3.0


def kernel_tile(position, centres, screen, soften, couple):
    delta_x = position[0][:, None] - centres[0][None, :]
    delta_y = position[1][:, None] - centres[1][None, :]
    delta_z = position[2][:, None] - centres[2][None, :]
    distance = jnp.sqrt(delta_x * delta_x + delta_y * delta_y + delta_z * delta_z + soften)
    return couple * jnp.exp(-screen * distance) / distance


def block_solve(inverse, values):
    rhs_rows, columns = values.shape
    block_count, block_size, _ = inverse.shape
    shaped = values.reshape(rhs_rows, block_count, block_size)
    solved = jnp.einsum("bjk,rbk->rbj", inverse, shaped, precision=HIGH)
    return solved.reshape(rhs_rows, columns)


def reduce_kernel(sizes, pieces, *refs):
    axes = ("drop", "elec")
    count = len(axes)
    ins = refs[:count]
    outs = refs[count:2 * count]
    scratch = refs[2 * count:]
    first = scratch[0:count]
    second = scratch[count:2 * count]
    summed = scratch[2 * count:3 * count]
    sems = scratch[3 * count:]

    barrier = pltpu.get_barrier_semaphore()
    total = 0
    for axis, size in zip(axes, sizes):
        me = lax.axis_index(axis)
        for step in range(1, size):
            peer = lax.rem(me + step, size)
            pl.semaphore_signal(barrier, inc=1, device_id={axis: peer}, device_id_type=MESH)
        total += size - 1
    pl.semaphore_wait(barrier, total)

    def rows(index, piece):
        return pl.ds(pl.multiple_of(index * piece, piece), piece)

    def exchange(phase, source_of, target):
        copies = []
        for a, (axis, size) in enumerate(zip(axes, sizes)):
            me = lax.axis_index(axis)
            send_sem, recv_sem = sems[4 * a + 2 * phase], sems[4 * a + 2 * phase + 1]
            for step in range(1, size):
                peer = lax.rem(me + step, size)
                copy = pltpu.make_async_remote_copy(
                    src_ref=source_of(a, peer),
                    dst_ref=target[a].at[step],
                    send_sem=send_sem.at[step],
                    recv_sem=recv_sem.at[step],
                    device_id={axis: peer},
                    device_id_type=MESH,
                )
                copy.start()
                copies.append(copy)
        for copy in copies:
            copy.wait()

    exchange(0, lambda a, peer: ins[a].at[rows(peer, pieces[a])], first)

    for a, (axis, size) in enumerate(zip(axes, sizes)):
        me = lax.axis_index(axis)
        acc = ins[a][rows(me, pieces[a]), :]
        for step in range(1, size):
            acc = acc + first[a][step]
        summed[a][...] = acc
        outs[a][rows(me, pieces[a]), :] = acc

    exchange(1, lambda a, peer: summed[a], second)

    for a, (axis, size) in enumerate(zip(axes, sizes)):
        me = lax.axis_index(axis)
        for step in range(1, size):
            source = lax.rem(me - step + size, size)
            outs[a][rows(source, pieces[a]), :] = second[a][step]


def all_reduce_both(part_elec, part_drop, sizes, collective):
    operands = (part_elec, part_drop)
    pieces = tuple(x.shape[0] // size for x, size in zip(operands, sizes))
    scratch = []
    for x, size in zip(operands, sizes):
        scratch.append(pltpu.VMEM((size, x.shape[0] // size, x.shape[1]), jnp.float32))
    for x, size in zip(operands, sizes):
        scratch.append(pltpu.VMEM((size, x.shape[0] // size, x.shape[1]), jnp.float32))
    for x, size in zip(operands, sizes):
        scratch.append(pltpu.VMEM((x.shape[0] // size, x.shape[1]), jnp.float32))
    for size in sizes:
        for _ in range(4):
            scratch.append(pltpu.SemaphoreType.DMA((size,)))
    vmem = pl.BlockSpec(memory_space=pltpu.VMEM)
    return pl.pallas_call(
        functools.partial(reduce_kernel, sizes, pieces),
        out_shape=tuple(jax.ShapeDtypeStruct(x.shape, x.dtype) for x in operands),
        in_specs=[vmem, vmem],
        out_specs=(vmem, vmem),
        scratch_shapes=scratch,
        compiler_params=pltpu.CompilerParams(collective_id=collective, has_side_effects=True),
    )(*operands)


def on_device(elec_pos, drop_vert, drop_conn, elec_rhs, drop_rhs, elec_inv, drop_inv):
    drop_devices = lax.axis_size("drop")
    elec_devices = lax.axis_size("elec")
    rhs_count, elec_local = elec_rhs.shape
    drop_local = drop_rhs.shape[1]
    screen, soften, couple = constants(drop_local * drop_devices)
    half_block = drop_vert.shape[1]
    local_conn = drop_conn - lax.axis_index("drop") * half_block
    centres = centroids(drop_vert, local_conn)
    kernel = lax.optimization_barrier(kernel_tile(elec_pos, centres, screen, soften, couple))

    charge_elec = block_solve(elec_inv, elec_rhs)
    charge_drop = block_solve(drop_inv, drop_rhs)
    for iteration in range(ITERS):
        part_elec = lax.dot_general(charge_drop, kernel, (((1,), (1,)), ((), ())), precision=HIGH)
        part_drop = jnp.dot(charge_elec, kernel, precision=HIGH)
        field_elec, field_drop = all_reduce_both(
            part_elec, part_drop, (drop_devices, elec_devices), iteration
        )
        charge_elec = block_solve(elec_inv, elec_rhs - field_elec)
        charge_drop = block_solve(drop_inv, drop_rhs - field_drop)
    return (charge_elec, charge_drop)


def solution(mesh):
    placed = (
        P(None, "elec"),
        P(None, "drop"),
        P(None, "drop"),
        P(None, "elec"),
        P(None, "drop"),
        P("elec", None, None),
        P("drop", None, None),
    )
    return jax.shard_map(
        on_device,
        mesh=mesh,
        in_specs=placed,
        out_specs=(P(None, "elec"), P(None, "drop")),
        check_vma=False,
    )
```

```python
import functools
import math

import jax
import jax.numpy as jnp
from jax import lax
from jax.experimental import pallas as pl
from jax.experimental.pallas import tpu as pltpu
from jax.sharding import PartitionSpec as P

ITERS = 2


HIGH = lax.Precision.HIGHEST
MESH = pl.DeviceIdType.MESH


def constants(total_drop):
    screen = 1.0
    soften = 0.001
    couple = 1.0 / (3.0 * math.sqrt(total_drop))
    return (screen, soften, couple)


def centroids(drop_vert, conn):
    vertices = lax.broadcasted_iota(jnp.int32, (drop_vert.shape[1], conn.shape[1]), 0)
    counts = sum((conn[k][None, :] == vertices).astype(jnp.float32) for k in range(3))
    return jnp.dot(drop_vert, counts, precision=HIGH) / 3.0


def kernel_tile(position, centres, screen, soften, couple):
    delta_x = position[0][:, None] - centres[0][None, :]
    delta_y = position[1][:, None] - centres[1][None, :]
    delta_z = position[2][:, None] - centres[2][None, :]
    distance = jnp.sqrt(delta_x * delta_x + delta_y * delta_y + delta_z * delta_z + soften)
    return couple * jnp.exp(-screen * distance) / distance


def block_solve(inverse, values):
    rhs_rows, columns = values.shape
    block_count, block_size, _ = inverse.shape
    shaped = values.reshape(rhs_rows, block_count, block_size)
    solved = jnp.einsum("bjk,rbk->rbj", inverse, shaped, precision=HIGH)
    return solved.reshape(rhs_rows, columns)


def reduce_kernel(sizes, *refs):
    n_d, n_e = sizes
    in_d, in_e, out_d, out_e = refs[:4]
    (first_d, second_d, summed_d, buf_a, buf_b, buf_c, buf_d, half_s, piece_t, half_h,
     sd1, rd1, sd2, rd2, sa, ra, sb, rb, sc, rc, sdd, rdd) = refs[4:]
    chips = n_e // 2
    rows_d = in_d.shape[0] // n_d
    half = in_e.shape[0] // 2
    rows_e = half // chips
    me_d = lax.axis_index("drop")
    me_e = lax.axis_index("elec")
    core = lax.rem(me_e, 2)
    chip = me_e // 2
    partner = me_e + 1 - 2 * core

    def elec_peer(step):
        return 2 * lax.rem(chip + step, chips) + core

    barrier = pltpu.get_barrier_semaphore()
    for step in range(1, n_d):
        pl.semaphore_signal(barrier, inc=1, device_id={"drop": lax.rem(me_d + step, n_d)}, device_id_type=MESH)
    pl.semaphore_signal(barrier, inc=1, device_id={"elec": partner}, device_id_type=MESH)
    for step in range(1, chips):
        pl.semaphore_signal(barrier, inc=1, device_id={"elec": elec_peer(step)}, device_id_type=MESH)
    pl.semaphore_wait(barrier, n_d - 1 + chips)

    def rows(index, count):
        return pl.ds(pl.multiple_of(index * count, count), count)

    def send(src, dst, send_sem, recv_sem, axis, peer):
        copy = pltpu.make_async_remote_copy(
            src_ref=src, dst_ref=dst, send_sem=send_sem, recv_sem=recv_sem,
            device_id={axis: peer}, device_id_type=MESH,
        )
        copy.start()
        return copy

    def wait_all(copies):
        for copy in copies:
            copy.wait()

    drop_copies = [
        send(in_d.at[rows(lax.rem(me_d + step, n_d), rows_d)], first_d.at[step], sd1.at[step], rd1.at[step],
             "drop", lax.rem(me_d + step, n_d))
        for step in range(1, n_d)
    ]
    mine = pl.multiple_of(core * half, half)
    other = pl.multiple_of((1 - core) * half, half)
    elec_a = [send(in_e.at[pl.ds(other, half)], buf_a, sa.at[0], ra.at[0], "elec", partner)]

    wait_all(elec_a)
    half_s[...] = in_e[pl.ds(mine, half), :] + buf_a[...]
    elec_b = [
        send(half_s.at[rows(lax.rem(chip + step, chips), rows_e)], buf_b.at[step], sb.at[step], rb.at[step],
             "elec", elec_peer(step))
        for step in range(1, chips)
    ]

    wait_all(drop_copies)
    acc = in_d[rows(me_d, rows_d), :]
    for step in range(1, n_d):
        acc = acc + first_d[step]
    summed_d[...] = acc
    out_d[rows(me_d, rows_d), :] = acc
    drop_copies = [
        send(summed_d, second_d.at[step], sd2.at[step], rd2.at[step], "drop", lax.rem(me_d + step, n_d))
        for step in range(1, n_d)
    ]

    wait_all(elec_b)
    acc = half_s[rows(chip, rows_e), :]
    for step in range(1, chips):
        acc = acc + buf_b[step]
    piece_t[...] = acc
    half_h[rows(chip, rows_e), :] = acc
    elec_c = [
        send(piece_t, buf_c.at[step], sc.at[step], rc.at[step], "elec", elec_peer(step))
        for step in range(1, chips)
    ]

    wait_all(drop_copies)
    for step in range(1, n_d):
        source = lax.rem(me_d - step + n_d, n_d)
        out_d[rows(source, rows_d), :] = second_d[step]

    wait_all(elec_c)
    for step in range(1, chips):
        source = lax.rem(chip - step + chips, chips)
        half_h[rows(source, rows_e), :] = buf_c[step]
    elec_d = [send(half_h, buf_d, sdd.at[0], rdd.at[0], "elec", partner)]
    out_e[pl.ds(mine, half), :] = half_h[...]
    wait_all(elec_d)
    out_e[pl.ds(other, half), :] = buf_d[...]


def all_reduce_both(part_elec, part_drop, sizes, collective):
    n_d, n_e = sizes
    chips = n_e // 2
    rows_d = part_elec.shape[0] // n_d
    half = part_drop.shape[0] // 2
    rows_e = half // chips
    cols_d = part_elec.shape[1]
    cols_e = part_drop.shape[1]
    f32 = jnp.float32
    scratch = [
        pltpu.VMEM((n_d, rows_d, cols_d), f32),
        pltpu.VMEM((n_d, rows_d, cols_d), f32),
        pltpu.VMEM((rows_d, cols_d), f32),
        pltpu.VMEM((half, cols_e), f32),
        pltpu.VMEM((chips, rows_e, cols_e), f32),
        pltpu.VMEM((chips, rows_e, cols_e), f32),
        pltpu.VMEM((half, cols_e), f32),
        pltpu.VMEM((half, cols_e), f32),
        pltpu.VMEM((rows_e, cols_e), f32),
        pltpu.VMEM((half, cols_e), f32),
    ]
    for count in (n_d, n_d, n_d, n_d, 1, 1, chips, chips, chips, chips, 1, 1):
        scratch.append(pltpu.SemaphoreType.DMA((count,)))
    vmem = pl.BlockSpec(memory_space=pltpu.VMEM)
    return pl.pallas_call(
        functools.partial(reduce_kernel, sizes),
        out_shape=(jax.ShapeDtypeStruct(part_elec.shape, f32), jax.ShapeDtypeStruct(part_drop.shape, f32)),
        in_specs=[vmem, vmem],
        out_specs=(vmem, vmem),
        scratch_shapes=scratch,
        compiler_params=pltpu.CompilerParams(collective_id=collective, has_side_effects=True),
    )(part_elec, part_drop)


def on_device(elec_pos, drop_vert, drop_conn, elec_rhs, drop_rhs, elec_inv, drop_inv):
    drop_devices = lax.axis_size("drop")
    elec_devices = lax.axis_size("elec")
    rhs_count, elec_local = elec_rhs.shape
    drop_local = drop_rhs.shape[1]
    screen, soften, couple = constants(drop_local * drop_devices)
    half_block = drop_vert.shape[1]
    local_conn = drop_conn - lax.axis_index("drop") * half_block
    centres = centroids(drop_vert, local_conn)
    kernel = lax.optimization_barrier(kernel_tile(elec_pos, centres, screen, soften, couple))

    charge_elec = block_solve(elec_inv, elec_rhs)
    charge_drop = block_solve(drop_inv, drop_rhs)
    for iteration in range(ITERS):
        part_elec = lax.dot_general(charge_drop, kernel, (((1,), (1,)), ((), ())), precision=HIGH)
        part_drop = jnp.dot(charge_elec, kernel, precision=HIGH)
        field_elec, field_drop = all_reduce_both(
            part_elec, part_drop, (drop_devices, elec_devices), iteration
        )
        charge_elec = block_solve(elec_inv, elec_rhs - field_elec)
        charge_drop = block_solve(drop_inv, drop_rhs - field_drop)
    return (charge_elec, charge_drop)


def solution(mesh):
    placed = (
        P(None, "elec"),
        P(None, "drop"),
        P(None, "drop"),
        P(None, "elec"),
        P(None, "drop"),
        P("elec", None, None),
        P("drop", None, None),
    )
    return jax.shard_map(
        on_device,
        mesh=mesh,
        in_specs=placed,
        out_specs=(P(None, "elec"), P(None, "drop")),
        check_vma=False,
    )
```

```python
import functools
import math

import jax
import jax.numpy as jnp
from jax import lax
from jax.experimental import pallas as pl
from jax.experimental.pallas import tpu as pltpu
from jax.sharding import PartitionSpec as P

ITERS = 2


HIGH = lax.Precision.HIGHEST
FAST = lax.Precision.HIGH
MESH = pl.DeviceIdType.MESH


def constants(total_drop):
    screen = 1.0
    soften = 0.001
    couple = 1.0 / (3.0 * math.sqrt(total_drop))
    return (screen, soften, couple)


def centroids(drop_vert, conn):
    vertices = lax.broadcasted_iota(jnp.int32, (conn.shape[1], drop_vert.shape[1]), 1)
    counts = sum((conn[k][:, None] == vertices).astype(jnp.float32) for k in range(3))
    return jnp.dot(counts, drop_vert.T, precision=HIGH).T / 3.0


def kernel_tile(position, centres, screen, soften, couple):
    delta_x = position[0][:, None] - centres[0][None, :]
    delta_y = position[1][:, None] - centres[1][None, :]
    delta_z = position[2][:, None] - centres[2][None, :]
    distance = jnp.sqrt(delta_x * delta_x + delta_y * delta_y + delta_z * delta_z + soften)
    return couple * jnp.exp(-screen * distance) / distance


def block_solve(inverse, values):
    rhs_rows, columns = values.shape
    block_count, block_size, _ = inverse.shape
    shaped = values.reshape(rhs_rows, block_count, block_size)
    solved = jnp.einsum("bjk,rbk->rbj", inverse, shaped, precision=FAST)
    return solved.reshape(rhs_rows, columns)


def reduce_kernel(sizes, *refs):
    n_d, n_e = sizes
    in_d, in_e, out_d, out_e = refs[:4]
    (first_d, second_d, summed_d, buf_a, buf_b, buf_c, buf_d, half_s, piece_t, half_h,
     sd1, rd1, sd2, rd2, sa, ra, sb, rb, sc, rc, sdd, rdd) = refs[4:]
    chips = n_e // 2
    rows_d = in_d.shape[0] // n_d
    half = in_e.shape[0] // 2
    rows_e = half // chips
    me_d = lax.axis_index("drop")
    me_e = lax.axis_index("elec")
    core = lax.rem(me_e, 2)
    chip = me_e // 2
    partner = me_e + 1 - 2 * core

    def elec_peer(step):
        return 2 * lax.rem(chip + step, chips) + core

    barrier = pltpu.get_barrier_semaphore()
    for step in range(1, n_d):
        pl.semaphore_signal(barrier, inc=1, device_id={"drop": lax.rem(me_d + step, n_d)}, device_id_type=MESH)
    pl.semaphore_signal(barrier, inc=1, device_id={"elec": partner}, device_id_type=MESH)
    for step in range(1, chips):
        pl.semaphore_signal(barrier, inc=1, device_id={"elec": elec_peer(step)}, device_id_type=MESH)
    pl.semaphore_wait(barrier, n_d - 1 + chips)

    def rows(index, count):
        return pl.ds(pl.multiple_of(index * count, count), count)

    def send(src, dst, send_sem, recv_sem, axis, peer):
        copy = pltpu.make_async_remote_copy(
            src_ref=src, dst_ref=dst, send_sem=send_sem, recv_sem=recv_sem,
            device_id={axis: peer}, device_id_type=MESH,
        )
        copy.start()
        return copy

    def wait_all(copies):
        for copy in copies:
            copy.wait()

    drop_copies = [
        send(in_d.at[rows(lax.rem(me_d + step, n_d), rows_d)], first_d.at[step], sd1.at[step], rd1.at[step],
             "drop", lax.rem(me_d + step, n_d))
        for step in range(1, n_d)
    ]
    mine = pl.multiple_of(core * half, half)
    other = pl.multiple_of((1 - core) * half, half)
    elec_a = [send(in_e.at[pl.ds(other, half)], buf_a, sa.at[0], ra.at[0], "elec", partner)]

    wait_all(elec_a)
    half_s[...] = in_e[pl.ds(mine, half), :] + buf_a[...]
    elec_b = [
        send(half_s.at[rows(lax.rem(chip + step, chips), rows_e)], buf_b.at[step], sb.at[step], rb.at[step],
             "elec", elec_peer(step))
        for step in range(1, chips)
    ]

    wait_all(drop_copies)
    acc = in_d[rows(me_d, rows_d), :]
    for step in range(1, n_d):
        acc = acc + first_d[step]
    summed_d[...] = acc
    out_d[rows(me_d, rows_d), :] = acc
    drop_copies = [
        send(summed_d, second_d.at[step], sd2.at[step], rd2.at[step], "drop", lax.rem(me_d + step, n_d))
        for step in range(1, n_d)
    ]

    wait_all(elec_b)
    acc = half_s[rows(chip, rows_e), :]
    for step in range(1, chips):
        acc = acc + buf_b[step]
    piece_t[...] = acc
    half_h[rows(chip, rows_e), :] = acc
    elec_c = [
        send(piece_t, buf_c.at[step], sc.at[step], rc.at[step], "elec", elec_peer(step))
        for step in range(1, chips)
    ]

    wait_all(drop_copies)
    for step in range(1, n_d):
        source = lax.rem(me_d - step + n_d, n_d)
        out_d[rows(source, rows_d), :] = second_d[step]

    wait_all(elec_c)
    for step in range(1, chips):
        source = lax.rem(chip - step + chips, chips)
        half_h[rows(source, rows_e), :] = buf_c[step]
    elec_d = [send(half_h, buf_d, sdd.at[0], rdd.at[0], "elec", partner)]
    out_e[pl.ds(mine, half), :] = half_h[...]
    wait_all(elec_d)
    out_e[pl.ds(other, half), :] = buf_d[...]


def all_reduce_both(part_elec, part_drop, sizes, collective):
    n_d, n_e = sizes
    chips = n_e // 2
    rows_d = part_elec.shape[0] // n_d
    half = part_drop.shape[0] // 2
    rows_e = half // chips
    cols_d = part_elec.shape[1]
    cols_e = part_drop.shape[1]
    f32 = jnp.float32
    scratch = [
        pltpu.VMEM((n_d, rows_d, cols_d), f32),
        pltpu.VMEM((n_d, rows_d, cols_d), f32),
        pltpu.VMEM((rows_d, cols_d), f32),
        pltpu.VMEM((half, cols_e), f32),
        pltpu.VMEM((chips, rows_e, cols_e), f32),
        pltpu.VMEM((chips, rows_e, cols_e), f32),
        pltpu.VMEM((half, cols_e), f32),
        pltpu.VMEM((half, cols_e), f32),
        pltpu.VMEM((rows_e, cols_e), f32),
        pltpu.VMEM((half, cols_e), f32),
    ]
    for count in (n_d, n_d, n_d, n_d, 1, 1, chips, chips, chips, chips, 1, 1):
        scratch.append(pltpu.SemaphoreType.DMA((count,)))
    vmem = pl.BlockSpec(memory_space=pltpu.VMEM)
    return pl.pallas_call(
        functools.partial(reduce_kernel, sizes),
        out_shape=(jax.ShapeDtypeStruct(part_elec.shape, f32), jax.ShapeDtypeStruct(part_drop.shape, f32)),
        in_specs=[vmem, vmem],
        out_specs=(vmem, vmem),
        scratch_shapes=scratch,
        compiler_params=pltpu.CompilerParams(collective_id=collective, has_side_effects=True),
    )(part_elec, part_drop)


def on_device(elec_pos, drop_vert, drop_conn, elec_rhs, drop_rhs, elec_inv, drop_inv):
    drop_devices = lax.axis_size("drop")
    elec_devices = lax.axis_size("elec")
    rhs_count, elec_local = elec_rhs.shape
    drop_local = drop_rhs.shape[1]
    screen, soften, couple = constants(drop_local * drop_devices)
    half_block = drop_vert.shape[1]
    local_conn = drop_conn - lax.axis_index("drop") * half_block
    centres = centroids(drop_vert, local_conn)
    kernel = lax.optimization_barrier(kernel_tile(elec_pos, centres, screen, soften, couple))

    charge_elec = block_solve(elec_inv, elec_rhs)
    charge_drop = block_solve(drop_inv, drop_rhs)
    for iteration in range(ITERS):
        part_elec = lax.dot_general(charge_drop, kernel, (((1,), (1,)), ((), ())), precision=FAST)
        part_drop = jnp.dot(charge_elec, kernel, precision=FAST)
        field_elec, field_drop = all_reduce_both(
            part_elec, part_drop, (drop_devices, elec_devices), iteration
        )
        charge_elec = block_solve(elec_inv, elec_rhs - field_elec)
        charge_drop = block_solve(drop_inv, drop_rhs - field_drop)
    return (charge_elec, charge_drop)


def solution(mesh):
    placed = (
        P(None, "elec"),
        P(None, "drop"),
        P(None, "drop"),
        P(None, "elec"),
        P(None, "drop"),
        P("elec", None, None),
        P("drop", None, None),
    )
    return jax.shard_map(
        on_device,
        mesh=mesh,
        in_specs=placed,
        out_specs=(P(None, "elec"), P(None, "drop")),
        check_vma=False,
    )
```

```python
import functools
import math

import jax
import jax.numpy as jnp
from jax import lax
from jax.experimental import pallas as pl
from jax.experimental.pallas import tpu as pltpu
from jax.sharding import PartitionSpec as P

ITERS = 2


HIGH = lax.Precision.HIGHEST
FAST = lax.Precision.HIGH
MESH = pl.DeviceIdType.MESH


def constants(total_drop):
    screen = 1.0
    soften = 0.001
    couple = 1.0 / (3.0 * math.sqrt(total_drop))
    return (screen, soften, couple)


def centroids(drop_vert, conn):
    vertices = lax.broadcasted_iota(jnp.int32, (drop_vert.shape[1], conn.shape[1]), 0)
    counts = sum((conn[k][None, :] == vertices).astype(jnp.float32) for k in range(3))
    counts = counts.astype(jnp.bfloat16)
    parts = []
    rest = drop_vert
    for _ in range(3):
        part = lax.reduce_precision(rest, exponent_bits=8, mantissa_bits=7)
        parts.append(part.astype(jnp.bfloat16))
        rest = rest - part
    stacked = jnp.concatenate(parts, axis=0)
    summed = jnp.dot(stacked, counts, preferred_element_type=jnp.float32)
    coords = drop_vert.shape[0]
    return (summed[:coords] + summed[coords:2 * coords] + summed[2 * coords:]) / 3.0


def kernel_tile(position, centres, screen, soften, couple):
    delta_x = position[0][:, None] - centres[0][None, :]
    delta_y = position[1][:, None] - centres[1][None, :]
    delta_z = position[2][:, None] - centres[2][None, :]
    distance = jnp.sqrt(delta_x * delta_x + delta_y * delta_y + delta_z * delta_z + soften)
    return couple * jnp.exp(-screen * distance) / distance


def block_solve(inverse, values):
    rhs_rows, columns = values.shape
    block_count, block_size, _ = inverse.shape
    shaped = values.reshape(rhs_rows, block_count, block_size)
    solved = jnp.einsum("bjk,rbk->rbj", inverse, shaped, precision=HIGH)
    return solved.reshape(rhs_rows, columns)


def reduce_kernel(sizes, *refs):
    n_d, n_e = sizes
    in_d, in_e, out_d, out_e = refs[:4]
    (first_d, second_d, summed_d, buf_a, buf_b, buf_c, buf_d, half_s, piece_t, half_h,
     sd1, rd1, sd2, rd2, sa, ra, sb, rb, sc, rc, sdd, rdd) = refs[4:]
    chips = n_e // 2
    rows_d = in_d.shape[0] // n_d
    half = in_e.shape[0] // 2
    rows_e = half // chips
    me_d = lax.axis_index("drop")
    me_e = lax.axis_index("elec")
    core = lax.rem(me_e, 2)
    chip = me_e // 2
    partner = me_e + 1 - 2 * core

    def elec_peer(step):
        return 2 * lax.rem(chip + step, chips) + core

    barrier = pltpu.get_barrier_semaphore()
    for step in range(1, n_d):
        pl.semaphore_signal(barrier, inc=1, device_id={"drop": lax.rem(me_d + step, n_d)}, device_id_type=MESH)
    pl.semaphore_signal(barrier, inc=1, device_id={"elec": partner}, device_id_type=MESH)
    for step in range(1, chips):
        pl.semaphore_signal(barrier, inc=1, device_id={"elec": elec_peer(step)}, device_id_type=MESH)
    pl.semaphore_wait(barrier, n_d - 1 + chips)

    def rows(index, count):
        return pl.ds(pl.multiple_of(index * count, count), count)

    def send(src, dst, send_sem, recv_sem, axis, peer):
        copy = pltpu.make_async_remote_copy(
            src_ref=src, dst_ref=dst, send_sem=send_sem, recv_sem=recv_sem,
            device_id={axis: peer}, device_id_type=MESH,
        )
        copy.start()
        return copy

    def wait_all(copies):
        for copy in copies:
            copy.wait()

    drop_copies = [
        send(in_d.at[rows(lax.rem(me_d + step, n_d), rows_d)], first_d.at[step], sd1.at[step], rd1.at[step],
             "drop", lax.rem(me_d + step, n_d))
        for step in range(1, n_d)
    ]
    mine = pl.multiple_of(core * half, half)
    other = pl.multiple_of((1 - core) * half, half)
    elec_a = [send(in_e.at[pl.ds(other, half)], buf_a, sa.at[0], ra.at[0], "elec", partner)]

    wait_all(elec_a)
    half_s[...] = in_e[pl.ds(mine, half), :] + buf_a[...]
    elec_b = [
        send(half_s.at[rows(lax.rem(chip + step, chips), rows_e)], buf_b.at[step], sb.at[step], rb.at[step],
             "elec", elec_peer(step))
        for step in range(1, chips)
    ]

    wait_all(drop_copies)
    acc = in_d[rows(me_d, rows_d), :]
    for step in range(1, n_d):
        acc = acc + first_d[step]
    summed_d[...] = acc
    out_d[rows(me_d, rows_d), :] = acc
    drop_copies = [
        send(summed_d, second_d.at[step], sd2.at[step], rd2.at[step], "drop", lax.rem(me_d + step, n_d))
        for step in range(1, n_d)
    ]

    wait_all(elec_b)
    acc = half_s[rows(chip, rows_e), :]
    for step in range(1, chips):
        acc = acc + buf_b[step]
    piece_t[...] = acc
    half_h[rows(chip, rows_e), :] = acc
    elec_c = [
        send(piece_t, buf_c.at[step], sc.at[step], rc.at[step], "elec", elec_peer(step))
        for step in range(1, chips)
    ]

    wait_all(drop_copies)
    for step in range(1, n_d):
        source = lax.rem(me_d - step + n_d, n_d)
        out_d[rows(source, rows_d), :] = second_d[step]

    wait_all(elec_c)
    for step in range(1, chips):
        source = lax.rem(chip - step + chips, chips)
        half_h[rows(source, rows_e), :] = buf_c[step]
    elec_d = [send(half_h, buf_d, sdd.at[0], rdd.at[0], "elec", partner)]
    out_e[pl.ds(mine, half), :] = half_h[...]
    wait_all(elec_d)
    out_e[pl.ds(other, half), :] = buf_d[...]


def all_reduce_both(part_elec, part_drop, sizes, collective):
    n_d, n_e = sizes
    chips = n_e // 2
    rows_d = part_elec.shape[0] // n_d
    half = part_drop.shape[0] // 2
    rows_e = half // chips
    cols_d = part_elec.shape[1]
    cols_e = part_drop.shape[1]
    f32 = jnp.float32
    scratch = [
        pltpu.VMEM((n_d, rows_d, cols_d), f32),
        pltpu.VMEM((n_d, rows_d, cols_d), f32),
        pltpu.VMEM((rows_d, cols_d), f32),
        pltpu.VMEM((half, cols_e), f32),
        pltpu.VMEM((chips, rows_e, cols_e), f32),
        pltpu.VMEM((chips, rows_e, cols_e), f32),
        pltpu.VMEM((half, cols_e), f32),
        pltpu.VMEM((half, cols_e), f32),
        pltpu.VMEM((rows_e, cols_e), f32),
        pltpu.VMEM((half, cols_e), f32),
    ]
    for count in (n_d, n_d, n_d, n_d, 1, 1, chips, chips, chips, chips, 1, 1):
        scratch.append(pltpu.SemaphoreType.DMA((count,)))
    vmem = pl.BlockSpec(memory_space=pltpu.VMEM)
    return pl.pallas_call(
        functools.partial(reduce_kernel, sizes),
        out_shape=(jax.ShapeDtypeStruct(part_elec.shape, f32), jax.ShapeDtypeStruct(part_drop.shape, f32)),
        in_specs=[vmem, vmem],
        out_specs=(vmem, vmem),
        scratch_shapes=scratch,
        compiler_params=pltpu.CompilerParams(collective_id=collective, has_side_effects=True),
    )(part_elec, part_drop)


def on_device(elec_pos, drop_vert, drop_conn, elec_rhs, drop_rhs, elec_inv, drop_inv):
    drop_devices = lax.axis_size("drop")
    elec_devices = lax.axis_size("elec")
    rhs_count, elec_local = elec_rhs.shape
    drop_local = drop_rhs.shape[1]
    screen, soften, couple = constants(drop_local * drop_devices)
    half_block = drop_vert.shape[1]
    local_conn = drop_conn - lax.axis_index("drop") * half_block
    centres = centroids(drop_vert, local_conn)
    kernel = lax.optimization_barrier(kernel_tile(elec_pos, centres, screen, soften, couple))

    charge_elec = block_solve(elec_inv, elec_rhs)
    charge_drop = block_solve(drop_inv, drop_rhs)
    for iteration in range(ITERS):
        part_elec = lax.dot_general(charge_drop, kernel, (((1,), (1,)), ((), ())), precision=FAST)
        part_drop = jnp.dot(charge_elec, kernel, precision=FAST)
        field_elec, field_drop = all_reduce_both(
            part_elec, part_drop, (drop_devices, elec_devices), iteration
        )
        charge_elec = block_solve(elec_inv, elec_rhs - field_elec)
        charge_drop = block_solve(drop_inv, drop_rhs - field_drop)
    return (charge_elec, charge_drop)


def solution(mesh):
    placed = (
        P(None, "elec"),
        P(None, "drop"),
        P(None, "drop"),
        P(None, "elec"),
        P(None, "drop"),
        P("elec", None, None),
        P("drop", None, None),
    )
    return jax.shard_map(
        on_device,
        mesh=mesh,
        in_specs=placed,
        out_specs=(P(None, "elec"), P(None, "drop")),
        check_vma=False,
    )
```

```python
import functools
import math

import jax
import jax.numpy as jnp
from jax import lax
from jax.experimental import pallas as pl
from jax.experimental.pallas import tpu as pltpu
from jax.sharding import PartitionSpec as P

ITERS = 2


HIGH = lax.Precision.HIGHEST
FAST = lax.Precision.HIGH
MESH = pl.DeviceIdType.MESH


def constants(total_drop):
    screen = 1.0
    soften = 0.001
    couple = 1.0 / (3.0 * math.sqrt(total_drop))
    return (screen, soften, couple)


def centroids(drop_vert, conn):
    vertices = lax.broadcasted_iota(jnp.int32, (drop_vert.shape[1], conn.shape[1]), 0)
    counts = sum((conn[k][None, :] == vertices).astype(jnp.float32) for k in range(3))
    counts = counts.astype(jnp.bfloat16)
    parts = []
    rest = drop_vert
    for _ in range(3):
        part = lax.reduce_precision(rest, exponent_bits=8, mantissa_bits=7)
        parts.append(part.astype(jnp.bfloat16))
        rest = rest - part
    stacked = jnp.concatenate(parts, axis=0)
    summed = jnp.dot(stacked, counts, preferred_element_type=jnp.float32)
    coords = drop_vert.shape[0]
    return (summed[:coords] + summed[coords:2 * coords] + summed[2 * coords:]) / 3.0


def kernel_tile(position, centres, screen, soften, couple):
    delta_x = position[0][:, None] - centres[0][None, :]
    delta_y = position[1][:, None] - centres[1][None, :]
    delta_z = position[2][:, None] - centres[2][None, :]
    distance = jnp.sqrt(delta_x * delta_x + delta_y * delta_y + delta_z * delta_z + soften)
    return couple * jnp.exp(-screen * distance) / distance


def block_solve(inverse, values):
    rhs_rows, columns = values.shape
    block_count, block_size, _ = inverse.shape
    shaped = values.reshape(rhs_rows, block_count, block_size)
    solved = jnp.einsum("bjk,rbk->rbj", inverse, shaped, precision=HIGH)
    return solved.reshape(rhs_rows, columns)


def reduce_kernel(plans, *refs):
    count = len(plans)
    ins = refs[:count]
    outs = refs[count:2 * count]
    rest = refs[2 * count:]
    bufs = [rest[6 * a:6 * a + 6] for a in range(count)]
    sems = rest[6 * count:]
    sems = [sems[8 * a:8 * a + 8] for a in range(count)]

    info = []
    for axis, size, stride in plans:
        me = lax.axis_index(axis)
        bit = lax.rem(me // stride, 2)
        partner = me + stride - 2 * stride * bit
        group = lax.rem(me, stride) + (me // (2 * stride)) * stride
        members = size // 2

        def member(offset, bit=bit, group=group, stride=stride, members=members):
            g = lax.rem(group + offset, members)
            return lax.rem(g, stride) + (g // stride) * 2 * stride + bit * stride

        info.append((axis, bit, partner, group, members, member))

    barrier = pltpu.get_barrier_semaphore()
    signals = 0
    for axis, bit, partner, group, members, member in info:
        pl.semaphore_signal(barrier, inc=1, device_id={axis: partner}, device_id_type=MESH)
        for step in range(1, members):
            pl.semaphore_signal(barrier, inc=1, device_id={axis: member(step)}, device_id_type=MESH)
        signals += members
    pl.semaphore_wait(barrier, signals)

    def send(src, dst, send_sem, recv_sem, axis, peer):
        copy = pltpu.make_async_remote_copy(
            src_ref=src, dst_ref=dst, send_sem=send_sem, recv_sem=recv_sem,
            device_id={axis: peer}, device_id_type=MESH,
        )
        copy.start()
        return copy

    def wait_all(copies):
        for copy in copies:
            copy.wait()

    shapes = []
    for a in range(count):
        half = ins[a].shape[0] // 2
        piece = half // info[a][4]
        mine = pl.multiple_of(info[a][1] * half, half)
        other = pl.multiple_of((1 - info[a][1]) * half, half)
        shapes.append((half, piece, mine, other))

    def rows(index, piece):
        return pl.ds(pl.multiple_of(index * piece, piece), piece)

    pending = []
    for a in range(count):
        axis, bit, partner, group, members, member = info[a]
        half, piece, mine, other = shapes[a]
        buf_a = bufs[a][0]
        pending.append([send(ins[a].at[pl.ds(other, half)], buf_a, sems[a][0].at[0], sems[a][1].at[0], axis, partner)])

    for a in range(count):
        axis, bit, partner, group, members, member = info[a]
        half, piece, mine, other = shapes[a]
        buf_a, buf_b, buf_c, buf_d, half_s, piece_t = bufs[a]
        wait_all(pending[a])
        half_s[...] = ins[a][pl.ds(mine, half), :] + buf_a[...]
        pending[a] = [
            send(half_s.at[rows(lax.rem(group + step, members), piece)], buf_b.at[step],
                 sems[a][2].at[step], sems[a][3].at[step], axis, member(step))
            for step in range(1, members)
        ]

    for a in range(count):
        axis, bit, partner, group, members, member = info[a]
        half, piece, mine, other = shapes[a]
        buf_a, buf_b, buf_c, buf_d, half_s, piece_t = bufs[a]
        wait_all(pending[a])
        acc = half_s[rows(group, piece), :]
        for step in range(1, members):
            acc = acc + buf_b[step]
        piece_t[...] = acc
        outs[a][pl.ds(mine + group * piece, piece), :] = acc
        pending[a] = [
            send(piece_t, buf_c.at[step], sems[a][4].at[step], sems[a][5].at[step], axis, member(step))
            for step in range(1, members)
        ]

    for a in range(count):
        axis, bit, partner, group, members, member = info[a]
        half, piece, mine, other = shapes[a]
        buf_a, buf_b, buf_c, buf_d, half_s, piece_t = bufs[a]
        wait_all(pending[a])
        for step in range(1, members):
            source = lax.rem(group - step + members, members)
            half_s[rows(source, piece), :] = buf_c[step]
        half_s[rows(group, piece), :] = piece_t[...]
        pending[a] = [send(half_s, buf_d, sems[a][6].at[0], sems[a][7].at[0], axis, partner)]
        outs[a][pl.ds(mine, half), :] = half_s[...]

    for a in range(count):
        half, piece, mine, other = shapes[a]
        wait_all(pending[a])
        outs[a][pl.ds(other, half), :] = bufs[a][3][...]


def all_reduce_both(part_elec, part_drop, plans, collective):
    operands = (part_elec, part_drop)
    f32 = jnp.float32
    scratch = []
    sem_shapes = []
    for x, (axis, size, stride) in zip(operands, plans):
        members = size // 2
        half = x.shape[0] // 2
        piece = half // members
        cols = x.shape[1]
        scratch += [
            pltpu.VMEM((half, cols), f32),
            pltpu.VMEM((members, piece, cols), f32),
            pltpu.VMEM((members, piece, cols), f32),
            pltpu.VMEM((half, cols), f32),
            pltpu.VMEM((half, cols), f32),
            pltpu.VMEM((piece, cols), f32),
        ]
        for slots in (1, 1, members, members, members, members, 1, 1):
            sem_shapes.append(pltpu.SemaphoreType.DMA((slots,)))
    vmem = pl.BlockSpec(memory_space=pltpu.VMEM)
    return pl.pallas_call(
        functools.partial(reduce_kernel, plans),
        out_shape=tuple(jax.ShapeDtypeStruct(x.shape, f32) for x in operands),
        in_specs=[vmem, vmem],
        out_specs=(vmem, vmem),
        scratch_shapes=scratch + sem_shapes,
        compiler_params=pltpu.CompilerParams(collective_id=collective, has_side_effects=True),
    )(*operands)


def on_device(elec_pos, drop_vert, drop_conn, elec_rhs, drop_rhs, elec_inv, drop_inv):
    drop_devices = lax.axis_size("drop")
    elec_devices = lax.axis_size("elec")
    rhs_count, elec_local = elec_rhs.shape
    drop_local = drop_rhs.shape[1]
    screen, soften, couple = constants(drop_local * drop_devices)
    half_block = drop_vert.shape[1]
    local_conn = drop_conn - lax.axis_index("drop") * half_block
    centres = centroids(drop_vert, local_conn)
    kernel = lax.optimization_barrier(kernel_tile(elec_pos, centres, screen, soften, couple))

    charge_elec = block_solve(elec_inv, elec_rhs)
    charge_drop = block_solve(drop_inv, drop_rhs)
    for iteration in range(ITERS):
        part_elec = lax.dot_general(charge_drop, kernel, (((1,), (1,)), ((), ())), precision=FAST)
        part_drop = jnp.dot(charge_elec, kernel, precision=FAST)
        plans = (("drop", drop_devices, drop_devices // 2), ("elec", elec_devices, 1))
        field_elec, field_drop = all_reduce_both(part_elec, part_drop, plans, iteration)
        charge_elec = block_solve(elec_inv, elec_rhs - field_elec)
        charge_drop = block_solve(drop_inv, drop_rhs - field_drop)
    return (charge_elec, charge_drop)


def solution(mesh):
    placed = (
        P(None, "elec"),
        P(None, "drop"),
        P(None, "drop"),
        P(None, "elec"),
        P(None, "drop"),
        P("elec", None, None),
        P("drop", None, None),
    )
    return jax.shard_map(
        on_device,
        mesh=mesh,
        in_specs=placed,
        out_specs=(P(None, "elec"), P(None, "drop")),
        check_vma=False,
    )
```

```python
import functools
import math

import jax
import jax.numpy as jnp
from jax import lax
from jax.experimental import pallas as pl
from jax.experimental.pallas import tpu as pltpu
from jax.sharding import PartitionSpec as P

ITERS = 2


HIGH = lax.Precision.HIGHEST
FAST = lax.Precision.HIGH
MESH = pl.DeviceIdType.MESH


def constants(total_drop):
    screen = 1.0
    soften = 0.001
    couple = 1.0 / (3.0 * math.sqrt(total_drop))
    return (screen, soften, couple)


def centroids(drop_vert, conn):
    vertices = lax.broadcasted_iota(jnp.int32, (drop_vert.shape[1], conn.shape[1]), 0)
    counts = sum((conn[k][None, :] == vertices).astype(jnp.float32) for k in range(3))
    counts = counts.astype(jnp.bfloat16)
    parts = []
    rest = drop_vert
    for _ in range(3):
        part = lax.reduce_precision(rest, exponent_bits=8, mantissa_bits=7)
        parts.append(part.astype(jnp.bfloat16))
        rest = rest - part
    stacked = jnp.concatenate(parts, axis=0)
    summed = jnp.dot(stacked, counts, preferred_element_type=jnp.float32)
    coords = drop_vert.shape[0]
    return (summed[:coords] + summed[coords:2 * coords] + summed[2 * coords:]) / 3.0


def kernel_tile(position, centres, screen, soften, couple):
    delta_x = position[0][:, None] - centres[0][None, :]
    delta_y = position[1][:, None] - centres[1][None, :]
    delta_z = position[2][:, None] - centres[2][None, :]
    distance = jnp.sqrt(delta_x * delta_x + delta_y * delta_y + delta_z * delta_z + soften)
    return couple * jnp.exp(-screen * distance) / distance


def block_solve(inverse, values):
    rhs_rows, columns = values.shape
    block_count, block_size, _ = inverse.shape
    shaped = values.reshape(rhs_rows, block_count, block_size)
    solved = jnp.einsum("bjk,rbk->rbj", inverse, shaped, precision=HIGH)
    return solved.reshape(rhs_rows, columns)


def reduce_kernel(plans, *refs):
    count = len(plans)
    ins = refs[:count]
    rhs = refs[count:2 * count]
    inv = refs[2 * count:3 * count]
    outs = refs[3 * count:4 * count]
    rest = refs[4 * count:]
    bufs = [rest[6 * a:6 * a + 6] for a in range(count)]
    sems = rest[6 * count:]
    sems = [sems[8 * a:8 * a + 8] for a in range(count)]

    info = []
    for axis, size, stride in plans:
        me = lax.axis_index(axis)
        bit = lax.rem(me // stride, 2)
        partner = me + stride - 2 * stride * bit
        group = lax.rem(me, stride) + (me // (2 * stride)) * stride
        members = size // 2

        def member(offset, bit=bit, group=group, stride=stride, members=members):
            g = lax.rem(group + offset, members)
            return lax.rem(g, stride) + (g // stride) * 2 * stride + bit * stride

        info.append((axis, bit, partner, group, members, member))

    barrier = pltpu.get_barrier_semaphore()
    signals = 0
    for axis, bit, partner, group, members, member in info:
        pl.semaphore_signal(barrier, inc=1, device_id={axis: partner}, device_id_type=MESH)
        for step in range(1, members):
            pl.semaphore_signal(barrier, inc=1, device_id={axis: member(step)}, device_id_type=MESH)
        signals += members
    pl.semaphore_wait(barrier, signals)

    def send(src, dst, send_sem, recv_sem, axis, peer):
        copy = pltpu.make_async_remote_copy(
            src_ref=src, dst_ref=dst, send_sem=send_sem, recv_sem=recv_sem,
            device_id={axis: peer}, device_id_type=MESH,
        )
        copy.start()
        return copy

    def wait_all(copies):
        for copy in copies:
            copy.wait()

    shapes = []
    for a in range(count):
        half = ins[a].shape[0] // 2
        piece = half // info[a][4]
        mine = pl.multiple_of(info[a][1] * half, half)
        other = pl.multiple_of((1 - info[a][1]) * half, half)
        shapes.append((half, piece, mine, other))

    def rows(index, piece):
        return pl.ds(pl.multiple_of(index * piece, piece), piece)

    pending = []
    for a in range(count):
        axis, bit, partner, group, members, member = info[a]
        half, piece, mine, other = shapes[a]
        buf_a = bufs[a][0]
        pending.append([send(ins[a].at[pl.ds(other, half)], buf_a, sems[a][0].at[0], sems[a][1].at[0], axis, partner)])

    for a in range(count):
        axis, bit, partner, group, members, member = info[a]
        half, piece, mine, other = shapes[a]
        buf_a, buf_b, buf_c, buf_d, half_s, piece_t = bufs[a]
        wait_all(pending[a])
        half_s[...] = ins[a][pl.ds(mine, half), :] + buf_a[...]
        pending[a] = [
            send(half_s.at[rows(lax.rem(group + step, members), piece)], buf_b.at[step],
                 sems[a][2].at[step], sems[a][3].at[step], axis, member(step))
            for step in range(1, members)
        ]

    for a in range(count):
        axis, bit, partner, group, members, member = info[a]
        half, piece, mine, other = shapes[a]
        buf_a, buf_b, buf_c, buf_d, half_s, piece_t = bufs[a]
        wait_all(pending[a])
        acc = half_s[rows(group, piece), :]
        for step in range(1, members):
            acc = acc + buf_b[step]
        values = rhs[a][pl.ds(mine + group * piece, piece), :] - acc
        size = inv[a].shape[1]
        for block in range(inv[a].shape[0]):
            columns = slice(block * size, (block + 1) * size)
            piece_t[:, columns] = lax.dot_general(
                values[:, columns], inv[a][block], (((1,), (1,)), ((), ())),
                precision=HIGH, preferred_element_type=jnp.float32,
            )
        outs[a][pl.ds(mine + group * piece, piece), :] = piece_t[...]
        pending[a] = [
            send(piece_t, buf_c.at[step], sems[a][4].at[step], sems[a][5].at[step], axis, member(step))
            for step in range(1, members)
        ]

    for a in range(count):
        axis, bit, partner, group, members, member = info[a]
        half, piece, mine, other = shapes[a]
        buf_a, buf_b, buf_c, buf_d, half_s, piece_t = bufs[a]
        wait_all(pending[a])
        for step in range(1, members):
            source = lax.rem(group - step + members, members)
            half_s[rows(source, piece), :] = buf_c[step]
        half_s[rows(group, piece), :] = piece_t[...]
        pending[a] = [send(half_s, buf_d, sems[a][6].at[0], sems[a][7].at[0], axis, partner)]
        outs[a][pl.ds(mine, half), :] = half_s[...]

    for a in range(count):
        half, piece, mine, other = shapes[a]
        wait_all(pending[a])
        outs[a][pl.ds(other, half), :] = bufs[a][3][...]


def sum_and_solve(part_elec, part_drop, elec_rhs, drop_rhs, elec_inv, drop_inv, plans, collective):
    operands = (part_elec, part_drop)
    f32 = jnp.float32
    scratch = []
    sem_shapes = []
    for x, (axis, size, stride) in zip(operands, plans):
        members = size // 2
        half = x.shape[0] // 2
        piece = half // members
        cols = x.shape[1]
        scratch += [
            pltpu.VMEM((half, cols), f32),
            pltpu.VMEM((members, piece, cols), f32),
            pltpu.VMEM((members, piece, cols), f32),
            pltpu.VMEM((half, cols), f32),
            pltpu.VMEM((half, cols), f32),
            pltpu.VMEM((piece, cols), f32),
        ]
        for slots in (1, 1, members, members, members, members, 1, 1):
            sem_shapes.append(pltpu.SemaphoreType.DMA((slots,)))
    vmem = pl.BlockSpec(memory_space=pltpu.VMEM)
    return pl.pallas_call(
        functools.partial(reduce_kernel, plans),
        out_shape=tuple(jax.ShapeDtypeStruct(x.shape, f32) for x in operands),
        in_specs=[vmem] * 6,
        out_specs=(vmem, vmem),
        scratch_shapes=scratch + sem_shapes,
        compiler_params=pltpu.CompilerParams(collective_id=collective, has_side_effects=True),
    )(part_elec, part_drop, elec_rhs, drop_rhs, elec_inv, drop_inv)


def on_device(elec_pos, drop_vert, drop_conn, elec_rhs, drop_rhs, elec_inv, drop_inv):
    drop_devices = lax.axis_size("drop")
    elec_devices = lax.axis_size("elec")
    rhs_count, elec_local = elec_rhs.shape
    drop_local = drop_rhs.shape[1]
    screen, soften, couple = constants(drop_local * drop_devices)
    half_block = drop_vert.shape[1]
    local_conn = drop_conn - lax.axis_index("drop") * half_block
    centres = centroids(drop_vert, local_conn)
    kernel = lax.optimization_barrier(kernel_tile(elec_pos, centres, screen, soften, couple))

    charge_elec = block_solve(elec_inv, elec_rhs)
    charge_drop = block_solve(drop_inv, drop_rhs)
    for iteration in range(ITERS):
        part_elec = lax.dot_general(charge_drop, kernel, (((1,), (1,)), ((), ())), precision=FAST)
        part_drop = jnp.dot(charge_elec, kernel, precision=FAST)
        plans = (("drop", drop_devices, drop_devices // 2), ("elec", elec_devices, 1))
        charge_elec, charge_drop = sum_and_solve(
            part_elec, part_drop, elec_rhs, drop_rhs, elec_inv, drop_inv, plans, iteration
        )
    return (charge_elec, charge_drop)


def solution(mesh):
    placed = (
        P(None, "elec"),
        P(None, "drop"),
        P(None, "drop"),
        P(None, "elec"),
        P(None, "drop"),
        P("elec", None, None),
        P("drop", None, None),
    )
    return jax.shard_map(
        on_device,
        mesh=mesh,
        in_specs=placed,
        out_specs=(P(None, "elec"), P(None, "drop")),
        check_vma=False,
    )
```

```python
import functools
import math

import jax
import jax.numpy as jnp
from jax import lax
from jax.experimental import pallas as pl
from jax.experimental.pallas import tpu as pltpu
from jax.sharding import PartitionSpec as P

ITERS = 2


HIGH = lax.Precision.HIGHEST
FAST = lax.Precision.HIGH
MESH = pl.DeviceIdType.MESH


def constants(total_drop):
    screen = 1.0
    soften = 0.001
    couple = 1.0 / (3.0 * math.sqrt(total_drop))
    return (screen, soften, couple)


def centroids(drop_vert, conn):
    vertices = lax.broadcasted_iota(jnp.int32, (drop_vert.shape[1], conn.shape[1]), 0)
    counts = sum((conn[k][None, :] == vertices).astype(jnp.float32) for k in range(3))
    counts = counts.astype(jnp.bfloat16)
    parts = []
    rest = drop_vert
    for _ in range(3):
        part = lax.reduce_precision(rest, exponent_bits=8, mantissa_bits=7)
        parts.append(part.astype(jnp.bfloat16))
        rest = rest - part
    stacked = jnp.concatenate(parts, axis=0)
    summed = jnp.dot(stacked, counts, preferred_element_type=jnp.float32)
    coords = drop_vert.shape[0]
    return (summed[:coords] + summed[coords:2 * coords] + summed[2 * coords:]) / 3.0


def kernel_tile(position, centres, screen, soften, couple):
    delta_x = position[0][:, None] - centres[0][None, :]
    delta_y = position[1][:, None] - centres[1][None, :]
    delta_z = position[2][:, None] - centres[2][None, :]
    distance = jnp.sqrt(delta_x * delta_x + delta_y * delta_y + delta_z * delta_z + soften)
    return couple * jnp.exp(-screen * distance) / distance


def block_solve(inverse, values):
    rhs_rows, columns = values.shape
    block_count, block_size, _ = inverse.shape
    shaped = values.reshape(rhs_rows, block_count, block_size)
    solved = jnp.einsum("bjk,rbk->rbj", inverse, shaped, precision=HIGH)
    return solved.reshape(rhs_rows, columns)


def axis_info(axis, size, stride):
    me = lax.axis_index(axis)
    bit = lax.rem(me // stride, 2)
    partner = me + stride - 2 * stride * bit
    group = lax.rem(me, stride) + (me // (2 * stride)) * stride
    members = size // 2

    def member(offset):
        g = lax.rem(group + offset, members)
        return lax.rem(g, stride) + (g // stride) * 2 * stride + bit * stride

    return (axis, bit, partner, group, members, member)


def send(src, dst, send_sem, recv_sem, axis, peer):
    copy = pltpu.make_async_remote_copy(
        src_ref=src, dst_ref=dst, send_sem=send_sem, recv_sem=recv_sem,
        device_id={axis: peer}, device_id_type=MESH,
    )
    copy.start()
    return copy


def wait_all(copies):
    for copy in copies:
        copy.wait()


def rows(index, piece):
    return pl.ds(pl.multiple_of(index * piece, piece), piece)


def exchange(info, ins, rhs, inv, outs, bufs, sems):
    count = len(info)
    shapes = []
    for a in range(count):
        half = ins[a].shape[0] // 2
        piece = half // info[a][4]
        mine = pl.multiple_of(info[a][1] * half, half)
        other = pl.multiple_of((1 - info[a][1]) * half, half)
        shapes.append((half, piece, mine, other))

    pending = []
    for a in range(count):
        axis, bit, partner, group, members, member = info[a]
        half, piece, mine, other = shapes[a]
        pending.append([send(ins[a].at[pl.ds(other, half)], bufs[a][0], sems[a][0].at[0], sems[a][1].at[0], axis, partner)])

    for a in range(count):
        axis, bit, partner, group, members, member = info[a]
        half, piece, mine, other = shapes[a]
        buf_a, buf_b, buf_c, buf_d, half_s, piece_t = bufs[a]
        wait_all(pending[a])
        half_s[...] = ins[a][pl.ds(mine, half), :] + buf_a[...]
        pending[a] = [
            send(half_s.at[rows(lax.rem(group + step, members), piece)], buf_b.at[step],
                 sems[a][2].at[step], sems[a][3].at[step], axis, member(step))
            for step in range(1, members)
        ]

    for a in range(count):
        axis, bit, partner, group, members, member = info[a]
        half, piece, mine, other = shapes[a]
        buf_a, buf_b, buf_c, buf_d, half_s, piece_t = bufs[a]
        wait_all(pending[a])
        acc = half_s[rows(group, piece), :]
        for step in range(1, members):
            acc = acc + buf_b[step]
        values = rhs[a][pl.ds(mine + group * piece, piece), :] - acc
        size = inv[a].shape[1]
        for block in range(inv[a].shape[0]):
            columns = slice(block * size, (block + 1) * size)
            piece_t[:, columns] = lax.dot_general(
                values[:, columns], inv[a][block], (((1,), (1,)), ((), ())),
                precision=HIGH, preferred_element_type=jnp.float32,
            )
        outs[a][pl.ds(mine + group * piece, piece), :] = piece_t[...]
        pending[a] = [
            send(piece_t, buf_c.at[step], sems[a][4].at[step], sems[a][5].at[step], axis, member(step))
            for step in range(1, members)
        ]

    for a in range(count):
        axis, bit, partner, group, members, member = info[a]
        half, piece, mine, other = shapes[a]
        buf_a, buf_b, buf_c, buf_d, half_s, piece_t = bufs[a]
        wait_all(pending[a])
        for step in range(1, members):
            source = lax.rem(group - step + members, members)
            half_s[rows(source, piece), :] = buf_c[step]
        half_s[rows(group, piece), :] = piece_t[...]
        pending[a] = [send(half_s, buf_d, sems[a][6].at[0], sems[a][7].at[0], axis, partner)]
        outs[a][pl.ds(mine, half), :] = half_s[...]

    for a in range(count):
        half, piece, mine, other = shapes[a]
        wait_all(pending[a])
        outs[a][pl.ds(other, half), :] = bufs[a][3][...]


def sweep_kernel(plans, iters, *refs):
    kernel, charge_elec, charge_drop, elec_rhs, drop_rhs, elec_inv, drop_inv = refs[:7]
    out_elec, out_drop = refs[7:9]
    part_elec, part_drop, mid_elec, mid_drop = refs[9:13]
    rest = refs[13:]
    count = len(plans)
    per_round = 6 * count
    bufs = [[rest[r * per_round + 6 * a:r * per_round + 6 * a + 6] for a in range(count)] for r in range(iters)]
    sem_base = iters * per_round
    sems = [[rest[sem_base + r * 8 * count + 8 * a:sem_base + r * 8 * count + 8 * a + 8] for a in range(count)]
            for r in range(iters)]
    info = [axis_info(*plan) for plan in plans]

    barrier = pltpu.get_barrier_semaphore()
    signals = 0
    for axis, bit, partner, group, members, member in info:
        pl.semaphore_signal(barrier, inc=1, device_id={axis: partner}, device_id_type=MESH)
        for step in range(1, members):
            pl.semaphore_signal(barrier, inc=1, device_id={axis: member(step)}, device_id_type=MESH)
        signals += members

    def partials(ce, cd):
        part_elec[...] = lax.dot_general(
            cd[...], kernel[...], (((1,), (1,)), ((), ())), precision=HIGH,
            preferred_element_type=jnp.float32)
        part_drop[...] = jnp.dot(ce[...], kernel[...], precision=HIGH, preferred_element_type=jnp.float32)

    partials(charge_elec, charge_drop)
    pl.semaphore_wait(barrier, signals)
    ce, cd = charge_elec, charge_drop
    for r in range(iters):
        targets = (out_elec, out_drop) if r == iters - 1 else (mid_elec, mid_drop)
        if r > 0:
            partials(ce, cd)
        exchange(info, (part_elec, part_drop), (elec_rhs, drop_rhs), (elec_inv, drop_inv),
                 targets, bufs[r], sems[r])
        ce, cd = targets


def sweeps(kernel, charge_elec, charge_drop, elec_rhs, drop_rhs, elec_inv, drop_inv, plans, iters):
    f32 = jnp.float32
    shapes = (charge_elec.shape, charge_drop.shape)
    scratch = [pltpu.VMEM(shape, f32) for shape in shapes] * 2
    sem_shapes = []
    for r in range(iters):
        for shape, (axis, size, stride) in zip(shapes, plans):
            members = size // 2
            half = shape[0] // 2
            piece = half // members
            cols = shape[1]
            scratch += [
                pltpu.VMEM((half, cols), f32),
                pltpu.VMEM((members, piece, cols), f32),
                pltpu.VMEM((members, piece, cols), f32),
                pltpu.VMEM((half, cols), f32),
                pltpu.VMEM((half, cols), f32),
                pltpu.VMEM((piece, cols), f32),
            ]
            for slots in (1, 1, members, members, members, members, 1, 1):
                sem_shapes.append(pltpu.SemaphoreType.DMA((slots,)))
    vmem = pl.BlockSpec(memory_space=pltpu.VMEM)
    return pl.pallas_call(
        functools.partial(sweep_kernel, plans, iters),
        out_shape=tuple(jax.ShapeDtypeStruct(shape, f32) for shape in shapes),
        in_specs=[vmem] * 7,
        out_specs=(vmem, vmem),
        scratch_shapes=scratch + sem_shapes,
        compiler_params=pltpu.CompilerParams(
            collective_id=0, has_side_effects=True, vmem_limit_bytes=60 * 1024 * 1024),
    )(kernel, charge_elec, charge_drop, elec_rhs, drop_rhs, elec_inv, drop_inv)


def on_device(elec_pos, drop_vert, drop_conn, elec_rhs, drop_rhs, elec_inv, drop_inv):
    drop_devices = lax.axis_size("drop")
    elec_devices = lax.axis_size("elec")
    rhs_count, elec_local = elec_rhs.shape
    drop_local = drop_rhs.shape[1]
    screen, soften, couple = constants(drop_local * drop_devices)
    half_block = drop_vert.shape[1]
    local_conn = drop_conn - lax.axis_index("drop") * half_block
    centres = centroids(drop_vert, local_conn)
    kernel = kernel_tile(elec_pos, centres, screen, soften, couple)

    charge_elec = block_solve(elec_inv, elec_rhs)
    charge_drop = block_solve(drop_inv, drop_rhs)
    plans = (("drop", drop_devices, drop_devices // 2), ("elec", elec_devices, 1))
    charge_elec, charge_drop = sweeps(
        kernel, charge_elec, charge_drop, elec_rhs, drop_rhs, elec_inv, drop_inv, plans, ITERS
    )
    return (charge_elec, charge_drop)


def solution(mesh):
    placed = (
        P(None, "elec"),
        P(None, "drop"),
        P(None, "drop"),
        P(None, "elec"),
        P(None, "drop"),
        P("elec", None, None),
        P("drop", None, None),
    )
    return jax.shard_map(
        on_device,
        mesh=mesh,
        in_specs=placed,
        out_specs=(P(None, "elec"), P(None, "drop")),
        check_vma=False,
    )
```

```python
import functools
import math

import jax
import jax.numpy as jnp
from jax import lax
from jax.experimental import pallas as pl
from jax.experimental.pallas import tpu as pltpu
from jax.sharding import PartitionSpec as P

ITERS = 2


HIGH = lax.Precision.HIGHEST
FAST = lax.Precision.HIGH
MESH = pl.DeviceIdType.MESH


def constants(total_drop):
    screen = 1.0
    soften = 0.001
    couple = 1.0 / (3.0 * math.sqrt(total_drop))
    return (screen, soften, couple)


def centroids(drop_vert, conn):
    vertices = lax.broadcasted_iota(jnp.int32, (drop_vert.shape[1], conn.shape[1]), 0)
    counts = sum((conn[k][None, :] == vertices).astype(jnp.float32) for k in range(3))
    counts = counts.astype(jnp.bfloat16)
    parts = []
    rest = drop_vert
    for _ in range(3):
        part = lax.reduce_precision(rest, exponent_bits=8, mantissa_bits=7)
        parts.append(part.astype(jnp.bfloat16))
        rest = rest - part
    stacked = jnp.concatenate(parts, axis=0)
    summed = jnp.dot(stacked, counts, preferred_element_type=jnp.float32)
    coords = drop_vert.shape[0]
    return (summed[:coords] + summed[coords:2 * coords] + summed[2 * coords:]) / 3.0


def kernel_tile(position, centres, screen, soften, couple):
    delta_x = position[0][:, None] - centres[0][None, :]
    delta_y = position[1][:, None] - centres[1][None, :]
    delta_z = position[2][:, None] - centres[2][None, :]
    distance = jnp.sqrt(delta_x * delta_x + delta_y * delta_y + delta_z * delta_z + soften)
    return couple * jnp.exp(-screen * distance) / distance


def block_solve(inverse, values):
    rhs_rows, columns = values.shape
    block_count, block_size, _ = inverse.shape
    shaped = values.reshape(rhs_rows, block_count, block_size)
    solved = jnp.einsum("bjk,rbk->rbj", inverse, shaped, precision=HIGH)
    return solved.reshape(rhs_rows, columns)


def axis_info(axis, size, stride):
    me = lax.axis_index(axis)
    bit = lax.rem(me // stride, 2)
    partner = me + stride - 2 * stride * bit
    group = lax.rem(me, stride) + (me // (2 * stride)) * stride
    members = size // 2

    def member(offset):
        g = lax.rem(group + offset, members)
        return lax.rem(g, stride) + (g // stride) * 2 * stride + bit * stride

    return (axis, bit, partner, group, members, member)


def send(src, dst, send_sem, recv_sem, axis, peer):
    copy = pltpu.make_async_remote_copy(
        src_ref=src, dst_ref=dst, send_sem=send_sem, recv_sem=recv_sem,
        device_id={axis: peer}, device_id_type=MESH,
    )
    copy.start()
    return copy


def wait_all(copies):
    for copy in copies:
        copy.wait()


def rows(index, piece):
    return pl.ds(pl.multiple_of(index * piece, piece), piece)


def exchange(info, source, rhs, inv, out, bufs, sems, first, width):
    axis, bit, partner, group, members, member = info
    half = source.shape[0] // 2
    piece = half // members
    mine = pl.multiple_of(bit * half, half)
    other = pl.multiple_of((1 - bit) * half, half)
    cols = pl.ds(first, width)
    buf_a, buf_b, buf_c, buf_d, half_s, piece_t = bufs

    pending = [send(source.at[pl.ds(other, half), cols], buf_a, sems[0].at[0], sems[1].at[0], axis, partner)]
    yield
    wait_all(pending)
    half_s[...] = source[pl.ds(mine, half), cols] + buf_a[...]
    pending = [
        send(half_s.at[rows(lax.rem(group + step, members), piece)], buf_b.at[step],
             sems[2].at[step], sems[3].at[step], axis, member(step))
        for step in range(1, members)
    ]
    yield
    wait_all(pending)
    acc = half_s[rows(group, piece), :]
    for step in range(1, members):
        acc = acc + buf_b[step]
    values = rhs[pl.ds(mine + group * piece, piece), cols] - acc
    size = inv.shape[1]
    for block in range(width // size):
        local = slice(block * size, (block + 1) * size)
        piece_t[:, local] = lax.dot_general(
            values[:, local], inv[first // size + block], (((1,), (1,)), ((), ())),
            precision=HIGH, preferred_element_type=jnp.float32,
        )
    out[pl.ds(mine + group * piece, piece), cols] = piece_t[...]
    pending = [
        send(piece_t, buf_c.at[step], sems[4].at[step], sems[5].at[step], axis, member(step))
        for step in range(1, members)
    ]
    yield
    wait_all(pending)
    for step in range(1, members):
        origin = lax.rem(group - step + members, members)
        half_s[rows(origin, piece), :] = buf_c[step]
    half_s[rows(group, piece), :] = piece_t[...]
    pending = [send(half_s, buf_d, sems[6].at[0], sems[7].at[0], axis, partner)]
    out[pl.ds(mine, half), cols] = half_s[...]
    yield
    wait_all(pending)
    out[pl.ds(other, half), cols] = buf_d[...]


def run_all(gens):
    live = list(gens)
    while live:
        still = []
        for gen in live:
            try:
                next(gen)
                still.append(gen)
            except StopIteration:
                pass
        live = still


def sweep_kernel(plans, iters, chunks, *refs):
    kernel, charge_elec, charge_drop, elec_rhs, drop_rhs, elec_inv, drop_inv = refs[:7]
    out_elec, out_drop = refs[7:9]
    part_elec, part_drop, mid_elec, mid_drop = refs[9:13]
    rest = refs[13:]
    count = len(plans)
    per = iters * count * chunks
    bufs = [rest[6 * g:6 * g + 6] for g in range(per)]
    sems = [rest[6 * per + 8 * g:6 * per + 8 * g + 8] for g in range(per)]
    info = [axis_info(*plan) for plan in plans]

    barrier = pltpu.get_barrier_semaphore()
    signals = 0
    for axis, bit, partner, group, members, member in info:
        pl.semaphore_signal(barrier, inc=1, device_id={axis: partner}, device_id_type=MESH)
        for step in range(1, members):
            pl.semaphore_signal(barrier, inc=1, device_id={axis: member(step)}, device_id_type=MESH)
        signals += members

    parts = (part_elec, part_drop)
    rhs = (elec_rhs, drop_rhs)
    inv = (elec_inv, drop_inv)

    def partial(a, ce, cd):
        if a == 0:
            part_elec[...] = lax.dot_general(
                cd[...], kernel[...], (((1,), (1,)), ((), ())), precision=HIGH,
                preferred_element_type=jnp.float32)
        else:
            part_drop[...] = jnp.dot(ce[...], kernel[...], precision=HIGH, preferred_element_type=jnp.float32)

    def gens(r, a, target):
        width = parts[a].shape[1] // chunks
        out = []
        for c in range(chunks):
            g = (r * count + a) * chunks + c
            out.append(exchange(info[a], parts[a], rhs[a], inv[a], target, bufs[g], sems[g], c * width, width))
        return out

    partial(0, charge_elec, charge_drop)
    partial(1, charge_elec, charge_drop)
    pl.semaphore_wait(barrier, signals)
    mids = (mid_elec, mid_drop)
    outs = (out_elec, out_drop)
    current = [gens(0, 0, mids[0] if iters > 1 else outs[0]), gens(0, 1, mids[1] if iters > 1 else outs[1])]
    for r in range(1, iters):
        target = outs if r == iters - 1 else mids
        for _ in range(4):
            for gen in current[0] + current[1]:
                next(gen)
        run_all(current[0])
        partial(1, mids[0], mids[1])
        following = gens(r, 1, target[1])
        for gen in following:
            next(gen)
        run_all(current[1])
        partial(0, mids[0], mids[1])
        current = [gens(r, 0, target[0]), following]
    run_all(current[0] + current[1])


def sweeps(kernel, charge_elec, charge_drop, elec_rhs, drop_rhs, elec_inv, drop_inv, plans, iters, chunks=2):
    f32 = jnp.float32
    shapes = (charge_elec.shape, charge_drop.shape)
    scratch = [pltpu.VMEM(shape, f32) for shape in shapes] * 2
    sem_shapes = []
    for shape, (axis, size, stride) in [item for _ in range(iters) for item in zip(shapes, plans) for _c in range(chunks)]:
            members = size // 2
            half = shape[0] // 2
            piece = half // members
            cols = shape[1] // chunks
            scratch += [
                pltpu.VMEM((half, cols), f32),
                pltpu.VMEM((members, piece, cols), f32),
                pltpu.VMEM((members, piece, cols), f32),
                pltpu.VMEM((half, cols), f32),
                pltpu.VMEM((half, cols), f32),
                pltpu.VMEM((piece, cols), f32),
            ]
            for slots in (1, 1, members, members, members, members, 1, 1):
                sem_shapes.append(pltpu.SemaphoreType.DMA((slots,)))
    vmem = pl.BlockSpec(memory_space=pltpu.VMEM)
    return pl.pallas_call(
        functools.partial(sweep_kernel, plans, iters, chunks),
        out_shape=tuple(jax.ShapeDtypeStruct(shape, f32) for shape in shapes),
        in_specs=[vmem] * 7,
        out_specs=(vmem, vmem),
        scratch_shapes=scratch + sem_shapes,
        compiler_params=pltpu.CompilerParams(
            collective_id=0, has_side_effects=True, vmem_limit_bytes=60 * 1024 * 1024),
    )(kernel, charge_elec, charge_drop, elec_rhs, drop_rhs, elec_inv, drop_inv)


def on_device(elec_pos, drop_vert, drop_conn, elec_rhs, drop_rhs, elec_inv, drop_inv):
    drop_devices = lax.axis_size("drop")
    elec_devices = lax.axis_size("elec")
    rhs_count, elec_local = elec_rhs.shape
    drop_local = drop_rhs.shape[1]
    screen, soften, couple = constants(drop_local * drop_devices)
    half_block = drop_vert.shape[1]
    local_conn = drop_conn - lax.axis_index("drop") * half_block
    centres = centroids(drop_vert, local_conn)
    kernel = kernel_tile(elec_pos, centres, screen, soften, couple)

    charge_elec = block_solve(elec_inv, elec_rhs)
    charge_drop = block_solve(drop_inv, drop_rhs)
    plans = (("drop", drop_devices, drop_devices // 2), ("elec", elec_devices, 1))
    charge_elec, charge_drop = sweeps(
        kernel, charge_elec, charge_drop, elec_rhs, drop_rhs, elec_inv, drop_inv, plans, ITERS
    )
    return (charge_elec, charge_drop)


def solution(mesh):
    placed = (
        P(None, "elec"),
        P(None, "drop"),
        P(None, "drop"),
        P(None, "elec"),
        P(None, "drop"),
        P("elec", None, None),
        P("drop", None, None),
    )
    return jax.shard_map(
        on_device,
        mesh=mesh,
        in_specs=placed,
        out_specs=(P(None, "elec"), P(None, "drop")),
        check_vma=False,
    )
```

```python
import functools
import math

import jax
import jax.numpy as jnp
from jax import lax
from jax.experimental import pallas as pl
from jax.experimental.pallas import tpu as pltpu
from jax.sharding import PartitionSpec as P

ITERS = 2


HIGH = lax.Precision.HIGHEST
FAST = lax.Precision.HIGH
MESH = pl.DeviceIdType.MESH


def constants(total_drop):
    screen = 1.0
    soften = 0.001
    couple = 1.0 / (3.0 * math.sqrt(total_drop))
    return (screen, soften, couple)


def centroids(drop_vert, conn):
    vertices = lax.broadcasted_iota(jnp.int32, (drop_vert.shape[1], conn.shape[1]), 0)
    counts = sum((conn[k][None, :] == vertices).astype(jnp.float32) for k in range(3))
    counts = counts.astype(jnp.bfloat16)
    parts = []
    rest = drop_vert
    for _ in range(3):
        part = lax.reduce_precision(rest, exponent_bits=8, mantissa_bits=7)
        parts.append(part.astype(jnp.bfloat16))
        rest = rest - part
    stacked = jnp.concatenate(parts, axis=0)
    summed = jnp.dot(stacked, counts, preferred_element_type=jnp.float32)
    coords = drop_vert.shape[0]
    return (summed[:coords] + summed[coords:2 * coords] + summed[2 * coords:]) / 3.0


def kernel_tile(position, centres, screen, soften, couple):
    delta_x = position[0][:, None] - centres[0][None, :]
    delta_y = position[1][:, None] - centres[1][None, :]
    delta_z = position[2][:, None] - centres[2][None, :]
    distance = jnp.sqrt(delta_x * delta_x + delta_y * delta_y + delta_z * delta_z + soften)
    return couple * jnp.exp(-screen * distance) / distance


def block_solve(inverse, values):
    rhs_rows, columns = values.shape
    block_count, block_size, _ = inverse.shape
    shaped = values.reshape(rhs_rows, block_count, block_size)
    solved = jnp.einsum("bjk,rbk->rbj", inverse, shaped, precision=HIGH)
    return solved.reshape(rhs_rows, columns)


def axis_info(axis, size, stride):
    me = lax.axis_index(axis)
    bit = lax.rem(me // stride, 2)
    partner = me + stride - 2 * stride * bit
    group = lax.rem(me, stride) + (me // (2 * stride)) * stride
    members = size // 2

    def member(offset):
        g = lax.rem(group + offset, members)
        return lax.rem(g, stride) + (g // stride) * 2 * stride + bit * stride

    return (axis, bit, partner, group, members, member)


def send(src, dst, send_sem, recv_sem, axis, peer):
    copy = pltpu.make_async_remote_copy(
        src_ref=src, dst_ref=dst, send_sem=send_sem, recv_sem=recv_sem,
        device_id={axis: peer}, device_id_type=MESH,
    )
    copy.start()
    return copy


def wait_all(copies):
    for copy in copies:
        copy.wait()


def rows(index, piece):
    return pl.ds(pl.multiple_of(index * piece, piece), piece)


def exchange(info, source, rhs, inv, out, bufs, sems, first, width):
    axis, bit, partner, group, members, member = info
    half = source.shape[0] // 2
    piece = half // members
    mine = pl.multiple_of(bit * half, half)
    other = pl.multiple_of((1 - bit) * half, half)
    cols = pl.ds(first, width)
    buf_a, buf_b, buf_c, buf_d, half_s, piece_t = bufs

    pending = [send(source.at[pl.ds(other, half), cols], buf_a, sems[0].at[0], sems[1].at[0], axis, partner)]
    yield
    wait_all(pending)
    half_s[...] = source[pl.ds(mine, half), cols] + buf_a[...]
    pending = [
        send(half_s.at[rows(lax.rem(group + step, members), piece)], buf_b.at[step],
             sems[2].at[step], sems[3].at[step], axis, member(step))
        for step in range(1, members)
    ]
    yield
    wait_all(pending)
    acc = half_s[rows(group, piece), :]
    for step in range(1, members):
        acc = acc + buf_b[step]
    values = rhs[pl.ds(mine + group * piece, piece), cols] - acc
    size = inv.shape[1]
    for block in range(width // size):
        local = slice(block * size, (block + 1) * size)
        piece_t[:, local] = lax.dot_general(
            values[:, local], inv[first // size + block], (((1,), (1,)), ((), ())),
            precision=HIGH, preferred_element_type=jnp.float32,
        )
    out[pl.ds(mine + group * piece, piece), cols] = piece_t[...]
    pending = [
        send(piece_t, buf_c.at[step], sems[4].at[step], sems[5].at[step], axis, member(step))
        for step in range(1, members)
    ]
    yield
    wait_all(pending)
    for step in range(1, members):
        origin = lax.rem(group - step + members, members)
        half_s[rows(origin, piece), :] = buf_c[step]
    half_s[rows(group, piece), :] = piece_t[...]
    pending = [send(half_s, buf_d, sems[6].at[0], sems[7].at[0], axis, partner)]
    out[pl.ds(mine, half), cols] = half_s[...]
    yield
    wait_all(pending)
    out[pl.ds(other, half), cols] = buf_d[...]


def run_all(gens):
    live = list(gens)
    while live:
        still = []
        for gen in live:
            try:
                next(gen)
                still.append(gen)
            except StopIteration:
                pass
        live = still


def sweep_kernel(plans, iters, chunks, *refs):
    kernel, charge_elec, charge_drop, elec_rhs, drop_rhs, elec_inv, drop_inv = refs[:7]
    out_elec, out_drop = refs[7:9]
    part_elec, part_drop, mid_elec, mid_drop = refs[9:13]
    rest = refs[13:]
    count = len(plans)
    per = iters * count * chunks
    bufs = [rest[6 * g:6 * g + 6] for g in range(per)]
    sems = [rest[6 * per + 8 * g:6 * per + 8 * g + 8] for g in range(per)]
    info = [axis_info(*plan) for plan in plans]

    barrier = pltpu.get_barrier_semaphore()
    signals = 0
    for axis, bit, partner, group, members, member in info:
        pl.semaphore_signal(barrier, inc=1, device_id={axis: partner}, device_id_type=MESH)
        for step in range(1, members):
            pl.semaphore_signal(barrier, inc=1, device_id={axis: member(step)}, device_id_type=MESH)
        signals += members

    parts = (part_elec, part_drop)
    rhs = (elec_rhs, drop_rhs)
    inv = (elec_inv, drop_inv)

    def partial(a, ce, cd):
        if a == 0:
            part_elec[...] = lax.dot_general(
                cd[...], kernel[...], (((1,), (1,)), ((), ())), precision=HIGH,
                preferred_element_type=jnp.float32)
        else:
            part_drop[...] = jnp.dot(ce[...], kernel[...], precision=HIGH, preferred_element_type=jnp.float32)

    def gens(r, a, target):
        width = parts[a].shape[1] // chunks
        out = []
        for c in range(chunks):
            g = (r * count + a) * chunks + c
            out.append(exchange(info[a], parts[a], rhs[a], inv[a], target, bufs[g], sems[g], c * width, width))
        return out

    partial(0, charge_elec, charge_drop)
    partial(1, charge_elec, charge_drop)
    pl.semaphore_wait(barrier, signals)
    mids = (mid_elec, mid_drop)
    outs = (out_elec, out_drop)
    current = [gens(0, 0, mids[0] if iters > 1 else outs[0]), gens(0, 1, mids[1] if iters > 1 else outs[1])]
    for r in range(1, iters):
        target = outs if r == iters - 1 else mids
        for _ in range(4):
            for gen in current[0] + current[1]:
                next(gen)
        run_all(current[0])
        partial(1, mids[0], mids[1])
        following = gens(r, 1, target[1])
        for gen in following:
            next(gen)
        run_all(current[1])
        partial(0, mids[0], mids[1])
        current = [gens(r, 0, target[0]), following]
    run_all(current[0] + current[1])


def sweeps(kernel, charge_elec, charge_drop, elec_rhs, drop_rhs, elec_inv, drop_inv, plans, iters, chunks=4):
    f32 = jnp.float32
    shapes = (charge_elec.shape, charge_drop.shape)
    scratch = [pltpu.VMEM(shape, f32) for shape in shapes] * 2
    sem_shapes = []
    for shape, (axis, size, stride) in [item for _ in range(iters) for item in zip(shapes, plans) for _c in range(chunks)]:
            members = size // 2
            half = shape[0] // 2
            piece = half // members
            cols = shape[1] // chunks
            scratch += [
                pltpu.VMEM((half, cols), f32),
                pltpu.VMEM((members, piece, cols), f32),
                pltpu.VMEM((members, piece, cols), f32),
                pltpu.VMEM((half, cols), f32),
                pltpu.VMEM((half, cols), f32),
                pltpu.VMEM((piece, cols), f32),
            ]
            for slots in (1, 1, members, members, members, members, 1, 1):
                sem_shapes.append(pltpu.SemaphoreType.DMA((slots,)))
    vmem = pl.BlockSpec(memory_space=pltpu.VMEM)
    return pl.pallas_call(
        functools.partial(sweep_kernel, plans, iters, chunks),
        out_shape=tuple(jax.ShapeDtypeStruct(shape, f32) for shape in shapes),
        in_specs=[vmem] * 7,
        out_specs=(vmem, vmem),
        scratch_shapes=scratch + sem_shapes,
        compiler_params=pltpu.CompilerParams(
            collective_id=0, has_side_effects=True, vmem_limit_bytes=60 * 1024 * 1024),
    )(kernel, charge_elec, charge_drop, elec_rhs, drop_rhs, elec_inv, drop_inv)


def on_device(elec_pos, drop_vert, drop_conn, elec_rhs, drop_rhs, elec_inv, drop_inv):
    drop_devices = lax.axis_size("drop")
    elec_devices = lax.axis_size("elec")
    rhs_count, elec_local = elec_rhs.shape
    drop_local = drop_rhs.shape[1]
    screen, soften, couple = constants(drop_local * drop_devices)
    half_block = drop_vert.shape[1]
    local_conn = drop_conn - lax.axis_index("drop") * half_block
    centres = centroids(drop_vert, local_conn)
    kernel = kernel_tile(elec_pos, centres, screen, soften, couple)

    charge_elec = block_solve(elec_inv, elec_rhs)
    charge_drop = block_solve(drop_inv, drop_rhs)
    plans = (("drop", drop_devices, drop_devices // 2), ("elec", elec_devices, 1))
    charge_elec, charge_drop = sweeps(
        kernel, charge_elec, charge_drop, elec_rhs, drop_rhs, elec_inv, drop_inv, plans, ITERS
    )
    return (charge_elec, charge_drop)


def solution(mesh):
    placed = (
        P(None, "elec"),
        P(None, "drop"),
        P(None, "drop"),
        P(None, "elec"),
        P(None, "drop"),
        P("elec", None, None),
        P("drop", None, None),
    )
    return jax.shard_map(
        on_device,
        mesh=mesh,
        in_specs=placed,
        out_specs=(P(None, "elec"), P(None, "drop")),
        check_vma=False,
    )
```

```python
import functools
import math

import jax
import jax.numpy as jnp
from jax import lax
from jax.experimental import pallas as pl
from jax.experimental.pallas import tpu as pltpu
from jax.sharding import PartitionSpec as P

ITERS = 2


HIGH = lax.Precision.HIGHEST
FAST = lax.Precision.HIGH
MESH = pl.DeviceIdType.MESH


def constants(total_drop):
    screen = 1.0
    soften = 0.001
    couple = 1.0 / (3.0 * math.sqrt(total_drop))
    return (screen, soften, couple)


def centroids(drop_vert, conn):
    vertices = lax.broadcasted_iota(jnp.int32, (drop_vert.shape[1], conn.shape[1]), 0)
    counts = sum((conn[k][None, :] == vertices).astype(jnp.float32) for k in range(3))
    counts = counts.astype(jnp.bfloat16)
    parts = []
    rest = drop_vert
    for _ in range(3):
        part = lax.reduce_precision(rest, exponent_bits=8, mantissa_bits=7)
        parts.append(part.astype(jnp.bfloat16))
        rest = rest - part
    stacked = jnp.concatenate(parts, axis=0)
    summed = jnp.dot(stacked, counts, preferred_element_type=jnp.float32)
    coords = drop_vert.shape[0]
    return (summed[:coords] + summed[coords:2 * coords] + summed[2 * coords:]) / 3.0


def kernel_tile(position, centres, screen, soften, couple):
    delta_x = position[0][:, None] - centres[0][None, :]
    delta_y = position[1][:, None] - centres[1][None, :]
    delta_z = position[2][:, None] - centres[2][None, :]
    distance = jnp.sqrt(delta_x * delta_x + delta_y * delta_y + delta_z * delta_z + soften)
    return couple * jnp.exp(-screen * distance) / distance


def block_solve(inverse, values):
    rhs_rows, columns = values.shape
    block_count, block_size, _ = inverse.shape
    shaped = values.reshape(rhs_rows, block_count, block_size)
    solved = jnp.einsum("bjk,rbk->rbj", inverse, shaped, precision=HIGH)
    return solved.reshape(rhs_rows, columns)


def axis_info(axis, size, stride):
    me = lax.axis_index(axis)
    bit = lax.rem(me // stride, 2)
    partner = me + stride - 2 * stride * bit
    group = lax.rem(me, stride) + (me // (2 * stride)) * stride
    members = size // 2

    def member(offset):
        g = lax.rem(group + offset, members)
        return lax.rem(g, stride) + (g // stride) * 2 * stride + bit * stride

    return (axis, bit, partner, group, members, member)


def send(src, dst, send_sem, recv_sem, axis, peer):
    copy = pltpu.make_async_remote_copy(
        src_ref=src, dst_ref=dst, send_sem=send_sem, recv_sem=recv_sem,
        device_id={axis: peer}, device_id_type=MESH,
    )
    copy.start()
    return copy


def wait_all(copies):
    for copy in copies:
        copy.wait()


def rows(index, piece):
    return pl.ds(pl.multiple_of(index * piece, piece), piece)


def exchange(info, source, rhs, inv, out, bufs, sems, first, width):
    axis, bit, partner, group, members, member = info
    half = source.shape[0] // 2
    piece = half // members
    mine = pl.multiple_of(bit * half, half)
    other = pl.multiple_of((1 - bit) * half, half)
    cols = pl.ds(first, width)
    buf_a, buf_b, buf_c, buf_d, half_s, piece_t = bufs

    pending = [send(source.at[pl.ds(other, half), cols], buf_a, sems[0].at[0], sems[1].at[0], axis, partner)]
    yield
    wait_all(pending)
    half_s[...] = source[pl.ds(mine, half), cols] + buf_a[...]
    pending = [
        send(half_s.at[rows(lax.rem(group + step, members), piece)], buf_b.at[step],
             sems[2].at[step], sems[3].at[step], axis, member(step))
        for step in range(1, members)
    ]
    yield
    wait_all(pending)
    acc = half_s[rows(group, piece), :]
    for step in range(1, members):
        acc = acc + buf_b[step]
    values = rhs[pl.ds(mine + group * piece, piece), cols] - acc
    size = inv.shape[1]
    for block in range(width // size):
        local = slice(block * size, (block + 1) * size)
        piece_t[:, local] = lax.dot_general(
            values[:, local], inv[first // size + block], (((1,), (1,)), ((), ())),
            precision=HIGH, preferred_element_type=jnp.float32,
        )
    out[pl.ds(mine + group * piece, piece), cols] = piece_t[...]
    pending = [
        send(piece_t, buf_c.at[step], sems[4].at[step], sems[5].at[step], axis, member(step))
        for step in range(1, members)
    ]
    yield
    wait_all(pending)
    for step in range(1, members):
        origin = lax.rem(group - step + members, members)
        half_s[rows(origin, piece), :] = buf_c[step]
    half_s[rows(group, piece), :] = piece_t[...]
    pending = [send(half_s, buf_d, sems[6].at[0], sems[7].at[0], axis, partner)]
    out[pl.ds(mine, half), cols] = half_s[...]
    yield
    wait_all(pending)
    out[pl.ds(other, half), cols] = buf_d[...]


def run_all(gens):
    live = list(gens)
    while live:
        still = []
        for gen in live:
            try:
                next(gen)
                still.append(gen)
            except StopIteration:
                pass
        live = still


def sweep_kernel(plans, iters, chunks, *refs):
    kernel, charge_elec, charge_drop, elec_rhs, drop_rhs, elec_inv, drop_inv = refs[:7]
    out_elec, out_drop = refs[7:9]
    part_elec, part_drop, mid_elec, mid_drop = refs[9:13]
    rest = refs[13:]
    count = len(plans)
    per = iters * count * chunks
    bufs = [rest[6 * g:6 * g + 6] for g in range(per)]
    sems = [rest[6 * per + 8 * g:6 * per + 8 * g + 8] for g in range(per)]
    info = [axis_info(*plan) for plan in plans]

    barrier = pltpu.get_barrier_semaphore()
    signals = 0
    for axis, bit, partner, group, members, member in info:
        pl.semaphore_signal(barrier, inc=1, device_id={axis: partner}, device_id_type=MESH)
        for step in range(1, members):
            pl.semaphore_signal(barrier, inc=1, device_id={axis: member(step)}, device_id_type=MESH)
        signals += members

    parts = (part_elec, part_drop)
    rhs = (elec_rhs, drop_rhs)
    inv = (elec_inv, drop_inv)

    def partial(a, c, ce, cd):
        width = parts[a].shape[1] // chunks
        cols = slice(c * width, (c + 1) * width)
        if a == 0:
            part_elec[:, cols] = lax.dot_general(
                cd[...], kernel[cols, :], (((1,), (1,)), ((), ())), precision=HIGH,
                preferred_element_type=jnp.float32)
        else:
            part_drop[:, cols] = jnp.dot(
                ce[...], kernel[:, cols], precision=HIGH, preferred_element_type=jnp.float32)

    def gens(r, a, target):
        width = parts[a].shape[1] // chunks
        out = []
        for c in range(chunks):
            g = (r * count + a) * chunks + c
            out.append(exchange(info[a], parts[a], rhs[a], inv[a], target, bufs[g], sems[g], c * width, width))
        return out

    mids = (mid_elec, mid_drop)
    outs = (out_elec, out_drop)
    current = [gens(0, 0, mids[0] if iters > 1 else outs[0]), gens(0, 1, mids[1] if iters > 1 else outs[1])]
    for c in range(chunks):
        partial(0, c, charge_elec, charge_drop)
        partial(1, c, charge_elec, charge_drop)
        if c == 0:
            pl.semaphore_wait(barrier, signals)
        next(current[0][c])
        next(current[1][c])
    for r in range(1, iters):
        target = outs if r == iters - 1 else mids
        for _ in range(3):
            for gen in current[0] + current[1]:
                next(gen)
        run_all(current[0])
        following = gens(r, 1, target[1])
        for c in range(chunks):
            partial(1, c, mids[0], mids[1])
            next(following[c])
        run_all(current[1])
        leading = gens(r, 0, target[0])
        for c in range(chunks):
            partial(0, c, mids[0], mids[1])
            next(leading[c])
        current = [leading, following]
    run_all(current[0] + current[1])


def sweeps(kernel, charge_elec, charge_drop, elec_rhs, drop_rhs, elec_inv, drop_inv, plans, iters, chunks=2):
    f32 = jnp.float32
    shapes = (charge_elec.shape, charge_drop.shape)
    scratch = [pltpu.VMEM(shape, f32) for shape in shapes] * 2
    sem_shapes = []
    for shape, (axis, size, stride) in [item for _ in range(iters) for item in zip(shapes, plans) for _c in range(chunks)]:
            members = size // 2
            half = shape[0] // 2
            piece = half // members
            cols = shape[1] // chunks
            scratch += [
                pltpu.VMEM((half, cols), f32),
                pltpu.VMEM((members, piece, cols), f32),
                pltpu.VMEM((members, piece, cols), f32),
                pltpu.VMEM((half, cols), f32),
                pltpu.VMEM((half, cols), f32),
                pltpu.VMEM((piece, cols), f32),
            ]
            for slots in (1, 1, members, members, members, members, 1, 1):
                sem_shapes.append(pltpu.SemaphoreType.DMA((slots,)))
    vmem = pl.BlockSpec(memory_space=pltpu.VMEM)
    return pl.pallas_call(
        functools.partial(sweep_kernel, plans, iters, chunks),
        out_shape=tuple(jax.ShapeDtypeStruct(shape, f32) for shape in shapes),
        in_specs=[vmem] * 7,
        out_specs=(vmem, vmem),
        scratch_shapes=scratch + sem_shapes,
        compiler_params=pltpu.CompilerParams(
            collective_id=0, has_side_effects=True, vmem_limit_bytes=60 * 1024 * 1024),
    )(kernel, charge_elec, charge_drop, elec_rhs, drop_rhs, elec_inv, drop_inv)


def on_device(elec_pos, drop_vert, drop_conn, elec_rhs, drop_rhs, elec_inv, drop_inv):
    drop_devices = lax.axis_size("drop")
    elec_devices = lax.axis_size("elec")
    rhs_count, elec_local = elec_rhs.shape
    drop_local = drop_rhs.shape[1]
    screen, soften, couple = constants(drop_local * drop_devices)
    half_block = drop_vert.shape[1]
    local_conn = drop_conn - lax.axis_index("drop") * half_block
    centres = centroids(drop_vert, local_conn)
    kernel = kernel_tile(elec_pos, centres, screen, soften, couple)

    charge_elec = block_solve(elec_inv, elec_rhs)
    charge_drop = block_solve(drop_inv, drop_rhs)
    plans = (("drop", drop_devices, drop_devices // 2), ("elec", elec_devices, 1))
    charge_elec, charge_drop = sweeps(
        kernel, charge_elec, charge_drop, elec_rhs, drop_rhs, elec_inv, drop_inv, plans, ITERS
    )
    return (charge_elec, charge_drop)


def solution(mesh):
    placed = (
        P(None, "elec"),
        P(None, "drop"),
        P(None, "drop"),
        P(None, "elec"),
        P(None, "drop"),
        P("elec", None, None),
        P("drop", None, None),
    )
    return jax.shard_map(
        on_device,
        mesh=mesh,
        in_specs=placed,
        out_specs=(P(None, "elec"), P(None, "drop")),
        check_vma=False,
    )
```

```python
import functools
import math

import jax
import jax.numpy as jnp
from jax import lax
from jax.experimental import pallas as pl
from jax.experimental.pallas import tpu as pltpu
from jax.sharding import PartitionSpec as P

ITERS = 2


HIGH = lax.Precision.HIGHEST
FAST = lax.Precision.HIGH
MESH = pl.DeviceIdType.MESH


def constants(total_drop):
    screen = 1.0
    soften = 0.001
    couple = 1.0 / (3.0 * math.sqrt(total_drop))
    return (screen, soften, couple)


def centroids(drop_vert, conn):
    vertices = lax.broadcasted_iota(jnp.int32, (drop_vert.shape[1], conn.shape[1]), 0)
    counts = sum((conn[k][None, :] == vertices).astype(jnp.float32) for k in range(3))
    counts = counts.astype(jnp.bfloat16)
    parts = []
    rest = drop_vert
    for _ in range(3):
        part = lax.reduce_precision(rest, exponent_bits=8, mantissa_bits=7)
        parts.append(part.astype(jnp.bfloat16))
        rest = rest - part
    stacked = jnp.concatenate(parts, axis=0)
    summed = jnp.dot(stacked, counts, preferred_element_type=jnp.float32)
    coords = drop_vert.shape[0]
    return (summed[:coords] + summed[coords:2 * coords] + summed[2 * coords:]) / 3.0


def kernel_tile(position, centres, screen, soften, couple):
    delta_x = position[0][:, None] - centres[0][None, :]
    delta_y = position[1][:, None] - centres[1][None, :]
    delta_z = position[2][:, None] - centres[2][None, :]
    distance = jnp.sqrt(delta_x * delta_x + delta_y * delta_y + delta_z * delta_z + soften)
    return couple * jnp.exp(-screen * distance) / distance


def block_solve(inverse, values):
    rhs_rows, columns = values.shape
    block_count, block_size, _ = inverse.shape
    shaped = values.reshape(rhs_rows, block_count, block_size)
    solved = jnp.einsum("bjk,rbk->rbj", inverse, shaped, precision=HIGH)
    return solved.reshape(rhs_rows, columns)


def axis_info(axis, size, stride):
    me = lax.axis_index(axis)
    bit = lax.rem(me // stride, 2)
    partner = me + stride - 2 * stride * bit
    group = lax.rem(me, stride) + (me // (2 * stride)) * stride
    members = size // 2

    def member(offset):
        g = lax.rem(group + offset, members)
        return lax.rem(g, stride) + (g // stride) * 2 * stride + bit * stride

    return (axis, bit, partner, group, members, member)


def send(src, dst, send_sem, recv_sem, axis, peer):
    copy = pltpu.make_async_remote_copy(
        src_ref=src, dst_ref=dst, send_sem=send_sem, recv_sem=recv_sem,
        device_id={axis: peer}, device_id_type=MESH,
    )
    copy.start()
    return copy


def wait_all(copies):
    for copy in copies:
        copy.wait()


def rows(index, piece):
    return pl.ds(pl.multiple_of(index * piece, piece), piece)


def exchange(info, source, rhs, inv, out, bufs, sems, first, width):
    axis, bit, partner, group, members, member = info
    half = source.shape[0] // 2
    piece = half // members
    mine = pl.multiple_of(bit * half, half)
    other = pl.multiple_of((1 - bit) * half, half)
    cols = pl.ds(first, width)
    buf_a, buf_b, buf_c, buf_d, half_s, piece_t = bufs

    pending = [send(source.at[pl.ds(other, half), cols], buf_a, sems[0].at[0], sems[1].at[0], axis, partner)]
    yield
    wait_all(pending)
    half_s[...] = source[pl.ds(mine, half), cols] + buf_a[...]
    pending = [
        send(half_s.at[rows(lax.rem(group + step, members), piece)], buf_b.at[step],
             sems[2].at[step], sems[3].at[step], axis, member(step))
        for step in range(1, members)
    ]
    yield
    wait_all(pending)
    acc = half_s[rows(group, piece), :]
    for step in range(1, members):
        acc = acc + buf_b[step]
    values = rhs[pl.ds(mine + group * piece, piece), cols] - acc
    size = inv.shape[1]
    for block in range(width // size):
        local = slice(block * size, (block + 1) * size)
        piece_t[:, local] = lax.dot_general(
            values[:, local], inv[first // size + block], (((1,), (1,)), ((), ())),
            precision=HIGH, preferred_element_type=jnp.float32,
        )
    out[pl.ds(mine + group * piece, piece), cols] = piece_t[...]
    pending = [
        send(piece_t, buf_c.at[step], sems[4].at[step], sems[5].at[step], axis, member(step))
        for step in range(1, members)
    ]
    yield
    wait_all(pending)
    for step in range(1, members):
        origin = lax.rem(group - step + members, members)
        half_s[rows(origin, piece), :] = buf_c[step]
    half_s[rows(group, piece), :] = piece_t[...]
    pending = [send(half_s, buf_d, sems[6].at[0], sems[7].at[0], axis, partner)]
    out[pl.ds(mine, half), cols] = half_s[...]
    yield
    wait_all(pending)
    out[pl.ds(other, half), cols] = buf_d[...]


def run_all(gens):
    live = list(gens)
    while live:
        still = []
        for gen in live:
            try:
                next(gen)
                still.append(gen)
            except StopIteration:
                pass
        live = still


def sweep_kernel(plans, iters, chunks, *refs):
    kernel, elec_rhs, drop_rhs, elec_inv, drop_inv = refs[:5]
    out_elec, out_drop = refs[5:7]
    part_elec, part_drop, mid_elec, mid_drop, charge_elec, charge_drop = refs[7:13]
    rest = refs[13:]
    count = len(plans)
    per = iters * count * chunks
    bufs = [rest[6 * g:6 * g + 6] for g in range(per)]
    sems = [rest[6 * per + 8 * g:6 * per + 8 * g + 8] for g in range(per)]
    info = [axis_info(*plan) for plan in plans]

    barrier = pltpu.get_barrier_semaphore()
    signals = 0
    for axis, bit, partner, group, members, member in info:
        pl.semaphore_signal(barrier, inc=1, device_id={axis: partner}, device_id_type=MESH)
        for step in range(1, members):
            pl.semaphore_signal(barrier, inc=1, device_id={axis: member(step)}, device_id_type=MESH)
        signals += members

    parts = (part_elec, part_drop)
    rhs = (elec_rhs, drop_rhs)
    inv = (elec_inv, drop_inv)

    def partial(a, ce, cd):
        if a == 0:
            part_elec[...] = lax.dot_general(
                cd[...], kernel[...], (((1,), (1,)), ((), ())), precision=HIGH,
                preferred_element_type=jnp.float32)
        else:
            part_drop[...] = jnp.dot(ce[...], kernel[...], precision=HIGH, preferred_element_type=jnp.float32)

    def gens(r, a, target):
        width = parts[a].shape[1] // chunks
        out = []
        for c in range(chunks):
            g = (r * count + a) * chunks + c
            out.append(exchange(info[a], parts[a], rhs[a], inv[a], target, bufs[g], sems[g], c * width, width))
        return out

    for values, inverse, charge in ((elec_rhs, elec_inv, charge_elec), (drop_rhs, drop_inv, charge_drop)):
        size = inverse.shape[1]
        for block in range(inverse.shape[0]):
            local = slice(block * size, (block + 1) * size)
            charge[:, local] = lax.dot_general(
                values[:, local], inverse[block], (((1,), (1,)), ((), ())),
                precision=HIGH, preferred_element_type=jnp.float32,
            )
    partial(0, charge_elec, charge_drop)
    partial(1, charge_elec, charge_drop)
    pl.semaphore_wait(barrier, signals)
    mids = (mid_elec, mid_drop)
    outs = (out_elec, out_drop)
    current = [gens(0, 0, mids[0] if iters > 1 else outs[0]), gens(0, 1, mids[1] if iters > 1 else outs[1])]
    for r in range(1, iters):
        target = outs if r == iters - 1 else mids
        for _ in range(4):
            for gen in current[0] + current[1]:
                next(gen)
        run_all(current[0])
        partial(1, mids[0], mids[1])
        following = gens(r, 1, target[1])
        for gen in following:
            next(gen)
        run_all(current[1])
        partial(0, mids[0], mids[1])
        current = [gens(r, 0, target[0]), following]
    run_all(current[0] + current[1])


def sweeps(kernel, elec_rhs, drop_rhs, elec_inv, drop_inv, plans, iters, chunks=2):
    f32 = jnp.float32
    shapes = (elec_rhs.shape, drop_rhs.shape)
    scratch = [pltpu.VMEM(shape, f32) for shape in shapes] * 3
    sem_shapes = []
    for shape, (axis, size, stride) in [item for _ in range(iters) for item in zip(shapes, plans) for _c in range(chunks)]:
            members = size // 2
            half = shape[0] // 2
            piece = half // members
            cols = shape[1] // chunks
            scratch += [
                pltpu.VMEM((half, cols), f32),
                pltpu.VMEM((members, piece, cols), f32),
                pltpu.VMEM((members, piece, cols), f32),
                pltpu.VMEM((half, cols), f32),
                pltpu.VMEM((half, cols), f32),
                pltpu.VMEM((piece, cols), f32),
            ]
            for slots in (1, 1, members, members, members, members, 1, 1):
                sem_shapes.append(pltpu.SemaphoreType.DMA((slots,)))
    vmem = pl.BlockSpec(memory_space=pltpu.VMEM)
    return pl.pallas_call(
        functools.partial(sweep_kernel, plans, iters, chunks),
        out_shape=tuple(jax.ShapeDtypeStruct(shape, f32) for shape in shapes),
        in_specs=[vmem] * 5,
        out_specs=(vmem, vmem),
        scratch_shapes=scratch + sem_shapes,
        compiler_params=pltpu.CompilerParams(
            collective_id=0, has_side_effects=True, vmem_limit_bytes=60 * 1024 * 1024),
    )(kernel, elec_rhs, drop_rhs, elec_inv, drop_inv)


def on_device(elec_pos, drop_vert, drop_conn, elec_rhs, drop_rhs, elec_inv, drop_inv):
    drop_devices = lax.axis_size("drop")
    elec_devices = lax.axis_size("elec")
    rhs_count, elec_local = elec_rhs.shape
    drop_local = drop_rhs.shape[1]
    screen, soften, couple = constants(drop_local * drop_devices)
    half_block = drop_vert.shape[1]
    local_conn = drop_conn - lax.axis_index("drop") * half_block
    centres = centroids(drop_vert, local_conn)
    kernel = kernel_tile(elec_pos, centres, screen, soften, couple)

    plans = (("drop", drop_devices, drop_devices // 2), ("elec", elec_devices, 1))
    charge_elec, charge_drop = sweeps(kernel, elec_rhs, drop_rhs, elec_inv, drop_inv, plans, ITERS)
    return (charge_elec, charge_drop)


def solution(mesh):
    placed = (
        P(None, "elec"),
        P(None, "drop"),
        P(None, "drop"),
        P(None, "elec"),
        P(None, "drop"),
        P("elec", None, None),
        P("drop", None, None),
    )
    return jax.shard_map(
        on_device,
        mesh=mesh,
        in_specs=placed,
        out_specs=(P(None, "elec"), P(None, "drop")),
        check_vma=False,
    )
```

```python
import functools
import math

import jax
import jax.numpy as jnp
from jax import lax
from jax.experimental import pallas as pl
from jax.experimental.pallas import tpu as pltpu
from jax.sharding import PartitionSpec as P

ITERS = 2


HIGH = lax.Precision.HIGHEST
FAST = lax.Precision.HIGH
MESH = pl.DeviceIdType.MESH


def constants(total_drop):
    screen = 1.0
    soften = 0.001
    couple = 1.0 / (3.0 * math.sqrt(total_drop))
    return (screen, soften, couple)


def centroids(drop_vert, conn):
    vertices = lax.broadcasted_iota(jnp.int32, (drop_vert.shape[1], conn.shape[1]), 0)
    counts = sum((conn[k][None, :] == vertices).astype(jnp.float32) for k in range(3))
    counts = counts.astype(jnp.bfloat16)
    parts = []
    rest = drop_vert
    for _ in range(3):
        part = lax.reduce_precision(rest, exponent_bits=8, mantissa_bits=7)
        parts.append(part.astype(jnp.bfloat16))
        rest = rest - part
    stacked = jnp.concatenate(parts, axis=0)
    summed = jnp.dot(stacked, counts, preferred_element_type=jnp.float32)
    coords = drop_vert.shape[0]
    return (summed[:coords] + summed[coords:2 * coords] + summed[2 * coords:]) / 3.0


def kernel_tile(position, centres, screen, soften, couple):
    delta_x = position[0][:, None] - centres[0][None, :]
    delta_y = position[1][:, None] - centres[1][None, :]
    delta_z = position[2][:, None] - centres[2][None, :]
    distance = jnp.sqrt(delta_x * delta_x + delta_y * delta_y + delta_z * delta_z + soften)
    return couple * jnp.exp(-screen * distance) / distance


def block_solve(inverse, values):
    rhs_rows, columns = values.shape
    block_count, block_size, _ = inverse.shape
    shaped = values.reshape(rhs_rows, block_count, block_size)
    solved = jnp.einsum("bjk,rbk->rbj", inverse, shaped, precision=HIGH)
    return solved.reshape(rhs_rows, columns)


def axis_info(axis, size, stride):
    me = lax.axis_index(axis)
    bit = lax.rem(me // stride, 2)
    partner = me + stride - 2 * stride * bit
    group = lax.rem(me, stride) + (me // (2 * stride)) * stride
    members = size // 2

    def member(offset):
        g = lax.rem(group + offset, members)
        return lax.rem(g, stride) + (g // stride) * 2 * stride + bit * stride

    return (axis, bit, partner, group, members, member)


def send(src, dst, send_sem, recv_sem, axis, peer):
    copy = pltpu.make_async_remote_copy(
        src_ref=src, dst_ref=dst, send_sem=send_sem, recv_sem=recv_sem,
        device_id={axis: peer}, device_id_type=MESH,
    )
    copy.start()
    return copy


def wait_all(copies):
    for copy in copies:
        copy.wait()


def rows(index, piece):
    return pl.ds(pl.multiple_of(index * piece, piece), piece)


def exchange(info, source, rhs, inv, out, bufs, sems, first, width):
    axis, bit, partner, group, members, member = info
    half = source.shape[0] // 2
    piece = half // members
    mine = pl.multiple_of(bit * half, half)
    other = pl.multiple_of((1 - bit) * half, half)
    cols = pl.ds(first, width)
    buf_a, buf_b, buf_c, buf_d, half_s, piece_t = bufs

    pending = [send(source.at[pl.ds(other, half), cols], buf_a, sems[0].at[0], sems[1].at[0], axis, partner)]
    yield
    wait_all(pending)
    half_s[...] = source[pl.ds(mine, half), cols] + buf_a[...]
    pending = [
        send(half_s.at[rows(lax.rem(group + step, members), piece)], buf_b.at[step],
             sems[2].at[step], sems[3].at[step], axis, member(step))
        for step in range(1, members)
    ]
    yield
    wait_all(pending)
    acc = half_s[rows(group, piece), :]
    for step in range(1, members):
        acc = acc + buf_b[step]
    values = rhs[pl.ds(mine + group * piece, piece), cols] - acc
    size = inv.shape[1]
    for block in range(width // size):
        local = slice(block * size, (block + 1) * size)
        piece_t[:, local] = lax.dot_general(
            values[:, local], inv[first // size + block], (((1,), (1,)), ((), ())),
            precision=HIGH, preferred_element_type=jnp.float32,
        )
    out[pl.ds(mine + group * piece, piece), cols] = piece_t[...]
    pending = [
        send(piece_t, buf_c.at[step], sems[4].at[step], sems[5].at[step], axis, member(step))
        for step in range(1, members)
    ]
    yield
    wait_all(pending)
    for step in range(1, members):
        origin = lax.rem(group - step + members, members)
        half_s[rows(origin, piece), :] = buf_c[step]
    half_s[rows(group, piece), :] = piece_t[...]
    pending = [send(half_s, buf_d, sems[6].at[0], sems[7].at[0], axis, partner)]
    out[pl.ds(mine, half), cols] = half_s[...]
    yield
    wait_all(pending)
    out[pl.ds(other, half), cols] = buf_d[...]


def run_all(gens):
    live = list(gens)
    while live:
        still = []
        for gen in live:
            try:
                next(gen)
                still.append(gen)
            except StopIteration:
                pass
        live = still


def sweep_kernel(plans, iters, chunks, *refs):
    kernel, elec_rhs, drop_rhs, elec_inv, drop_inv = refs[:5]
    result_elec, result_drop = refs[5:7]
    part_elec, part_drop, mid_elec, mid_drop, charge_elec, charge_drop, out_elec, out_drop = refs[7:15]
    store_sems = refs[15]
    rest = refs[16:]
    count = len(plans)
    per = iters * count * chunks
    bufs = [rest[6 * g:6 * g + 6] for g in range(per)]
    sems = [rest[6 * per + 8 * g:6 * per + 8 * g + 8] for g in range(per)]
    info = [axis_info(*plan) for plan in plans]

    barrier = pltpu.get_barrier_semaphore()
    signals = 0
    for axis, bit, partner, group, members, member in info:
        pl.semaphore_signal(barrier, inc=1, device_id={axis: partner}, device_id_type=MESH)
        for step in range(1, members):
            pl.semaphore_signal(barrier, inc=1, device_id={axis: member(step)}, device_id_type=MESH)
        signals += members

    parts = (part_elec, part_drop)
    rhs = (elec_rhs, drop_rhs)
    inv = (elec_inv, drop_inv)

    def partial(a, ce, cd):
        if a == 0:
            part_elec[...] = lax.dot_general(
                cd[...], kernel[...], (((1,), (1,)), ((), ())), precision=HIGH,
                preferred_element_type=jnp.float32)
        else:
            part_drop[...] = jnp.dot(ce[...], kernel[...], precision=HIGH, preferred_element_type=jnp.float32)

    def gens(r, a, target):
        width = parts[a].shape[1] // chunks
        out = []
        for c in range(chunks):
            g = (r * count + a) * chunks + c
            out.append(exchange(info[a], parts[a], rhs[a], inv[a], target, bufs[g], sems[g], c * width, width))
        return out

    for values, inverse, charge in ((elec_rhs, elec_inv, charge_elec), (drop_rhs, drop_inv, charge_drop)):
        size = inverse.shape[1]
        for block in range(inverse.shape[0]):
            local = slice(block * size, (block + 1) * size)
            charge[:, local] = lax.dot_general(
                values[:, local], inverse[block], (((1,), (1,)), ((), ())),
                precision=HIGH, preferred_element_type=jnp.float32,
            )
    partial(0, charge_elec, charge_drop)
    partial(1, charge_elec, charge_drop)
    pl.semaphore_wait(barrier, signals)
    mids = (mid_elec, mid_drop)
    outs = (out_elec, out_drop)
    current = [gens(0, 0, mids[0] if iters > 1 else outs[0]), gens(0, 1, mids[1] if iters > 1 else outs[1])]
    for r in range(1, iters):
        target = outs if r == iters - 1 else mids
        for _ in range(4):
            for gen in current[0] + current[1]:
                next(gen)
        run_all(current[0])
        partial(1, mids[0], mids[1])
        following = gens(r, 1, target[1])
        for gen in following:
            next(gen)
        run_all(current[1])
        partial(0, mids[0], mids[1])
        current = [gens(r, 0, target[0]), following]
    run_all(current[0] + current[1])
    stores = [pltpu.make_async_copy(src, dst, store_sems.at[k])
              for k, (src, dst) in enumerate(((out_elec, result_elec), (out_drop, result_drop)))]
    for store in stores:
        store.start()
    for store in stores:
        store.wait()


def sweeps(kernel, elec_rhs, drop_rhs, elec_inv, drop_inv, plans, iters, chunks=2):
    f32 = jnp.float32
    shapes = (elec_rhs.shape, drop_rhs.shape)
    scratch = [pltpu.VMEM(shape, f32) for shape in shapes] * 4 + [pltpu.SemaphoreType.DMA((2,))]
    sem_shapes = []
    for shape, (axis, size, stride) in [item for _ in range(iters) for item in zip(shapes, plans) for _c in range(chunks)]:
            members = size // 2
            half = shape[0] // 2
            piece = half // members
            cols = shape[1] // chunks
            scratch += [
                pltpu.VMEM((half, cols), f32),
                pltpu.VMEM((members, piece, cols), f32),
                pltpu.VMEM((members, piece, cols), f32),
                pltpu.VMEM((half, cols), f32),
                pltpu.VMEM((half, cols), f32),
                pltpu.VMEM((piece, cols), f32),
            ]
            for slots in (1, 1, members, members, members, members, 1, 1):
                sem_shapes.append(pltpu.SemaphoreType.DMA((slots,)))
    vmem = pl.BlockSpec(memory_space=pltpu.VMEM)
    return pl.pallas_call(
        functools.partial(sweep_kernel, plans, iters, chunks),
        out_shape=tuple(jax.ShapeDtypeStruct(shape, f32) for shape in shapes),
        in_specs=[vmem] * 5,
        out_specs=(pl.BlockSpec(memory_space=pl.ANY), pl.BlockSpec(memory_space=pl.ANY)),
        scratch_shapes=scratch + sem_shapes,
        compiler_params=pltpu.CompilerParams(
            collective_id=0, has_side_effects=True, vmem_limit_bytes=60 * 1024 * 1024),
    )(kernel, elec_rhs, drop_rhs, elec_inv, drop_inv)


def on_device(elec_pos, drop_vert, drop_conn, elec_rhs, drop_rhs, elec_inv, drop_inv):
    drop_devices = lax.axis_size("drop")
    elec_devices = lax.axis_size("elec")
    rhs_count, elec_local = elec_rhs.shape
    drop_local = drop_rhs.shape[1]
    screen, soften, couple = constants(drop_local * drop_devices)
    half_block = drop_vert.shape[1]
    local_conn = drop_conn - lax.axis_index("drop") * half_block
    centres = centroids(drop_vert, local_conn)
    kernel = kernel_tile(elec_pos, centres, screen, soften, couple)

    plans = (("drop", drop_devices, drop_devices // 2), ("elec", elec_devices, 1))
    charge_elec, charge_drop = sweeps(kernel, elec_rhs, drop_rhs, elec_inv, drop_inv, plans, ITERS)
    return (charge_elec, charge_drop)


def solution(mesh):
    placed = (
        P(None, "elec"),
        P(None, "drop"),
        P(None, "drop"),
        P(None, "elec"),
        P(None, "drop"),
        P("elec", None, None),
        P("drop", None, None),
    )
    return jax.shard_map(
        on_device,
        mesh=mesh,
        in_specs=placed,
        out_specs=(P(None, "elec"), P(None, "drop")),
        check_vma=False,
    )
```

```python
import functools
import math

import jax
import jax.numpy as jnp
from jax import lax
from jax.experimental import pallas as pl
from jax.experimental.pallas import tpu as pltpu
from jax.sharding import PartitionSpec as P

ITERS = 2


HIGH = lax.Precision.HIGHEST
FAST = lax.Precision.HIGH
MESH = pl.DeviceIdType.MESH


def constants(total_drop):
    screen = 1.0
    soften = 0.001
    couple = 1.0 / (3.0 * math.sqrt(total_drop))
    return (screen, soften, couple)


def centroids(drop_vert, conn):
    vertices = lax.broadcasted_iota(jnp.int32, (drop_vert.shape[1], conn.shape[1]), 0)
    counts = sum((conn[k][None, :] == vertices).astype(jnp.float32) for k in range(3))
    counts = counts.astype(jnp.bfloat16)
    parts = []
    rest = drop_vert
    for _ in range(3):
        part = lax.reduce_precision(rest, exponent_bits=8, mantissa_bits=7)
        parts.append(part.astype(jnp.bfloat16))
        rest = rest - part
    stacked = jnp.concatenate(parts, axis=0)
    summed = jnp.dot(stacked, counts, preferred_element_type=jnp.float32)
    coords = drop_vert.shape[0]
    return (summed[:coords] + summed[coords:2 * coords] + summed[2 * coords:]) / 3.0


def kernel_tile(position, centres, screen, soften, couple):
    delta_x = position[0][:, None] - centres[0][None, :]
    delta_y = position[1][:, None] - centres[1][None, :]
    delta_z = position[2][:, None] - centres[2][None, :]
    distance = jnp.sqrt(delta_x * delta_x + delta_y * delta_y + delta_z * delta_z + soften)
    return couple * jnp.exp(-screen * distance) / distance


def block_solve(inverse, values):
    rhs_rows, columns = values.shape
    block_count, block_size, _ = inverse.shape
    shaped = values.reshape(rhs_rows, block_count, block_size)
    solved = jnp.einsum("bjk,rbk->rbj", inverse, shaped, precision=HIGH)
    return solved.reshape(rhs_rows, columns)


def axis_info(axis, size, stride):
    me = lax.axis_index(axis)
    bit = lax.rem(me // stride, 2)
    partner = me + stride - 2 * stride * bit
    group = lax.rem(me, stride) + (me // (2 * stride)) * stride
    members = size // 2

    def member(offset):
        g = lax.rem(group + offset, members)
        return lax.rem(g, stride) + (g // stride) * 2 * stride + bit * stride

    return (axis, bit, partner, group, members, member)


def send(src, dst, send_sem, recv_sem, axis, peer):
    copy = pltpu.make_async_remote_copy(
        src_ref=src, dst_ref=dst, send_sem=send_sem, recv_sem=recv_sem,
        device_id={axis: peer}, device_id_type=MESH,
    )
    copy.start()
    return copy


def wait_all(copies):
    for copy in copies:
        copy.wait()


def rows(index, piece):
    return pl.ds(pl.multiple_of(index * piece, piece), piece)


def exchange(info, source, rhs, inv, out, bufs, sems, first, width):
    axis, bit, partner, group, members, member = info
    half = source.shape[0] // 2
    piece = half // members
    mine = pl.multiple_of(bit * half, half)
    other = pl.multiple_of((1 - bit) * half, half)
    cols = pl.ds(first, width)
    buf_a, buf_b, buf_c, buf_d, half_s, piece_t = bufs

    pending = [send(source.at[pl.ds(other, half), cols], buf_a, sems[0].at[0], sems[1].at[0], axis, partner)]
    yield
    wait_all(pending)
    half_s[...] = source[pl.ds(mine, half), cols] + buf_a[...]
    pending = [
        send(half_s.at[rows(lax.rem(group + step, members), piece)], buf_b.at[step],
             sems[2].at[step], sems[3].at[step], axis, member(step))
        for step in range(1, members)
    ]
    yield
    wait_all(pending)
    acc = half_s[rows(group, piece), :]
    for step in range(1, members):
        acc = acc + buf_b[step]
    values = rhs[pl.ds(mine + group * piece, piece), cols] - acc
    size = inv.shape[1]
    for block in range(width // size):
        local = slice(block * size, (block + 1) * size)
        piece_t[:, local] = lax.dot_general(
            values[:, local], inv[first // size + block], (((1,), (1,)), ((), ())),
            precision=HIGH, preferred_element_type=jnp.float32,
        )
    out[pl.ds(mine + group * piece, piece), cols] = piece_t[...]
    pending = [
        send(piece_t, buf_c.at[step], sems[4].at[step], sems[5].at[step], axis, member(step))
        for step in range(1, members)
    ]
    yield
    wait_all(pending)
    for step in range(1, members):
        origin = lax.rem(group - step + members, members)
        half_s[rows(origin, piece), :] = buf_c[step]
    half_s[rows(group, piece), :] = piece_t[...]
    pending = [send(half_s, buf_d, sems[6].at[0], sems[7].at[0], axis, partner)]
    out[pl.ds(mine, half), cols] = half_s[...]
    yield
    wait_all(pending)
    out[pl.ds(other, half), cols] = buf_d[...]


def run_all(gens):
    live = list(gens)
    while live:
        still = []
        for gen in live:
            try:
                next(gen)
                still.append(gen)
            except StopIteration:
                pass
        live = still


def sweep_kernel(plans, iters, chunks, *refs):
    kernel, elec_rhs, drop_rhs, elec_inv, drop_inv = refs[:5]
    out_elec, out_drop = refs[5:7]
    part_elec, part_drop, mid_elec, mid_drop, charge_elec, charge_drop = refs[7:13]
    rest = refs[13:]
    count = len(plans)
    per = iters * count * chunks
    bufs = [rest[6 * g:6 * g + 6] for g in range(per)]
    sems = [rest[6 * per + 8 * g:6 * per + 8 * g + 8] for g in range(per)]
    info = [axis_info(*plan) for plan in plans]

    barrier = pltpu.get_barrier_semaphore()
    signals = 0
    for axis, bit, partner, group, members, member in info:
        pl.semaphore_signal(barrier, inc=1, device_id={axis: partner}, device_id_type=MESH)
        for step in range(1, members):
            pl.semaphore_signal(barrier, inc=1, device_id={axis: member(step)}, device_id_type=MESH)
        signals += members

    parts = (part_elec, part_drop)
    rhs = (elec_rhs, drop_rhs)
    inv = (elec_inv, drop_inv)

    def partial(a, ce, cd):
        if a == 0:
            part_elec[...] = lax.dot_general(
                cd[...], kernel[...], (((1,), (1,)), ((), ())), precision=HIGH,
                preferred_element_type=jnp.float32)
        else:
            part_drop[...] = jnp.dot(ce[...], kernel[...], precision=HIGH, preferred_element_type=jnp.float32)

    def gens(r, a, target):
        width = parts[a].shape[1] // chunks
        out = []
        for c in range(chunks):
            g = (r * count + a) * chunks + c
            out.append(exchange(info[a], parts[a], rhs[a], inv[a], target, bufs[g], sems[g], c * width, width))
        return out

    for values, inverse, charge in ((elec_rhs, elec_inv, charge_elec), (drop_rhs, drop_inv, charge_drop)):
        size = inverse.shape[1]
        for block in range(inverse.shape[0]):
            local = slice(block * size, (block + 1) * size)
            charge[:, local] = lax.dot_general(
                values[:, local], inverse[block], (((1,), (1,)), ((), ())),
                precision=HIGH, preferred_element_type=jnp.float32,
            )
    partial(0, charge_elec, charge_drop)
    partial(1, charge_elec, charge_drop)
    pl.semaphore_wait(barrier, signals)
    mids = (mid_elec, mid_drop)
    outs = (out_elec, out_drop)
    current = [gens(0, 0, mids[0] if iters > 1 else outs[0]), gens(0, 1, mids[1] if iters > 1 else outs[1])]
    for r in range(1, iters):
        target = outs if r == iters - 1 else mids
        for _ in range(4):
            for gen in current[0] + current[1]:
                next(gen)
        run_all(current[1])
        partial(0, mids[0], mids[1])
        following = gens(r, 0, target[0])
        for gen in following:
            next(gen)
        run_all(current[0])
        partial(1, mids[0], mids[1])
        current = [following, gens(r, 1, target[1])]
    run_all(current[0] + current[1])


def sweeps(kernel, elec_rhs, drop_rhs, elec_inv, drop_inv, plans, iters, chunks=2):
    f32 = jnp.float32
    shapes = (elec_rhs.shape, drop_rhs.shape)
    scratch = [pltpu.VMEM(shape, f32) for shape in shapes] * 3
    sem_shapes = []
    for shape, (axis, size, stride) in [item for _ in range(iters) for item in zip(shapes, plans) for _c in range(chunks)]:
            members = size // 2
            half = shape[0] // 2
            piece = half // members
            cols = shape[1] // chunks
            scratch += [
                pltpu.VMEM((half, cols), f32),
                pltpu.VMEM((members, piece, cols), f32),
                pltpu.VMEM((members, piece, cols), f32),
                pltpu.VMEM((half, cols), f32),
                pltpu.VMEM((half, cols), f32),
                pltpu.VMEM((piece, cols), f32),
            ]
            for slots in (1, 1, members, members, members, members, 1, 1):
                sem_shapes.append(pltpu.SemaphoreType.DMA((slots,)))
    vmem = pl.BlockSpec(memory_space=pltpu.VMEM)
    return pl.pallas_call(
        functools.partial(sweep_kernel, plans, iters, chunks),
        out_shape=tuple(jax.ShapeDtypeStruct(shape, f32) for shape in shapes),
        in_specs=[vmem] * 5,
        out_specs=(vmem, vmem),
        scratch_shapes=scratch + sem_shapes,
        compiler_params=pltpu.CompilerParams(
            collective_id=0, has_side_effects=True, vmem_limit_bytes=60 * 1024 * 1024),
    )(kernel, elec_rhs, drop_rhs, elec_inv, drop_inv)


def on_device(elec_pos, drop_vert, drop_conn, elec_rhs, drop_rhs, elec_inv, drop_inv):
    drop_devices = lax.axis_size("drop")
    elec_devices = lax.axis_size("elec")
    rhs_count, elec_local = elec_rhs.shape
    drop_local = drop_rhs.shape[1]
    screen, soften, couple = constants(drop_local * drop_devices)
    half_block = drop_vert.shape[1]
    local_conn = drop_conn - lax.axis_index("drop") * half_block
    centres = centroids(drop_vert, local_conn)
    kernel = kernel_tile(elec_pos, centres, screen, soften, couple)

    plans = (("drop", drop_devices, drop_devices // 2), ("elec", elec_devices, 1))
    charge_elec, charge_drop = sweeps(kernel, elec_rhs, drop_rhs, elec_inv, drop_inv, plans, ITERS)
    return (charge_elec, charge_drop)


def solution(mesh):
    placed = (
        P(None, "elec"),
        P(None, "drop"),
        P(None, "drop"),
        P(None, "elec"),
        P(None, "drop"),
        P("elec", None, None),
        P("drop", None, None),
    )
    return jax.shard_map(
        on_device,
        mesh=mesh,
        in_specs=placed,
        out_specs=(P(None, "elec"), P(None, "drop")),
        check_vma=False,
    )
```

```python
import functools
import math

import jax
import jax.numpy as jnp
from jax import lax
from jax.experimental import pallas as pl
from jax.experimental.pallas import tpu as pltpu
from jax.sharding import PartitionSpec as P

ITERS = 2


HIGH = lax.Precision.HIGHEST
FAST = lax.Precision.HIGH
MESH = pl.DeviceIdType.MESH


def constants(total_drop):
    screen = 1.0
    soften = 0.001
    couple = 1.0 / (3.0 * math.sqrt(total_drop))
    return (screen, soften, couple)


def centroids(drop_vert, conn):
    vertices = lax.broadcasted_iota(jnp.int32, (drop_vert.shape[1], conn.shape[1]), 0)
    counts = sum((conn[k][None, :] == vertices).astype(jnp.float32) for k in range(3))
    counts = counts.astype(jnp.bfloat16)
    parts = []
    rest = drop_vert
    for _ in range(3):
        part = lax.reduce_precision(rest, exponent_bits=8, mantissa_bits=7)
        parts.append(part.astype(jnp.bfloat16))
        rest = rest - part
    stacked = jnp.concatenate(parts, axis=0)
    summed = jnp.dot(stacked, counts, preferred_element_type=jnp.float32)
    coords = drop_vert.shape[0]
    return (summed[:coords] + summed[coords:2 * coords] + summed[2 * coords:]) / 3.0


def kernel_tile(position, centres, screen, soften, couple):
    delta_x = position[0][:, None] - centres[0][None, :]
    delta_y = position[1][:, None] - centres[1][None, :]
    delta_z = position[2][:, None] - centres[2][None, :]
    distance = jnp.sqrt(delta_x * delta_x + delta_y * delta_y + delta_z * delta_z + soften)
    return couple * jnp.exp(-screen * distance) / distance


def block_solve(inverse, values):
    rhs_rows, columns = values.shape
    block_count, block_size, _ = inverse.shape
    shaped = values.reshape(rhs_rows, block_count, block_size)
    solved = jnp.einsum("bjk,rbk->rbj", inverse, shaped, precision=HIGH)
    return solved.reshape(rhs_rows, columns)


def axis_info(axis, size, stride):
    me = lax.axis_index(axis)
    bit = lax.rem(me // stride, 2)
    partner = me + stride - 2 * stride * bit
    group = lax.rem(me, stride) + (me // (2 * stride)) * stride
    members = size // 2

    def member(offset):
        g = lax.rem(group + offset, members)
        return lax.rem(g, stride) + (g // stride) * 2 * stride + bit * stride

    return (axis, bit, partner, group, members, member)


def send(src, dst, send_sem, recv_sem, axis, peer):
    copy = pltpu.make_async_remote_copy(
        src_ref=src, dst_ref=dst, send_sem=send_sem, recv_sem=recv_sem,
        device_id={axis: peer}, device_id_type=MESH,
    )
    copy.start()
    return copy


def wait_all(copies):
    for copy in copies:
        copy.wait()


def rows(index, piece):
    return pl.ds(pl.multiple_of(index * piece, piece), piece)


def exchange(info, source, rhs, inv, out, bufs, sems, first, width):
    axis, bit, partner, group, members, member = info
    half = source.shape[0] // 2
    piece = half // members
    mine = pl.multiple_of(bit * half, half)
    other = pl.multiple_of((1 - bit) * half, half)
    cols = pl.ds(first, width)
    buf_a, buf_b, buf_c, buf_d, half_s, piece_t = bufs

    pending = [send(source.at[pl.ds(other, half), cols], buf_a, sems[0].at[0], sems[1].at[0], axis, partner)]
    yield
    wait_all(pending)
    half_s[...] = source[pl.ds(mine, half), cols] + buf_a[...]
    pending = [
        send(half_s.at[rows(lax.rem(group + step, members), piece)], buf_b.at[step],
             sems[2].at[step], sems[3].at[step], axis, member(step))
        for step in range(1, members)
    ]
    yield
    wait_all(pending)
    acc = half_s[rows(group, piece), :]
    for step in range(1, members):
        acc = acc + buf_b[step]
    values = rhs[pl.ds(mine + group * piece, piece), cols] - acc
    size = inv.shape[1]
    for block in range(width // size):
        local = slice(block * size, (block + 1) * size)
        piece_t[:, local] = lax.dot_general(
            values[:, local], inv[first // size + block], (((1,), (1,)), ((), ())),
            precision=HIGH, preferred_element_type=jnp.float32,
        )
    out[pl.ds(mine + group * piece, piece), cols] = piece_t[...]
    pending = [
        send(piece_t, buf_c.at[step], sems[4].at[step], sems[5].at[step], axis, member(step))
        for step in range(1, members)
    ]
    yield
    wait_all(pending)
    for step in range(1, members):
        origin = lax.rem(group - step + members, members)
        half_s[rows(origin, piece), :] = buf_c[step]
    half_s[rows(group, piece), :] = piece_t[...]
    pending = [send(half_s, buf_d, sems[6].at[0], sems[7].at[0], axis, partner)]
    out[pl.ds(mine, half), cols] = half_s[...]
    yield
    wait_all(pending)
    out[pl.ds(other, half), cols] = buf_d[...]


def run_all(gens):
    live = list(gens)
    while live:
        still = []
        for gen in live:
            try:
                next(gen)
                still.append(gen)
            except StopIteration:
                pass
        live = still


def sweep_kernel(plans, iters, chunks, *refs):
    kernel, elec_rhs, drop_rhs, elec_inv, drop_inv = refs[:5]
    out_elec, out_drop = refs[5:7]
    part_elec, part_drop, mid_elec, mid_drop, charge_elec, charge_drop = refs[7:13]
    rest = refs[13:]
    count = len(plans)
    per = iters * count * chunks
    bufs = [rest[6 * g:6 * g + 6] for g in range(per)]
    sems = [rest[6 * per + 8 * g:6 * per + 8 * g + 8] for g in range(per)]
    info = [axis_info(*plan) for plan in plans]

    barrier = pltpu.get_barrier_semaphore()
    signals = 0
    for axis, bit, partner, group, members, member in info:
        pl.semaphore_signal(barrier, inc=1, device_id={axis: partner}, device_id_type=MESH)
        for step in range(1, members):
            pl.semaphore_signal(barrier, inc=1, device_id={axis: member(step)}, device_id_type=MESH)
        signals += members

    parts = (part_elec, part_drop)
    rhs = (elec_rhs, drop_rhs)
    inv = (elec_inv, drop_inv)

    def partial(a, ce, cd):
        if a == 0:
            part_elec[...] = lax.dot_general(
                cd[...], kernel[...], (((1,), (1,)), ((), ())), precision=HIGH,
                preferred_element_type=jnp.float32)
        else:
            part_drop[...] = jnp.dot(ce[...], kernel[...], precision=HIGH, preferred_element_type=jnp.float32)

    def gens(r, a, target):
        width = parts[a].shape[1] // chunks
        out = []
        for c in range(chunks):
            g = (r * count + a) * chunks + c
            out.append(exchange(info[a], parts[a], rhs[a], inv[a], target, bufs[g], sems[g], c * width, width))
        return out

    for values, inverse, charge in ((elec_rhs, elec_inv, charge_elec), (drop_rhs, drop_inv, charge_drop)):
        size = inverse.shape[1]
        for block in range(inverse.shape[0]):
            local = slice(block * size, (block + 1) * size)
            charge[:, local] = lax.dot_general(
                values[:, local], inverse[block], (((1,), (1,)), ((), ())),
                precision=HIGH, preferred_element_type=jnp.float32,
            )
    partial(0, charge_elec, charge_drop)
    partial(1, charge_elec, charge_drop)
    pl.semaphore_wait(barrier, signals)
    mids = (mid_elec, mid_drop)
    outs = (out_elec, out_drop)
    current = [gens(0, 0, mids[0] if iters > 1 else outs[0]), gens(0, 1, mids[1] if iters > 1 else outs[1])]
    for r in range(1, iters):
        target = outs if r == iters - 1 else mids
        for _ in range(4):
            for gen in current[1] + current[0]:
                next(gen)
        run_all(current[0])
        partial(1, mids[0], mids[1])
        following = gens(r, 1, target[1])
        for gen in following:
            next(gen)
        run_all(current[1])
        partial(0, mids[0], mids[1])
        current = [gens(r, 0, target[0]), following]
    run_all(current[1] + current[0])


def sweeps(kernel, elec_rhs, drop_rhs, elec_inv, drop_inv, plans, iters, chunks=2):
    f32 = jnp.float32
    shapes = (elec_rhs.shape, drop_rhs.shape)
    scratch = [pltpu.VMEM(shape, f32) for shape in shapes] * 3
    sem_shapes = []
    for shape, (axis, size, stride) in [item for _ in range(iters) for item in zip(shapes, plans) for _c in range(chunks)]:
            members = size // 2
            half = shape[0] // 2
            piece = half // members
            cols = shape[1] // chunks
            scratch += [
                pltpu.VMEM((half, cols), f32),
                pltpu.VMEM((members, piece, cols), f32),
                pltpu.VMEM((members, piece, cols), f32),
                pltpu.VMEM((half, cols), f32),
                pltpu.VMEM((half, cols), f32),
                pltpu.VMEM((piece, cols), f32),
            ]
            for slots in (1, 1, members, members, members, members, 1, 1):
                sem_shapes.append(pltpu.SemaphoreType.DMA((slots,)))
    vmem = pl.BlockSpec(memory_space=pltpu.VMEM)
    return pl.pallas_call(
        functools.partial(sweep_kernel, plans, iters, chunks),
        out_shape=tuple(jax.ShapeDtypeStruct(shape, f32) for shape in shapes),
        in_specs=[vmem] * 5,
        out_specs=(vmem, vmem),
        scratch_shapes=scratch + sem_shapes,
        compiler_params=pltpu.CompilerParams(
            collective_id=0, has_side_effects=True, vmem_limit_bytes=60 * 1024 * 1024),
    )(kernel, elec_rhs, drop_rhs, elec_inv, drop_inv)


def on_device(elec_pos, drop_vert, drop_conn, elec_rhs, drop_rhs, elec_inv, drop_inv):
    drop_devices = lax.axis_size("drop")
    elec_devices = lax.axis_size("elec")
    rhs_count, elec_local = elec_rhs.shape
    drop_local = drop_rhs.shape[1]
    screen, soften, couple = constants(drop_local * drop_devices)
    half_block = drop_vert.shape[1]
    local_conn = drop_conn - lax.axis_index("drop") * half_block
    centres = centroids(drop_vert, local_conn)
    kernel = kernel_tile(elec_pos, centres, screen, soften, couple)

    plans = (("drop", drop_devices, drop_devices // 2), ("elec", elec_devices, 1))
    charge_elec, charge_drop = sweeps(kernel, elec_rhs, drop_rhs, elec_inv, drop_inv, plans, ITERS)
    return (charge_elec, charge_drop)


def solution(mesh):
    placed = (
        P(None, "elec"),
        P(None, "drop"),
        P(None, "drop"),
        P(None, "elec"),
        P(None, "drop"),
        P("elec", None, None),
        P("drop", None, None),
    )
    return jax.shard_map(
        on_device,
        mesh=mesh,
        in_specs=placed,
        out_specs=(P(None, "elec"), P(None, "drop")),
        check_vma=False,
    )
```

```python
import functools
import math

import jax
import jax.numpy as jnp
from jax import lax
from jax.experimental import pallas as pl
from jax.experimental.pallas import tpu as pltpu
from jax.sharding import PartitionSpec as P

ITERS = 2


HIGH = lax.Precision.HIGHEST
FAST = lax.Precision.HIGH
MESH = pl.DeviceIdType.MESH


def constants(total_drop):
    screen = 1.0
    soften = 0.001
    couple = 1.0 / (3.0 * math.sqrt(total_drop))
    return (screen, soften, couple)


def centroids(drop_vert, conn):
    vertices = lax.broadcasted_iota(jnp.int32, (drop_vert.shape[1], conn.shape[1]), 0)
    counts = sum((conn[k][None, :] == vertices).astype(jnp.float32) for k in range(3))
    counts = counts.astype(jnp.bfloat16)
    parts = []
    rest = drop_vert
    for _ in range(3):
        part = lax.reduce_precision(rest, exponent_bits=8, mantissa_bits=7)
        parts.append(part.astype(jnp.bfloat16))
        rest = rest - part
    stacked = jnp.concatenate(parts, axis=0)
    summed = jnp.dot(stacked, counts, preferred_element_type=jnp.float32)
    coords = drop_vert.shape[0]
    return (summed[:coords] + summed[coords:2 * coords] + summed[2 * coords:]) / 3.0


def kernel_tile(position, centres, screen, soften, couple):
    delta_x = position[0][:, None] - centres[0][None, :]
    delta_y = position[1][:, None] - centres[1][None, :]
    delta_z = position[2][:, None] - centres[2][None, :]
    distance = jnp.sqrt(delta_x * delta_x + delta_y * delta_y + delta_z * delta_z + soften)
    return couple * jnp.exp(-screen * distance) / distance


def block_solve(inverse, values):
    rhs_rows, columns = values.shape
    block_count, block_size, _ = inverse.shape
    shaped = values.reshape(rhs_rows, block_count, block_size)
    solved = jnp.einsum("bjk,rbk->rbj", inverse, shaped, precision=HIGH)
    return solved.reshape(rhs_rows, columns)


def axis_info(axis, size, stride):
    me = lax.axis_index(axis)
    bit = lax.rem(me // stride, 2)
    partner = me + stride - 2 * stride * bit
    group = lax.rem(me, stride) + (me // (2 * stride)) * stride
    members = size // 2

    def member(offset):
        g = lax.rem(group + offset, members)
        return lax.rem(g, stride) + (g // stride) * 2 * stride + bit * stride

    return (axis, bit, partner, group, members, member)


def send(src, dst, send_sem, recv_sem, axis, peer):
    copy = pltpu.make_async_remote_copy(
        src_ref=src, dst_ref=dst, send_sem=send_sem, recv_sem=recv_sem,
        device_id={axis: peer}, device_id_type=MESH,
    )
    copy.start()
    return copy


def wait_all(copies):
    for copy in copies:
        copy.wait()


def rows(index, piece):
    return pl.ds(pl.multiple_of(index * piece, piece), piece)


def exchange(info, source, rhs, inv, out, bufs, sems, first, width):
    axis, bit, partner, group, members, member = info
    half = source.shape[0] // 2
    piece = half // members
    mine = pl.multiple_of(bit * half, half)
    other = pl.multiple_of((1 - bit) * half, half)
    cols = pl.ds(first, width)
    buf_a, buf_b, buf_c, buf_d, half_s, piece_t = bufs

    pending = [send(source.at[pl.ds(other, half), cols], buf_a, sems[0].at[0], sems[1].at[0], axis, partner)]
    yield
    wait_all(pending)
    half_s[...] = source[pl.ds(mine, half), cols] + buf_a[...]
    pending = [
        send(half_s.at[rows(lax.rem(group + step, members), piece)], buf_b.at[step],
             sems[2].at[step], sems[3].at[step], axis, member(step))
        for step in range(1, members)
    ]
    yield
    wait_all(pending)
    acc = half_s[rows(group, piece), :]
    for step in range(1, members):
        acc = acc + buf_b[step]
    values = rhs[pl.ds(mine + group * piece, piece), cols] - acc
    size = inv.shape[1]
    for block in range(width // size):
        local = slice(block * size, (block + 1) * size)
        piece_t[:, local] = lax.dot_general(
            values[:, local], inv[first // size + block], (((1,), (1,)), ((), ())),
            precision=HIGH, preferred_element_type=jnp.float32,
        )
    out[pl.ds(mine + group * piece, piece), cols] = piece_t[...]
    pending = [
        send(piece_t, buf_c.at[step], sems[4].at[step], sems[5].at[step], axis, member(step))
        for step in range(1, members)
    ]
    yield
    wait_all(pending)
    for step in range(1, members):
        origin = lax.rem(group - step + members, members)
        half_s[rows(origin, piece), :] = buf_c[step]
    half_s[rows(group, piece), :] = piece_t[...]
    pending = [send(half_s, buf_d, sems[6].at[0], sems[7].at[0], axis, partner)]
    out[pl.ds(mine, half), cols] = half_s[...]
    yield
    wait_all(pending)
    out[pl.ds(other, half), cols] = buf_d[...]


def run_all(gens):
    live = list(gens)
    while live:
        still = []
        for gen in live:
            try:
                next(gen)
                still.append(gen)
            except StopIteration:
                pass
        live = still


def sweep_kernel(plans, iters, chunks, *refs):
    kernel, elec_rhs, drop_rhs, elec_inv, drop_inv = refs[:5]
    out_elec, out_drop = refs[5:7]
    part_elec, part_drop, mid_elec, mid_drop, charge_elec, charge_drop = refs[7:13]
    rest = refs[13:]
    count = len(plans)
    per = iters * count * chunks
    bufs = [rest[6 * g:6 * g + 6] for g in range(per)]
    sems = [rest[6 * per + 8 * g:6 * per + 8 * g + 8] for g in range(per)]
    info = [axis_info(*plan) for plan in plans]

    barrier = pltpu.get_barrier_semaphore()
    signals = 0
    for axis, bit, partner, group, members, member in info:
        pl.semaphore_signal(barrier, inc=1, device_id={axis: partner}, device_id_type=MESH)
        for step in range(1, members):
            pl.semaphore_signal(barrier, inc=1, device_id={axis: member(step)}, device_id_type=MESH)
        signals += members

    parts = (part_elec, part_drop)
    rhs = (elec_rhs, drop_rhs)
    inv = (elec_inv, drop_inv)

    def partial(a, ce, cd):
        if a == 0:
            part_elec[...] = lax.dot_general(
                cd[...], kernel[...], (((1,), (1,)), ((), ())), precision=HIGH,
                preferred_element_type=jnp.float32)
        else:
            part_drop[...] = jnp.dot(ce[...], kernel[...], precision=HIGH, preferred_element_type=jnp.float32)

    def gens(r, a, target):
        width = parts[a].shape[1] // chunks
        out = []
        for c in range(chunks):
            g = (r * count + a) * chunks + c
            out.append(exchange(info[a], parts[a], rhs[a], inv[a], target, bufs[g], sems[g], c * width, width))
        return out

    for values, inverse, charge in ((elec_rhs, elec_inv, charge_elec), (drop_rhs, drop_inv, charge_drop)):
        size = inverse.shape[1]
        for block in range(inverse.shape[0]):
            local = slice(block * size, (block + 1) * size)
            charge[:, local] = lax.dot_general(
                values[:, local], inverse[block], (((1,), (1,)), ((), ())),
                precision=HIGH, preferred_element_type=jnp.float32,
            )
    partial(0, charge_elec, charge_drop)
    partial(1, charge_elec, charge_drop)
    pl.semaphore_wait(barrier, signals)
    mids = (mid_elec, mid_drop)
    outs = (out_elec, out_drop)
    current = [gens(0, 0, mids[0] if iters > 1 else outs[0]), gens(0, 1, mids[1] if iters > 1 else outs[1])]
    for r in range(1, iters):
        target = outs if r == iters - 1 else mids
        for _ in range(4):
            for gen in current[0] + current[1]:
                next(gen)
        run_all(current[0])
        partial(1, mids[0], mids[1])
        following = gens(r, 1, target[1])
        for gen in following:
            next(gen)
        run_all(current[1])
        partial(0, mids[0], mids[1])
        current = [gens(r, 0, target[0]), following]
    run_all(current[0] + current[1])


def sweeps(kernel, elec_rhs, drop_rhs, elec_inv, drop_inv, plans, iters, chunks=2):
    f32 = jnp.float32
    shapes = (elec_rhs.shape, drop_rhs.shape)
    scratch = [pltpu.VMEM(shape, f32) for shape in shapes] * 3
    sem_shapes = []
    for shape, (axis, size, stride) in [item for _ in range(iters) for item in zip(shapes, plans) for _c in range(chunks)]:
            members = size // 2
            half = shape[0] // 2
            piece = half // members
            cols = shape[1] // chunks
            scratch += [
                pltpu.VMEM((half, cols), f32),
                pltpu.VMEM((members, piece, cols), f32),
                pltpu.VMEM((members, piece, cols), f32),
                pltpu.VMEM((half, cols), f32),
                pltpu.VMEM((half, cols), f32),
                pltpu.VMEM((piece, cols), f32),
            ]
            for slots in (1, 1, members, members, members, members, 1, 1):
                sem_shapes.append(pltpu.SemaphoreType.DMA((slots,)))
    vmem = pl.BlockSpec(memory_space=pltpu.VMEM)
    return pl.pallas_call(
        functools.partial(sweep_kernel, plans, iters, chunks),
        out_shape=tuple(jax.ShapeDtypeStruct(shape, f32) for shape in shapes),
        in_specs=[vmem] * 5,
        out_specs=(vmem, vmem),
        scratch_shapes=scratch + sem_shapes,
        compiler_params=pltpu.CompilerParams(
            collective_id=0, has_side_effects=True, vmem_limit_bytes=60 * 1024 * 1024),
    )(kernel, elec_rhs, drop_rhs, elec_inv, drop_inv)


def on_device(elec_pos, drop_vert, drop_conn, elec_rhs, drop_rhs, elec_inv, drop_inv):
    drop_devices = lax.axis_size("drop")
    elec_devices = lax.axis_size("elec")
    rhs_count, elec_local = elec_rhs.shape
    drop_local = drop_rhs.shape[1]
    screen, soften, couple = constants(drop_local * drop_devices)
    half_block = drop_vert.shape[1]
    local_conn = drop_conn - lax.axis_index("drop") * half_block
    centres = centroids(drop_vert, local_conn)
    kernel = kernel_tile(elec_pos, centres, screen, soften, couple)

    plans = (("drop", drop_devices, 1), ("elec", elec_devices, 1))
    charge_elec, charge_drop = sweeps(kernel, elec_rhs, drop_rhs, elec_inv, drop_inv, plans, ITERS)
    return (charge_elec, charge_drop)


def solution(mesh):
    placed = (
        P(None, "elec"),
        P(None, "drop"),
        P(None, "drop"),
        P(None, "elec"),
        P(None, "drop"),
        P("elec", None, None),
        P("drop", None, None),
    )
    return jax.shard_map(
        on_device,
        mesh=mesh,
        in_specs=placed,
        out_specs=(P(None, "elec"), P(None, "drop")),
        check_vma=False,
    )
```

```python
import functools
import math

import jax
import jax.numpy as jnp
from jax import lax
from jax.experimental import pallas as pl
from jax.experimental.pallas import tpu as pltpu
from jax.sharding import PartitionSpec as P

ITERS = 2


HIGH = lax.Precision.HIGHEST
FAST = lax.Precision.HIGH
MESH = pl.DeviceIdType.MESH


def constants(total_drop):
    screen = 1.0
    soften = 0.001
    couple = 1.0 / (3.0 * math.sqrt(total_drop))
    return (screen, soften, couple)


def centroids(drop_vert, conn):
    vertices = lax.broadcasted_iota(jnp.int32, (drop_vert.shape[1], conn.shape[1]), 0)
    counts = sum((conn[k][None, :] == vertices).astype(jnp.float32) for k in range(3))
    counts = counts.astype(jnp.bfloat16)
    parts = []
    rest = drop_vert
    for _ in range(3):
        part = lax.reduce_precision(rest, exponent_bits=8, mantissa_bits=7)
        parts.append(part.astype(jnp.bfloat16))
        rest = rest - part
    stacked = jnp.concatenate(parts, axis=0)
    summed = jnp.dot(stacked, counts, preferred_element_type=jnp.float32)
    coords = drop_vert.shape[0]
    return (summed[:coords] + summed[coords:2 * coords] + summed[2 * coords:]) / 3.0


def kernel_tile(position, centres, screen, soften, couple):
    delta_x = position[0][:, None] - centres[0][None, :]
    delta_y = position[1][:, None] - centres[1][None, :]
    delta_z = position[2][:, None] - centres[2][None, :]
    distance = jnp.sqrt(delta_x * delta_x + delta_y * delta_y + delta_z * delta_z + soften)
    return couple * jnp.exp(-screen * distance) / distance


def block_solve(inverse, values):
    rhs_rows, columns = values.shape
    block_count, block_size, _ = inverse.shape
    shaped = values.reshape(rhs_rows, block_count, block_size)
    solved = jnp.einsum("bjk,rbk->rbj", inverse, shaped, precision=HIGH)
    return solved.reshape(rhs_rows, columns)


def axis_info(axis, size, stride):
    me = lax.axis_index(axis)
    bit = lax.rem(me // stride, 2)
    partner = me + stride - 2 * stride * bit
    group = lax.rem(me, stride) + (me // (2 * stride)) * stride
    members = size // 2

    def member(offset):
        g = lax.rem(group + offset, members)
        return lax.rem(g, stride) + (g // stride) * 2 * stride + bit * stride

    return (axis, bit, partner, group, members, member)


def send(src, dst, send_sem, recv_sem, axis, peer):
    copy = pltpu.make_async_remote_copy(
        src_ref=src, dst_ref=dst, send_sem=send_sem, recv_sem=recv_sem,
        device_id={axis: peer}, device_id_type=MESH,
    )
    copy.start()
    return copy


def wait_all(copies):
    for copy in copies:
        copy.wait()


def rows(index, piece):
    return pl.ds(pl.multiple_of(index * piece, piece), piece)


def exchange(info, source, rhs, inv, out, bufs, sems, first, width):
    axis, bit, partner, group, members, member = info
    half = source.shape[0] // 2
    piece = half // members
    mine = pl.multiple_of(bit * half, half)
    other = pl.multiple_of((1 - bit) * half, half)
    cols = pl.ds(first, width)
    buf_a, buf_b, buf_c, buf_d, half_s, piece_t = bufs

    pending = [send(source.at[pl.ds(other, half), cols], buf_a, sems[0].at[0], sems[1].at[0], axis, partner)]
    yield
    wait_all(pending)
    half_s[...] = source[pl.ds(mine, half), cols] + buf_a[...]
    pending = [
        send(half_s.at[rows(lax.rem(group + step, members), piece)], buf_b.at[step],
             sems[2].at[step], sems[3].at[step], axis, member(step))
        for step in range(1, members)
    ]
    yield
    wait_all(pending)
    acc = half_s[rows(group, piece), :]
    for step in range(1, members):
        acc = acc + buf_b[step]
    values = rhs[pl.ds(mine + group * piece, piece), cols] - acc
    size = inv.shape[1]
    for block in range(width // size):
        local = slice(block * size, (block + 1) * size)
        piece_t[:, local] = lax.dot_general(
            values[:, local], inv[first // size + block], (((1,), (1,)), ((), ())),
            precision=HIGH, preferred_element_type=jnp.float32,
        )
    out[pl.ds(mine + group * piece, piece), cols] = piece_t[...]
    pending = [
        send(piece_t, buf_c.at[step], sems[4].at[step], sems[5].at[step], axis, member(step))
        for step in range(1, members)
    ]
    yield
    wait_all(pending)
    for step in range(1, members):
        origin = lax.rem(group - step + members, members)
        half_s[rows(origin, piece), :] = buf_c[step]
    half_s[rows(group, piece), :] = piece_t[...]
    pending = [send(half_s, buf_d, sems[6].at[0], sems[7].at[0], axis, partner)]
    out[pl.ds(mine, half), cols] = half_s[...]
    yield
    wait_all(pending)
    out[pl.ds(other, half), cols] = buf_d[...]


def run_all(gens):
    live = list(gens)
    while live:
        still = []
        for gen in live:
            try:
                next(gen)
                still.append(gen)
            except StopIteration:
                pass
        live = still


def sweep_kernel(plans, iters, chunks, *refs):
    kernel, elec_rhs, drop_rhs, elec_inv, drop_inv = refs[:5]
    out_elec, out_drop = refs[5:7]
    part_elec, part_drop, mid_elec, mid_drop, charge_elec, charge_drop = refs[7:13]
    rest = refs[13:]
    count = len(plans)
    per = iters * sum(chunks)
    bufs = [rest[6 * g:6 * g + 6] for g in range(per)]
    sems = [rest[6 * per + 8 * g:6 * per + 8 * g + 8] for g in range(per)]
    info = [axis_info(*plan) for plan in plans]

    barrier = pltpu.get_barrier_semaphore()
    signals = 0
    for axis, bit, partner, group, members, member in info:
        pl.semaphore_signal(barrier, inc=1, device_id={axis: partner}, device_id_type=MESH)
        for step in range(1, members):
            pl.semaphore_signal(barrier, inc=1, device_id={axis: member(step)}, device_id_type=MESH)
        signals += members

    parts = (part_elec, part_drop)
    rhs = (elec_rhs, drop_rhs)
    inv = (elec_inv, drop_inv)

    def partial(a, ce, cd):
        if a == 0:
            part_elec[...] = lax.dot_general(
                cd[...], kernel[...], (((1,), (1,)), ((), ())), precision=HIGH,
                preferred_element_type=jnp.float32)
        else:
            part_drop[...] = jnp.dot(ce[...], kernel[...], precision=HIGH, preferred_element_type=jnp.float32)

    def gens(r, a, target):
        width = parts[a].shape[1] // chunks[a]
        out = []
        for c in range(chunks[a]):
            g = r * sum(chunks) + sum(chunks[:a]) + c
            out.append(exchange(info[a], parts[a], rhs[a], inv[a], target, bufs[g], sems[g], c * width, width))
        return out

    for values, inverse, charge in ((elec_rhs, elec_inv, charge_elec), (drop_rhs, drop_inv, charge_drop)):
        size = inverse.shape[1]
        for block in range(inverse.shape[0]):
            local = slice(block * size, (block + 1) * size)
            charge[:, local] = lax.dot_general(
                values[:, local], inverse[block], (((1,), (1,)), ((), ())),
                precision=HIGH, preferred_element_type=jnp.float32,
            )
    partial(0, charge_elec, charge_drop)
    partial(1, charge_elec, charge_drop)
    pl.semaphore_wait(barrier, signals)
    mids = (mid_elec, mid_drop)
    outs = (out_elec, out_drop)
    current = [gens(0, 0, mids[0] if iters > 1 else outs[0]), gens(0, 1, mids[1] if iters > 1 else outs[1])]
    for r in range(1, iters):
        target = outs if r == iters - 1 else mids
        for _ in range(4):
            for gen in current[0] + current[1]:
                next(gen)
        run_all(current[0])
        partial(1, mids[0], mids[1])
        following = gens(r, 1, target[1])
        for gen in following:
            next(gen)
        run_all(current[1])
        partial(0, mids[0], mids[1])
        current = [gens(r, 0, target[0]), following]
    run_all(current[0] + current[1])


def sweeps(kernel, elec_rhs, drop_rhs, elec_inv, drop_inv, plans, iters, chunks=(1, 2)):
    f32 = jnp.float32
    shapes = (elec_rhs.shape, drop_rhs.shape)
    scratch = [pltpu.VMEM(shape, f32) for shape in shapes] * 3
    sem_shapes = []
    for shape, (axis, size, stride), parts in [
            item for _ in range(iters) for item in zip(shapes, plans, chunks) for _c in range(item[2])]:
            members = size // 2
            half = shape[0] // 2
            piece = half // members
            cols = shape[1] // parts
            scratch += [
                pltpu.VMEM((half, cols), f32),
                pltpu.VMEM((members, piece, cols), f32),
                pltpu.VMEM((members, piece, cols), f32),
                pltpu.VMEM((half, cols), f32),
                pltpu.VMEM((half, cols), f32),
                pltpu.VMEM((piece, cols), f32),
            ]
            for slots in (1, 1, members, members, members, members, 1, 1):
                sem_shapes.append(pltpu.SemaphoreType.DMA((slots,)))
    vmem = pl.BlockSpec(memory_space=pltpu.VMEM)
    return pl.pallas_call(
        functools.partial(sweep_kernel, plans, iters, chunks),
        out_shape=tuple(jax.ShapeDtypeStruct(shape, f32) for shape in shapes),
        in_specs=[vmem] * 5,
        out_specs=(vmem, vmem),
        scratch_shapes=scratch + sem_shapes,
        compiler_params=pltpu.CompilerParams(
            collective_id=0, has_side_effects=True, vmem_limit_bytes=60 * 1024 * 1024),
    )(kernel, elec_rhs, drop_rhs, elec_inv, drop_inv)


def on_device(elec_pos, drop_vert, drop_conn, elec_rhs, drop_rhs, elec_inv, drop_inv):
    drop_devices = lax.axis_size("drop")
    elec_devices = lax.axis_size("elec")
    rhs_count, elec_local = elec_rhs.shape
    drop_local = drop_rhs.shape[1]
    screen, soften, couple = constants(drop_local * drop_devices)
    half_block = drop_vert.shape[1]
    local_conn = drop_conn - lax.axis_index("drop") * half_block
    centres = centroids(drop_vert, local_conn)
    kernel = kernel_tile(elec_pos, centres, screen, soften, couple)

    plans = (("drop", drop_devices, 1), ("elec", elec_devices, 1))
    charge_elec, charge_drop = sweeps(kernel, elec_rhs, drop_rhs, elec_inv, drop_inv, plans, ITERS)
    return (charge_elec, charge_drop)


def solution(mesh):
    placed = (
        P(None, "elec"),
        P(None, "drop"),
        P(None, "drop"),
        P(None, "elec"),
        P(None, "drop"),
        P("elec", None, None),
        P("drop", None, None),
    )
    return jax.shard_map(
        on_device,
        mesh=mesh,
        in_specs=placed,
        out_specs=(P(None, "elec"), P(None, "drop")),
        check_vma=False,
    )
```

```python
import functools
import math

import jax
import jax.numpy as jnp
from jax import lax
from jax.experimental import pallas as pl
from jax.experimental.pallas import tpu as pltpu
from jax.sharding import PartitionSpec as P

ITERS = 2


HIGH = lax.Precision.HIGHEST
FAST = lax.Precision.HIGH
MESH = pl.DeviceIdType.MESH


def constants(total_drop):
    screen = 1.0
    soften = 0.001
    couple = 1.0 / (3.0 * math.sqrt(total_drop))
    return (screen, soften, couple)


def centroids(drop_vert, conn):
    vertices = lax.broadcasted_iota(jnp.int32, (drop_vert.shape[1], conn.shape[1]), 0)
    counts = sum((conn[k][None, :] == vertices).astype(jnp.float32) for k in range(3))
    counts = counts.astype(jnp.bfloat16)
    parts = []
    rest = drop_vert
    for _ in range(3):
        part = lax.reduce_precision(rest, exponent_bits=8, mantissa_bits=7)
        parts.append(part.astype(jnp.bfloat16))
        rest = rest - part
    stacked = jnp.concatenate(parts, axis=0)
    summed = jnp.dot(stacked, counts, preferred_element_type=jnp.float32)
    coords = drop_vert.shape[0]
    return (summed[:coords] + summed[coords:2 * coords] + summed[2 * coords:]) / 3.0


def kernel_tile(position, centres, screen, soften, couple):
    delta_x = position[0][:, None] - centres[0][None, :]
    delta_y = position[1][:, None] - centres[1][None, :]
    delta_z = position[2][:, None] - centres[2][None, :]
    distance = jnp.sqrt(delta_x * delta_x + delta_y * delta_y + delta_z * delta_z + soften)
    return couple * jnp.exp(-screen * distance) / distance


def block_solve(inverse, values):
    rhs_rows, columns = values.shape
    block_count, block_size, _ = inverse.shape
    shaped = values.reshape(rhs_rows, block_count, block_size)
    solved = jnp.einsum("bjk,rbk->rbj", inverse, shaped, precision=HIGH)
    return solved.reshape(rhs_rows, columns)


def axis_info(axis, size, stride):
    me = lax.axis_index(axis)
    bit = lax.rem(me // stride, 2)
    partner = me + stride - 2 * stride * bit
    group = lax.rem(me, stride) + (me // (2 * stride)) * stride
    members = size // 2

    def member(offset):
        g = lax.rem(group + offset, members)
        return lax.rem(g, stride) + (g // stride) * 2 * stride + bit * stride

    return (axis, bit, partner, group, members, member)


def send(src, dst, send_sem, recv_sem, axis, peer):
    copy = pltpu.make_async_remote_copy(
        src_ref=src, dst_ref=dst, send_sem=send_sem, recv_sem=recv_sem,
        device_id={axis: peer}, device_id_type=MESH,
    )
    copy.start()
    return copy


def wait_all(copies):
    for copy in copies:
        copy.wait()


def rows(index, piece):
    return pl.ds(pl.multiple_of(index * piece, piece), piece)


def exchange(info, source, rhs, inv, out, bufs, sems, first, width):
    axis, bit, partner, group, members, member = info
    half = source.shape[0] // 2
    piece = half // members
    mine = pl.multiple_of(bit * half, half)
    other = pl.multiple_of((1 - bit) * half, half)
    cols = pl.ds(first, width)
    buf_a, buf_b, buf_c, buf_d, half_s, piece_t = bufs

    pending = [send(source.at[pl.ds(other, half), cols], buf_a, sems[0].at[0], sems[1].at[0], axis, partner)]
    yield
    wait_all(pending)
    half_s[...] = source[pl.ds(mine, half), cols] + buf_a[...]
    pending = [
        send(half_s.at[rows(lax.rem(group + step, members), piece)], buf_b.at[step],
             sems[2].at[step], sems[3].at[step], axis, member(step))
        for step in range(1, members)
    ]
    yield
    wait_all(pending)
    acc = half_s[rows(group, piece), :]
    for step in range(1, members):
        acc = acc + buf_b[step]
    values = rhs[pl.ds(mine + group * piece, piece), cols] - acc
    size = inv.shape[1]
    for block in range(width // size):
        local = slice(block * size, (block + 1) * size)
        piece_t[:, local] = lax.dot_general(
            values[:, local], inv[first // size + block], (((1,), (1,)), ((), ())),
            precision=HIGH, preferred_element_type=jnp.float32,
        )
    out[pl.ds(mine + group * piece, piece), cols] = piece_t[...]
    pending = [
        send(piece_t, buf_c.at[step], sems[4].at[step], sems[5].at[step], axis, member(step))
        for step in range(1, members)
    ]
    yield
    wait_all(pending)
    for step in range(1, members):
        origin = lax.rem(group - step + members, members)
        half_s[rows(origin, piece), :] = buf_c[step]
    half_s[rows(group, piece), :] = piece_t[...]
    pending = [send(half_s, buf_d, sems[6].at[0], sems[7].at[0], axis, partner)]
    out[pl.ds(mine, half), cols] = half_s[...]
    yield
    wait_all(pending)
    out[pl.ds(other, half), cols] = buf_d[...]


def run_all(gens):
    live = list(gens)
    while live:
        still = []
        for gen in live:
            try:
                next(gen)
                still.append(gen)
            except StopIteration:
                pass
        live = still


def sweep_kernel(plans, iters, chunks, *refs):
    kernel, elec_rhs, drop_rhs, elec_inv, drop_inv = refs[:5]
    out_elec, out_drop = refs[5:7]
    part_elec, part_drop, mid_elec, mid_drop, charge_elec, charge_drop = refs[7:13]
    rest = refs[13:]
    count = len(plans)
    per = iters * count * chunks
    bufs = [rest[6 * g:6 * g + 6] for g in range(per)]
    sems = [rest[6 * per + 8 * g:6 * per + 8 * g + 8] for g in range(per)]
    info = [axis_info(*plan) for plan in plans]

    barrier = pltpu.get_barrier_semaphore()
    signals = 0
    for axis, bit, partner, group, members, member in info:
        pl.semaphore_signal(barrier, inc=1, device_id={axis: partner}, device_id_type=MESH)
        for step in range(1, members):
            pl.semaphore_signal(barrier, inc=1, device_id={axis: member(step)}, device_id_type=MESH)
        signals += members

    parts = (part_elec, part_drop)
    rhs = (elec_rhs, drop_rhs)
    inv = (elec_inv, drop_inv)

    def partial(a, ce, cd, sent):
        half = parts[a].shape[0] // 2
        bit = info[a][1]
        start = (1 - bit) * half if sent else bit * half
        span = pl.ds(pl.multiple_of(start, half), half)
        if a == 0:
            part_elec[span, :] = lax.dot_general(
                cd[span, :], kernel[...], (((1,), (1,)), ((), ())), precision=HIGH,
                preferred_element_type=jnp.float32)
        else:
            part_drop[span, :] = jnp.dot(ce[span, :], kernel[...], precision=HIGH, preferred_element_type=jnp.float32)

    def begin(a, ce, cd, exchanges):
        partial(a, ce, cd, True)
        for gen in exchanges:
            next(gen)
        partial(a, ce, cd, False)

    def gens(r, a, target):
        width = parts[a].shape[1] // chunks
        out = []
        for c in range(chunks):
            g = (r * count + a) * chunks + c
            out.append(exchange(info[a], parts[a], rhs[a], inv[a], target, bufs[g], sems[g], c * width, width))
        return out

    for values, inverse, charge in ((elec_rhs, elec_inv, charge_elec), (drop_rhs, drop_inv, charge_drop)):
        size = inverse.shape[1]
        for block in range(inverse.shape[0]):
            local = slice(block * size, (block + 1) * size)
            charge[:, local] = lax.dot_general(
                values[:, local], inverse[block], (((1,), (1,)), ((), ())),
                precision=HIGH, preferred_element_type=jnp.float32,
            )
    partial(0, charge_elec, charge_drop, True)
    partial(1, charge_elec, charge_drop, True)
    pl.semaphore_wait(barrier, signals)
    mids = (mid_elec, mid_drop)
    outs = (out_elec, out_drop)
    current = [gens(0, 0, mids[0] if iters > 1 else outs[0]), gens(0, 1, mids[1] if iters > 1 else outs[1])]
    for gen in current[0] + current[1]:
        next(gen)
    partial(0, charge_elec, charge_drop, False)
    partial(1, charge_elec, charge_drop, False)
    for r in range(1, iters):
        target = outs if r == iters - 1 else mids
        for _ in range(3):
            for gen in current[0] + current[1]:
                next(gen)
        run_all(current[0])
        following = gens(r, 1, target[1])
        begin(1, mids[0], mids[1], following)
        run_all(current[1])
        leading = gens(r, 0, target[0])
        begin(0, mids[0], mids[1], leading)
        current = [leading, following]
    run_all(current[0] + current[1])


def sweeps(kernel, elec_rhs, drop_rhs, elec_inv, drop_inv, plans, iters, chunks=2):
    f32 = jnp.float32
    shapes = (elec_rhs.shape, drop_rhs.shape)
    scratch = [pltpu.VMEM(shape, f32) for shape in shapes] * 3
    sem_shapes = []
    for shape, (axis, size, stride) in [item for _ in range(iters) for item in zip(shapes, plans) for _c in range(chunks)]:
            members = size // 2
            half = shape[0] // 2
            piece = half // members
            cols = shape[1] // chunks
            scratch += [
                pltpu.VMEM((half, cols), f32),
                pltpu.VMEM((members, piece, cols), f32),
                pltpu.VMEM((members, piece, cols), f32),
                pltpu.VMEM((half, cols), f32),
                pltpu.VMEM((half, cols), f32),
                pltpu.VMEM((piece, cols), f32),
            ]
            for slots in (1, 1, members, members, members, members, 1, 1):
                sem_shapes.append(pltpu.SemaphoreType.DMA((slots,)))
    vmem = pl.BlockSpec(memory_space=pltpu.VMEM)
    return pl.pallas_call(
        functools.partial(sweep_kernel, plans, iters, chunks),
        out_shape=tuple(jax.ShapeDtypeStruct(shape, f32) for shape in shapes),
        in_specs=[vmem] * 5,
        out_specs=(vmem, vmem),
        scratch_shapes=scratch + sem_shapes,
        compiler_params=pltpu.CompilerParams(
            collective_id=0, has_side_effects=True, vmem_limit_bytes=60 * 1024 * 1024),
    )(kernel, elec_rhs, drop_rhs, elec_inv, drop_inv)


def on_device(elec_pos, drop_vert, drop_conn, elec_rhs, drop_rhs, elec_inv, drop_inv):
    drop_devices = lax.axis_size("drop")
    elec_devices = lax.axis_size("elec")
    rhs_count, elec_local = elec_rhs.shape
    drop_local = drop_rhs.shape[1]
    screen, soften, couple = constants(drop_local * drop_devices)
    half_block = drop_vert.shape[1]
    local_conn = drop_conn - lax.axis_index("drop") * half_block
    centres = centroids(drop_vert, local_conn)
    kernel = kernel_tile(elec_pos, centres, screen, soften, couple)

    plans = (("drop", drop_devices, 1), ("elec", elec_devices, 1))
    charge_elec, charge_drop = sweeps(kernel, elec_rhs, drop_rhs, elec_inv, drop_inv, plans, ITERS)
    return (charge_elec, charge_drop)


def solution(mesh):
    placed = (
        P(None, "elec"),
        P(None, "drop"),
        P(None, "drop"),
        P(None, "elec"),
        P(None, "drop"),
        P("elec", None, None),
        P("drop", None, None),
    )
    return jax.shard_map(
        on_device,
        mesh=mesh,
        in_specs=placed,
        out_specs=(P(None, "elec"), P(None, "drop")),
        check_vma=False,
    )
```

```python
import functools
import math

import jax
import jax.numpy as jnp
from jax import lax
from jax.experimental import pallas as pl
from jax.experimental.pallas import tpu as pltpu
from jax.sharding import PartitionSpec as P

ITERS = 2


HIGH = lax.Precision.HIGHEST
FAST = lax.Precision.HIGH
MESH = pl.DeviceIdType.MESH


def constants(total_drop):
    screen = 1.0
    soften = 0.001
    couple = 1.0 / (3.0 * math.sqrt(total_drop))
    return (screen, soften, couple)


def centroids(drop_vert, conn):
    vertices = lax.broadcasted_iota(jnp.int32, (drop_vert.shape[1], conn.shape[1]), 0)
    counts = sum((conn[k][None, :] == vertices).astype(jnp.float32) for k in range(3))
    counts = counts.astype(jnp.bfloat16)
    parts = []
    rest = drop_vert
    for _ in range(3):
        part = lax.reduce_precision(rest, exponent_bits=8, mantissa_bits=7)
        parts.append(part.astype(jnp.bfloat16))
        rest = rest - part
    stacked = jnp.concatenate(parts, axis=0)
    summed = jnp.dot(stacked, counts, preferred_element_type=jnp.float32)
    coords = drop_vert.shape[0]
    return (summed[:coords] + summed[coords:2 * coords] + summed[2 * coords:]) / 3.0


def kernel_tile(position, centres, screen, soften, couple):
    delta_x = position[0][:, None] - centres[0][None, :]
    delta_y = position[1][:, None] - centres[1][None, :]
    delta_z = position[2][:, None] - centres[2][None, :]
    distance = jnp.sqrt(delta_x * delta_x + delta_y * delta_y + delta_z * delta_z + soften)
    return couple * jnp.exp(-screen * distance) / distance


def block_solve(inverse, values):
    rhs_rows, columns = values.shape
    block_count, block_size, _ = inverse.shape
    shaped = values.reshape(rhs_rows, block_count, block_size)
    solved = jnp.einsum("bjk,rbk->rbj", inverse, shaped, precision=HIGH)
    return solved.reshape(rhs_rows, columns)


def axis_info(axis, size, stride):
    me = lax.axis_index(axis)
    bit = lax.rem(me // stride, 2)
    partner = me + stride - 2 * stride * bit
    group = lax.rem(me, stride) + (me // (2 * stride)) * stride
    members = size // 2

    def member(offset):
        g = lax.rem(group + offset, members)
        return lax.rem(g, stride) + (g // stride) * 2 * stride + bit * stride

    return (axis, bit, partner, group, members, member)


def send(src, dst, send_sem, recv_sem, axis, peer):
    copy = pltpu.make_async_remote_copy(
        src_ref=src, dst_ref=dst, send_sem=send_sem, recv_sem=recv_sem,
        device_id={axis: peer}, device_id_type=MESH,
    )
    copy.start()
    return copy


def wait_all(copies):
    for copy in copies:
        copy.wait()


def rows(index, piece):
    return pl.ds(pl.multiple_of(index * piece, piece), piece)


def exchange(info, source, rhs, inv, out, bufs, sems, first, width):
    axis, bit, partner, group, members, member = info
    half = source.shape[0] // 2
    piece = half // members
    mine = pl.multiple_of(bit * half, half)
    other = pl.multiple_of((1 - bit) * half, half)
    cols = pl.ds(first, width)
    buf_a, buf_b, buf_c, buf_d, half_s, piece_t = bufs

    pending = [send(source.at[pl.ds(other, half), cols], buf_a, sems[0].at[0], sems[1].at[0], axis, partner)]
    yield
    wait_all(pending)
    half_s[...] = source[pl.ds(mine, half), cols] + buf_a[...]
    pending = [
        send(half_s.at[rows(lax.rem(group + step, members), piece)], buf_b.at[step],
             sems[2].at[step], sems[3].at[step], axis, member(step))
        for step in range(1, members)
    ]
    yield
    wait_all(pending)
    acc = half_s[rows(group, piece), :]
    for step in range(1, members):
        acc = acc + buf_b[step]
    values = rhs[pl.ds(mine + group * piece, piece), cols] - acc
    size = inv.shape[1]
    for block in range(width // size):
        local = slice(block * size, (block + 1) * size)
        piece_t[:, local] = lax.dot_general(
            values[:, local], inv[first // size + block], (((1,), (1,)), ((), ())),
            precision=HIGH, preferred_element_type=jnp.float32,
        )
    out[pl.ds(mine + group * piece, piece), cols] = piece_t[...]
    pending = [
        send(piece_t, buf_c.at[step], sems[4].at[step], sems[5].at[step], axis, member(step))
        for step in range(1, members)
    ]
    yield
    wait_all(pending)
    for step in range(1, members):
        origin = lax.rem(group - step + members, members)
        half_s[rows(origin, piece), :] = buf_c[step]
    half_s[rows(group, piece), :] = piece_t[...]
    pending = [send(half_s, buf_d, sems[6].at[0], sems[7].at[0], axis, partner)]
    out[pl.ds(mine, half), cols] = half_s[...]
    yield
    wait_all(pending)
    out[pl.ds(other, half), cols] = buf_d[...]


def run_all(gens):
    live = list(gens)
    while live:
        still = []
        for gen in live:
            try:
                next(gen)
                still.append(gen)
            except StopIteration:
                pass
        live = still


def sweep_kernel(plans, iters, chunks, consts, *refs):
    position, centres, elec_rhs, drop_rhs, elec_inv, drop_inv = refs[:6]
    out_elec, out_drop = refs[6:8]
    part_elec, part_drop, mid_elec, mid_drop, charge_elec, charge_drop, kernel = refs[8:15]
    rest = refs[15:]
    count = len(plans)
    per = iters * count * chunks
    bufs = [rest[6 * g:6 * g + 6] for g in range(per)]
    sems = [rest[6 * per + 8 * g:6 * per + 8 * g + 8] for g in range(per)]
    info = [axis_info(*plan) for plan in plans]

    barrier = pltpu.get_barrier_semaphore()
    signals = 0
    for axis, bit, partner, group, members, member in info:
        pl.semaphore_signal(barrier, inc=1, device_id={axis: partner}, device_id_type=MESH)
        for step in range(1, members):
            pl.semaphore_signal(barrier, inc=1, device_id={axis: member(step)}, device_id_type=MESH)
        signals += members

    parts = (part_elec, part_drop)
    rhs = (elec_rhs, drop_rhs)
    inv = (elec_inv, drop_inv)

    def partial(a, ce, cd):
        if a == 0:
            part_elec[...] = lax.dot_general(
                cd[...], kernel[...], (((1,), (1,)), ((), ())), precision=HIGH,
                preferred_element_type=jnp.float32)
        else:
            part_drop[...] = jnp.dot(ce[...], kernel[...], precision=HIGH, preferred_element_type=jnp.float32)

    def gens(r, a, target):
        width = parts[a].shape[1] // chunks
        out = []
        for c in range(chunks):
            g = (r * count + a) * chunks + c
            out.append(exchange(info[a], parts[a], rhs[a], inv[a], target, bufs[g], sems[g], c * width, width))
        return out

    screen, soften, couple = consts
    delta_x = position[:, 0:1] - centres[0:1, :]
    delta_y = position[:, 1:2] - centres[1:2, :]
    delta_z = position[:, 2:3] - centres[2:3, :]
    distance = jnp.sqrt(delta_x * delta_x + delta_y * delta_y + delta_z * delta_z + soften)
    kernel[...] = couple * jnp.exp(-screen * distance) / distance

    for values, inverse, charge in ((elec_rhs, elec_inv, charge_elec), (drop_rhs, drop_inv, charge_drop)):
        size = inverse.shape[1]
        for block in range(inverse.shape[0]):
            local = slice(block * size, (block + 1) * size)
            charge[:, local] = lax.dot_general(
                values[:, local], inverse[block], (((1,), (1,)), ((), ())),
                precision=HIGH, preferred_element_type=jnp.float32,
            )
    partial(0, charge_elec, charge_drop)
    partial(1, charge_elec, charge_drop)
    pl.semaphore_wait(barrier, signals)
    mids = (mid_elec, mid_drop)
    outs = (out_elec, out_drop)
    current = [gens(0, 0, mids[0] if iters > 1 else outs[0]), gens(0, 1, mids[1] if iters > 1 else outs[1])]
    for r in range(1, iters):
        target = outs if r == iters - 1 else mids
        for _ in range(4):
            for gen in current[0] + current[1]:
                next(gen)
        run_all(current[0])
        partial(1, mids[0], mids[1])
        following = gens(r, 1, target[1])
        for gen in following:
            next(gen)
        run_all(current[1])
        partial(0, mids[0], mids[1])
        current = [gens(r, 0, target[0]), following]
    run_all(current[0] + current[1])


def sweeps(position, centres, consts, elec_rhs, drop_rhs, elec_inv, drop_inv, plans, iters, chunks=2):
    f32 = jnp.float32
    shapes = (elec_rhs.shape, drop_rhs.shape)
    scratch = [pltpu.VMEM(shape, f32) for shape in shapes] * 3
    scratch.append(pltpu.VMEM((position.shape[0], centres.shape[1]), f32))
    sem_shapes = []
    for shape, (axis, size, stride) in [item for _ in range(iters) for item in zip(shapes, plans) for _c in range(chunks)]:
            members = size // 2
            half = shape[0] // 2
            piece = half // members
            cols = shape[1] // chunks
            scratch += [
                pltpu.VMEM((half, cols), f32),
                pltpu.VMEM((members, piece, cols), f32),
                pltpu.VMEM((members, piece, cols), f32),
                pltpu.VMEM((half, cols), f32),
                pltpu.VMEM((half, cols), f32),
                pltpu.VMEM((piece, cols), f32),
            ]
            for slots in (1, 1, members, members, members, members, 1, 1):
                sem_shapes.append(pltpu.SemaphoreType.DMA((slots,)))
    vmem = pl.BlockSpec(memory_space=pltpu.VMEM)
    return pl.pallas_call(
        functools.partial(sweep_kernel, plans, iters, chunks, consts),
        out_shape=tuple(jax.ShapeDtypeStruct(shape, f32) for shape in shapes),
        in_specs=[vmem] * 6,
        out_specs=(vmem, vmem),
        scratch_shapes=scratch + sem_shapes,
        compiler_params=pltpu.CompilerParams(
            collective_id=0, has_side_effects=True, vmem_limit_bytes=60 * 1024 * 1024),
    )(position, centres, elec_rhs, drop_rhs, elec_inv, drop_inv)


def on_device(elec_pos, drop_vert, drop_conn, elec_rhs, drop_rhs, elec_inv, drop_inv):
    drop_devices = lax.axis_size("drop")
    elec_devices = lax.axis_size("elec")
    rhs_count, elec_local = elec_rhs.shape
    drop_local = drop_rhs.shape[1]
    screen, soften, couple = constants(drop_local * drop_devices)
    half_block = drop_vert.shape[1]
    local_conn = drop_conn - lax.axis_index("drop") * half_block
    centres = centroids(drop_vert, local_conn)

    plans = (("drop", drop_devices, 1), ("elec", elec_devices, 1))
    charge_elec, charge_drop = sweeps(
        elec_pos.T, centres, (screen, soften, couple), elec_rhs, drop_rhs, elec_inv, drop_inv, plans, ITERS)
    return (charge_elec, charge_drop)


def solution(mesh):
    placed = (
        P(None, "elec"),
        P(None, "drop"),
        P(None, "drop"),
        P(None, "elec"),
        P(None, "drop"),
        P("elec", None, None),
        P("drop", None, None),
    )
    return jax.shard_map(
        on_device,
        mesh=mesh,
        in_specs=placed,
        out_specs=(P(None, "elec"), P(None, "drop")),
        check_vma=False,
    )
```

```python
import functools
import math

import jax
import jax.numpy as jnp
from jax import lax
from jax.experimental import pallas as pl
from jax.experimental.pallas import tpu as pltpu
from jax.sharding import PartitionSpec as P

ITERS = 2


HIGH = lax.Precision.HIGHEST
FAST = lax.Precision.HIGH
MESH = pl.DeviceIdType.MESH


def constants(total_drop):
    screen = 1.0
    soften = 0.001
    couple = 1.0 / (3.0 * math.sqrt(total_drop))
    return (screen, soften, couple)


def centroids(drop_vert, conn):
    vertices = lax.broadcasted_iota(jnp.int32, (drop_vert.shape[1], conn.shape[1]), 0)
    counts = sum((conn[k][None, :] == vertices).astype(jnp.float32) for k in range(3))
    counts = counts.astype(jnp.bfloat16)
    parts = []
    rest = drop_vert
    for _ in range(3):
        part = lax.reduce_precision(rest, exponent_bits=8, mantissa_bits=7)
        parts.append(part.astype(jnp.bfloat16))
        rest = rest - part
    stacked = jnp.concatenate(parts, axis=0)
    summed = jnp.dot(stacked, counts, preferred_element_type=jnp.float32)
    coords = drop_vert.shape[0]
    return (summed[:coords] + summed[coords:2 * coords] + summed[2 * coords:]) / 3.0


def kernel_tile(position, centres, screen, soften, couple):
    delta_x = position[0][:, None] - centres[0][None, :]
    delta_y = position[1][:, None] - centres[1][None, :]
    delta_z = position[2][:, None] - centres[2][None, :]
    distance = jnp.sqrt(delta_x * delta_x + delta_y * delta_y + delta_z * delta_z + soften)
    return couple * jnp.exp(-screen * distance) / distance


def block_solve(inverse, values):
    rhs_rows, columns = values.shape
    block_count, block_size, _ = inverse.shape
    shaped = values.reshape(rhs_rows, block_count, block_size)
    solved = jnp.einsum("bjk,rbk->rbj", inverse, shaped, precision=HIGH)
    return solved.reshape(rhs_rows, columns)


def axis_info(axis, size, stride):
    me = lax.axis_index(axis)
    bit = lax.rem(me // stride, 2)
    partner = me + stride - 2 * stride * bit
    group = lax.rem(me, stride) + (me // (2 * stride)) * stride
    members = size // 2

    def member(offset):
        g = lax.rem(group + offset, members)
        return lax.rem(g, stride) + (g // stride) * 2 * stride + bit * stride

    return (axis, bit, partner, group, members, member)


def send(src, dst, send_sem, recv_sem, axis, peer):
    copy = pltpu.make_async_remote_copy(
        src_ref=src, dst_ref=dst, send_sem=send_sem, recv_sem=recv_sem,
        device_id={axis: peer}, device_id_type=MESH,
    )
    copy.start()
    return copy


def wait_all(copies):
    for copy in copies:
        copy.wait()


def rows(index, piece):
    return pl.ds(pl.multiple_of(index * piece, piece), piece)


def exchange(info, source, rhs, inv, out, bufs, sems, first, width):
    axis, bit, partner, group, members, member = info
    half = source.shape[0] // 2
    piece = half // members
    mine = pl.multiple_of(bit * half, half)
    other = pl.multiple_of((1 - bit) * half, half)
    cols = pl.ds(first, width)
    buf_a, buf_b, buf_c, buf_d, half_s, piece_t = bufs

    pending = [send(source.at[pl.ds(other, half), cols], buf_a, sems[0].at[0], sems[1].at[0], axis, partner)]
    yield
    wait_all(pending)
    half_s[...] = source[pl.ds(mine, half), cols] + buf_a[...]
    pending = [
        send(half_s.at[rows(lax.rem(group + step, members), piece)], buf_b.at[step],
             sems[2].at[step], sems[3].at[step], axis, member(step))
        for step in range(1, members)
    ]
    yield
    wait_all(pending)
    acc = half_s[rows(group, piece), :]
    for step in range(1, members):
        acc = acc + buf_b[step]
    values = rhs[pl.ds(mine + group * piece, piece), cols] - acc
    size = inv.shape[1]
    for block in range(width // size):
        local = slice(block * size, (block + 1) * size)
        piece_t[:, local] = lax.dot_general(
            values[:, local], inv[first // size + block], (((1,), (1,)), ((), ())),
            precision=HIGH, preferred_element_type=jnp.float32,
        )
    out[pl.ds(mine + group * piece, piece), cols] = piece_t[...]
    pending = [
        send(piece_t, buf_c.at[step], sems[4].at[step], sems[5].at[step], axis, member(step))
        for step in range(1, members)
    ]
    yield
    wait_all(pending)
    for step in range(1, members):
        origin = lax.rem(group - step + members, members)
        half_s[rows(origin, piece), :] = buf_c[step]
    half_s[rows(group, piece), :] = piece_t[...]
    pending = [send(half_s, buf_d, sems[6].at[0], sems[7].at[0], axis, partner)]
    out[pl.ds(mine, half), cols] = half_s[...]
    yield
    wait_all(pending)
    out[pl.ds(other, half), cols] = buf_d[...]


def run_all(gens):
    live = list(gens)
    while live:
        still = []
        for gen in live:
            try:
                next(gen)
                still.append(gen)
            except StopIteration:
                pass
        live = still


def sweep_kernel(plans, iters, chunks, consts, *refs):
    position, centres, elec_rhs, drop_rhs, elec_inv, drop_inv = refs[:6]
    out_elec, out_drop = refs[6:8]
    part_elec, part_drop, mid_elec, mid_drop, charge_elec, charge_drop, kernel = refs[8:15]
    rest = refs[15:]
    count = len(plans)
    per = iters * count * chunks
    bufs = [rest[6 * g:6 * g + 6] for g in range(per)]
    sems = [rest[6 * per + 8 * g:6 * per + 8 * g + 8] for g in range(per)]
    info = [axis_info(*plan) for plan in plans]

    barrier = pltpu.get_barrier_semaphore()
    signals = 0
    for axis, bit, partner, group, members, member in info:
        pl.semaphore_signal(barrier, inc=1, device_id={axis: partner}, device_id_type=MESH)
        for step in range(1, members):
            pl.semaphore_signal(barrier, inc=1, device_id={axis: member(step)}, device_id_type=MESH)
        signals += members

    parts = (part_elec, part_drop)
    rhs = (elec_rhs, drop_rhs)
    inv = (elec_inv, drop_inv)

    def partial(a, ce, cd):
        if a == 0:
            part_elec[...] = lax.dot_general(
                cd[...], kernel[...], (((1,), (1,)), ((), ())), precision=HIGH,
                preferred_element_type=jnp.float32)
        else:
            part_drop[...] = jnp.dot(ce[...], kernel[...], precision=HIGH, preferred_element_type=jnp.float32)

    def gens(r, a, target):
        width = parts[a].shape[1] // chunks
        out = []
        for c in range(chunks):
            g = (r * count + a) * chunks + c
            out.append(exchange(info[a], parts[a], rhs[a], inv[a], target, bufs[g], sems[g], c * width, width))
        return out

    screen, soften, couple = consts
    delta_x = position[:, 0:1] - centres[0:1, :]
    delta_y = position[:, 1:2] - centres[1:2, :]
    delta_z = position[:, 2:3] - centres[2:3, :]
    squared = delta_x * delta_x + delta_y * delta_y + delta_z * delta_z + soften
    inverse = lax.rsqrt(squared)
    kernel[...] = couple * jnp.exp(-screen * (squared * inverse)) * inverse

    for values, inverse, charge in ((elec_rhs, elec_inv, charge_elec), (drop_rhs, drop_inv, charge_drop)):
        size = inverse.shape[1]
        for block in range(inverse.shape[0]):
            local = slice(block * size, (block + 1) * size)
            charge[:, local] = lax.dot_general(
                values[:, local], inverse[block], (((1,), (1,)), ((), ())),
                precision=HIGH, preferred_element_type=jnp.float32,
            )
    partial(0, charge_elec, charge_drop)
    partial(1, charge_elec, charge_drop)
    pl.semaphore_wait(barrier, signals)
    mids = (mid_elec, mid_drop)
    outs = (out_elec, out_drop)
    current = [gens(0, 0, mids[0] if iters > 1 else outs[0]), gens(0, 1, mids[1] if iters > 1 else outs[1])]
    for r in range(1, iters):
        target = outs if r == iters - 1 else mids
        for _ in range(4):
            for gen in current[0] + current[1]:
                next(gen)
        run_all(current[0])
        partial(1, mids[0], mids[1])
        following = gens(r, 1, target[1])
        for gen in following:
            next(gen)
        run_all(current[1])
        partial(0, mids[0], mids[1])
        current = [gens(r, 0, target[0]), following]
    run_all(current[0] + current[1])


def sweeps(position, centres, consts, elec_rhs, drop_rhs, elec_inv, drop_inv, plans, iters, chunks=2):
    f32 = jnp.float32
    shapes = (elec_rhs.shape, drop_rhs.shape)
    scratch = [pltpu.VMEM(shape, f32) for shape in shapes] * 3
    scratch.append(pltpu.VMEM((position.shape[0], centres.shape[1]), f32))
    sem_shapes = []
    for shape, (axis, size, stride) in [item for _ in range(iters) for item in zip(shapes, plans) for _c in range(chunks)]:
            members = size // 2
            half = shape[0] // 2
            piece = half // members
            cols = shape[1] // chunks
            scratch += [
                pltpu.VMEM((half, cols), f32),
                pltpu.VMEM((members, piece, cols), f32),
                pltpu.VMEM((members, piece, cols), f32),
                pltpu.VMEM((half, cols), f32),
                pltpu.VMEM((half, cols), f32),
                pltpu.VMEM((piece, cols), f32),
            ]
            for slots in (1, 1, members, members, members, members, 1, 1):
                sem_shapes.append(pltpu.SemaphoreType.DMA((slots,)))
    vmem = pl.BlockSpec(memory_space=pltpu.VMEM)
    return pl.pallas_call(
        functools.partial(sweep_kernel, plans, iters, chunks, consts),
        out_shape=tuple(jax.ShapeDtypeStruct(shape, f32) for shape in shapes),
        in_specs=[vmem] * 6,
        out_specs=(vmem, vmem),
        scratch_shapes=scratch + sem_shapes,
        compiler_params=pltpu.CompilerParams(
            collective_id=0, has_side_effects=True, vmem_limit_bytes=60 * 1024 * 1024),
    )(position, centres, elec_rhs, drop_rhs, elec_inv, drop_inv)


def on_device(elec_pos, drop_vert, drop_conn, elec_rhs, drop_rhs, elec_inv, drop_inv):
    drop_devices = lax.axis_size("drop")
    elec_devices = lax.axis_size("elec")
    rhs_count, elec_local = elec_rhs.shape
    drop_local = drop_rhs.shape[1]
    screen, soften, couple = constants(drop_local * drop_devices)
    half_block = drop_vert.shape[1]
    local_conn = drop_conn - lax.axis_index("drop") * half_block
    centres = centroids(drop_vert, local_conn)

    plans = (("drop", drop_devices, 1), ("elec", elec_devices, 1))
    charge_elec, charge_drop = sweeps(
        elec_pos.T, centres, (screen, soften, couple), elec_rhs, drop_rhs, elec_inv, drop_inv, plans, ITERS)
    return (charge_elec, charge_drop)


def solution(mesh):
    placed = (
        P(None, "elec"),
        P(None, "drop"),
        P(None, "drop"),
        P(None, "elec"),
        P(None, "drop"),
        P("elec", None, None),
        P("drop", None, None),
    )
    return jax.shard_map(
        on_device,
        mesh=mesh,
        in_specs=placed,
        out_specs=(P(None, "elec"), P(None, "drop")),
        check_vma=False,
    )
```
